128 devices in a mesh: row: 8 (over z_hi, x), col: 16 (over z_lo, y, core).
Axes of the slice: x: 4, y: 4, z: 4 (z_hi: 2, z_lo: 2; z = z_hi * 2 + z_lo), core: 2. Of those that a mesh axis runs over, the one named last changes fastest.
Arguments:
- images: float32 [256, 28, 28, 3], P(('row', 'col')), may hold values from -6 to 6
- noise_field: float32 [256, 28, 28, 3], P(('row', 'col')), may hold values from -6 to 6
- stem_weight: bfloat16 [27, 256], replicated, may hold values from -1.25 to 1.25
- level_one: bfloat16 [4, 2304, 256], replicated, may hold values from -0.125 to 0.125
- down_weight: bfloat16 [1024, 256], replicated, may hold values from -0.1875 to 0.1875
- level_two: bfloat16 [2, 2304, 256], replicated, may hold values from -0.125 to 0.125
- up_weight: bfloat16 [256, 1024], replicated, may hold values from -0.375 to 0.375
- out_weight: bfloat16 [256, 3], replicated, may hold values from -0.375 to 0.375
- embed_weight: bfloat16 [588, 6144], replicated
- embed_bias: float32 [6144], replicated
- mlp_in: bfloat16 [6144, 24576], P('col', 'row'), may hold values from -0.078125 to 0.078125
- mlp_out: bfloat16 [24576, 6144], P('row', 'col'), may hold values from -0.0390625 to 0.0390625
Outputs:
- purified: float32 [256, 28, 28, 3], P(('row', 'col'))
- encoded: bfloat16 [1024, 6144], P('row', 'col')
The draws below stay inside these ranges and needn't reach their ends.
All inputs are finite; a program needn't handle non-finite values.
Results may differ from the reference program's by a relative error of at most 0.018.
Values may be sent and summed in bfloat16 or wider, within the bound.
No kernel may reach another device: no remote copies, remote signals or barrier semaphores. Data moves between devices by JAX's collectives and lax.ppermute only.
A program may use at most 128 MiB of HBM per device.

```python
import math
import jax
import jax.numpy as jnp
from jax import lax

D = 6144
FF = 24576
CH = 256
PATCH = 14
SIDE = 28
IMAGES = 256


def draw_embed_weight(key, part):
    first, second = jax.random.split(jax.random.fold_in(key, 11))
    position = jnp.arange(D, dtype=jnp.float32) / D
    base = jax.random.normal(first, (PATCH * PATCH * 3, D), jnp.float32)
    trend = jnp.sqrt(0.5 + position)
    spread = 10.0 ** (jax.random.uniform(second, (D,), jnp.float32) - 1.0)
    column_scale = 2.0 * spread * trend / math.sqrt(PATCH * PATCH * 3)
    return (base * column_scale[None, :]).astype(jnp.bfloat16)


def draw_embed_bias(key, part):
    position = jnp.arange(D, dtype=jnp.float32) / D
    level = jax.random.uniform(jax.random.fold_in(key, 23), (D,), jnp.float32, 0.5, 1.5)
    trend = 0.5 + position
    return level * trend


def level_of(stream_key, shape, cuts, least, top_value):
    loudness, own = 1.0, jax.random.fold_in(stream_key, 6)
    for axis_at, blocks in cuts:
        heights = jnp.exp(jax.random.uniform(jax.random.fold_in(own, axis_at), (blocks,), jnp.float32, least / len(cuts), top_value / len(cuts)))
        loudness = loudness * jnp.repeat(heights, shape[axis_at] // blocks).reshape([-1 if axis == axis_at else 1 for axis in range(len(shape))])
    return loudness


def normal_values(key, extent, deviation, most, cuts=(), kind=jnp.bfloat16):
    drawn = deviation * jax.random.normal(key, extent, jnp.float32)
    if cuts:
        drawn = drawn * level_of(key, extent, cuts, -0.22, 0.18)
    return jnp.clip(drawn, -most, most).astype(kind)


def setup_inputs(seed: int = 0) -> dict:
    key_list = jax.random.split(jax.random.key(seed), 13)
    return {
        "images": normal_values(key_list[0], (IMAGES, SIDE, SIDE, 3), 1.0, 6.0, ((0, 128),), jnp.float32),
        "noise_field": normal_values(key_list[1], (IMAGES, SIDE, SIDE, 3), 1.0, 6.0, ((0, 128),), jnp.float32),
        "stem_weight": normal_values(key_list[2], (27, CH), 27 ** -0.5, 1.25),
        "level_one": normal_values(key_list[3], (4, 9 * CH, CH), (9 * CH) ** -0.5, 0.125),
        "down_weight": normal_values(key_list[4], (4 * CH, CH), (4 * CH) ** -0.5, 0.1875),
        "level_two": normal_values(key_list[5], (2, 9 * CH, CH), (9 * CH) ** -0.5, 0.125),
        "up_weight": normal_values(key_list[6], (CH, 4 * CH), CH ** -0.5, 0.375),
        "out_weight": normal_values(key_list[7], (CH, 3), CH ** -0.5, 0.375),
        "embed_weight": draw_embed_weight(jax.random.fold_in(key_list[12], 71), 0),
        "embed_bias": draw_embed_bias(jax.random.fold_in(key_list[12], 71), 0),
        "mlp_in": normal_values(key_list[10], (D, FF), D ** -0.5, 0.078125, ((0, 16), (1, 8))),
        "mlp_out": normal_values(key_list[11], (FF, D), FF ** -0.5, 0.0390625, ((0, 8), (1, 16))),
    }


step_size = 0.25
noise_gain = math.sqrt(0.5)
ln_epsilon = 1e-06

def neighbours(field):
    height = field.shape[1]
    breadth = field.shape[2]
    padded = jnp.pad(field, ((0, 0), (1, 1), (1, 1), (0, 0)))
    parts = [padded[:, row_off:row_off + height, col_off:col_off + breadth, :] for row_off in range(3) for col_off in range(3)]
    return jnp.concatenate(parts, axis=-1)

def project(field, weight):
    flat = field.reshape(-1, field.shape[-1])
    result = jnp.dot(flat, weight, preferred_element_type=jnp.float32)
    return result.reshape(field.shape[:-1] + (weight.shape[1],))

def convolve(field, kernel):
    return project(neighbours(field), kernel)

def activate(field):
    return jax.nn.gelu(field).astype(jnp.bfloat16)

def fold_pixels(field):
    count, height, breadth, depth = field.shape
    grouped = field.reshape(count, height // 2, 2, breadth // 2, 2, depth).transpose(0, 1, 3, 2, 4, 5)
    return grouped.reshape(count, height // 2, breadth // 2, 4 * depth)

def unfold_pixels(field, depth):
    count, height, breadth, _ = field.shape
    grouped = field.reshape(count, height, breadth, 2, 2, depth).transpose(0, 1, 3, 2, 4, 5)
    return grouped.reshape(count, 2 * height, 2 * breadth, depth)

def score_net(pixels, stem_weight, level_one, down_weight, level_two, up_weight, out_weight):
    stream = convolve(pixels.astype(jnp.bfloat16), stem_weight)
    for layer in range(2):
        stream = stream + convolve(activate(stream), level_one[layer])
    skipped = stream
    coarse = project(fold_pixels(stream.astype(jnp.bfloat16)), down_weight)
    for layer in range(2):
        coarse = coarse + convolve(activate(coarse), level_two[layer])
    lifted = project(coarse.astype(jnp.bfloat16), up_weight)
    stream = unfold_pixels(lifted, up_weight.shape[0]) + skipped
    for layer in range(2, 4):
        stream = stream + convolve(activate(stream), level_one[layer])
    return project(activate(stream), out_weight)

def patchify(pixels, patch_side):
    count, side = (pixels.shape[0], pixels.shape[1])
    grid = side // patch_side
    blocks = pixels.reshape(count, grid, patch_side, grid, patch_side, 3).transpose(0, 1, 3, 2, 4, 5)
    return blocks.reshape(count * grid * grid, patch_side * patch_side * 3)

def reference(images, noise_field, stem_weight, level_one, down_weight, level_two, up_weight, out_weight, embed_weight, embed_bias, mlp_in, mlp_out):

    def single_score(single):
        return score_net(single[None], stem_weight, level_one, down_weight, level_two, up_weight, out_weight)[0]
    score_field = lax.map(single_score, images)
    purified = images + step_size * score_field + noise_gain * noise_field
    patches = patchify(purified.astype(jnp.bfloat16), PATCH)
    embedded = (jnp.dot(patches, embed_weight, preferred_element_type=jnp.float32) + embed_bias).astype(jnp.bfloat16)
    values = embedded.astype(jnp.float32)
    row_mean = lax.optimization_barrier(jnp.mean(values, axis=1, keepdims=True))
    row_square = lax.optimization_barrier(jnp.mean(values * values, axis=1, keepdims=True))
    normed = ((values - row_mean) * lax.rsqrt(row_square - row_mean * row_mean + ln_epsilon)).astype(jnp.bfloat16)
    hidden = jax.nn.gelu(jnp.dot(normed, mlp_in, preferred_element_type=jnp.float32)).astype(jnp.bfloat16)
    encoded = (values + jnp.dot(hidden, mlp_out, preferred_element_type=jnp.float32)).astype(jnp.bfloat16)
    return (purified, encoded)
```

```python
import functools
import math

import jax
import jax.numpy as jnp
from jax import lax
from jax.experimental import pallas as pl
from jax.experimental.pallas import tpu as pltpu
from jax.sharding import Mesh, PartitionSpec as P

step_size = 0.25
noise_gain = math.sqrt(0.5)
ln_epsilon = 1e-06
PATCH = 14
W1, W2 = 32, 16
CH = 256
f32, bf16 = jnp.float32, jnp.bfloat16


def gelu(v):
    inner = v * (0.7978845608028654 + 0.035677408136300125 * (v * v))
    half = 0.5 * v
    return half + half * jnp.tanh(inner)


def score_kernel(side, count, images, noise, stem_w, l1_hbm, down_hbm, l2_hbm, up_hbm, out_w,
                 purified, pix, stem_x, stem_k, out_k, xa, xb, ca, cb, stream, coarse,
                 l1, down, l2, up, sems):
    half = side // 2
    span1, span2 = side * W1, half * W2
    pitch1, pitch2 = span1 + W1, span2 + W2
    loads = [pltpu.make_async_copy(l1_hbm.at[0], l1.at[0], sems.at[0]),
             pltpu.make_async_copy(l1_hbm.at[1], l1.at[1], sems.at[1]),
             pltpu.make_async_copy(down_hbm, down, sems.at[2]),
             pltpu.make_async_copy(l2_hbm, l2, sems.at[3]),
             pltpu.make_async_copy(up_hbm, up, sems.at[4]),
             pltpu.make_async_copy(l1_hbm.at[2], l1.at[2], sems.at[5]),
             pltpu.make_async_copy(l1_hbm.at[3], l1.at[3], sems.at[6])]
    for load in loads:
        load.start()

    chunk = span1 // 2
    per_image = 2
    mask1 = (lax.broadcasted_iota(jnp.int32, (chunk, 1), 0) % W1) < side
    mask2 = (lax.broadcasted_iota(jnp.int32, (span2, 1), 0) % W2) < half

    def read(rows):
        return jnp.concatenate([stream[0, rows, :], stream[1, rows, :]], axis=1)

    def write(rows, value):
        stream[0, rows, :] = value[:, 0:128]
        stream[1, rows, :] = value[:, 128:256]

    for i in range(count + 1):
        z1 = jnp.zeros((W1, 3 * CH), bf16)
        z2 = jnp.zeros((W2, 3 * CH), bf16)
        xa[i * pitch1:i * pitch1 + W1, :] = z1
        xb[i * pitch1:i * pitch1 + W1, :] = z1
        ca[i * pitch2:i * pitch2 + W2, :] = z2
        cb[i * pitch2:i * pitch2 + W2, :] = z2
        stem_x[i * pitch1:i * pitch1 + W1, :] = jnp.zeros((W1, 128), bf16)
    pix[...] = jnp.zeros_like(pix)
    stem_k[...] = jnp.zeros_like(stem_k)
    out_k[...] = jnp.zeros_like(out_k)
    for dy in range(3):
        stem_k[dy, 0:9, :] = stem_w[9 * dy:9 * dy + 9, :].astype(f32)
    out_k[:, 0:3] = out_w[...].astype(f32)

    for i in range(count):
        def put(y, _, i=i):
            base = pl.multiple_of(W1 + i * pitch1 + y * W1, W1)
            pix[pl.ds(base, side), 0:3] = images[i, y].astype(bf16).astype(f32)
            return 0
        lax.fori_loop(0, side, put, 0)

    def shifted(ref, base, value):
        n = value.shape[0]
        ref[pl.ds(base, n), 0:CH] = pltpu.roll(value, 1, 0).astype(bf16)
        ref[pl.ds(base, n), CH:2 * CH] = value.astype(bf16)
        ref[pl.ds(base, n), 2 * CH:3 * CH] = pltpu.roll(value, n - 1, 0).astype(bf16)

    def each(body):
        def step(t, _):
            base = W1 + (t // per_image) * pitch1 + (t % per_image) * chunk
            body(t, pl.multiple_of(base, W1))
            return 0
        lax.fori_loop(0, count * per_image, step, 0)

    def conv(ref, base, n, width, weights):
        acc = jnp.dot(ref[pl.ds(base - width, n), :], weights[0:3 * CH, :], preferred_element_type=f32)
        acc += jnp.dot(ref[pl.ds(base, n), :], weights[3 * CH:6 * CH, :], preferred_element_type=f32)
        acc += jnp.dot(ref[pl.ds(base + width, n), :], weights[6 * CH:9 * CH, :], preferred_element_type=f32)
        return acc

    def stem_cols(t, base):
        v = pix[pl.ds(base, chunk), :]
        left = pltpu.roll(v, 1, 0)
        right = pltpu.roll(v, chunk - 1, 0)
        stem_x[pl.ds(base, chunk), :] = (left + pltpu.roll(v, 3, 1) + pltpu.roll(right, 6, 1)).astype(bf16)
    each(stem_cols)

    def stem_conv(t, base):
        acc = jnp.dot(stem_x[pl.ds(base - W1, chunk), :], stem_k[0].astype(bf16), preferred_element_type=f32)
        acc += jnp.dot(stem_x[pl.ds(base, chunk), :], stem_k[1].astype(bf16), preferred_element_type=f32)
        acc += jnp.dot(stem_x[pl.ds(base + W1, chunk), :], stem_k[2].astype(bf16), preferred_element_type=f32)
        write(pl.ds(base, chunk), acc)
        shifted(xa, base, jnp.where(mask1, gelu(acc), 0.0))
    each(stem_conv)

    loads[0].wait()

    def layer0(t, base):
        s = read(pl.ds(base, chunk)) + conv(xa, base, chunk, W1, l1.at[0])
        write(pl.ds(base, chunk), s)
        shifted(xb, base, jnp.where(mask1, gelu(s), 0.0))
    each(layer0)

    loads[1].wait()

    def layer1(t, base):
        write(pl.ds(base, chunk), read(pl.ds(base, chunk)) + conv(xb, base, chunk, W1, l1.at[1]))
    each(layer1)

    loads[2].wait()
    loads[3].wait()
    loads[4].wait()
    for i in range(count):
        base1, base2 = W1 + i * pitch1, W2 + i * pitch2
        acc = None
        for b in range(2):
            cols = read(pl.ds(base1 + b, span1 // 2, stride=2)).astype(bf16).reshape(half, 2, W2, CH)
            for a in range(2):
                part = jnp.dot(cols[:, a].reshape(span2, CH), down[(2 * a + b) * CH:(2 * a + b + 1) * CH, :],
                               preferred_element_type=f32)
                acc = part if acc is None else acc + part
        coarse[base2:base2 + span2, :] = acc
        shifted(ca, base2, jnp.where(mask2, gelu(acc), 0.0))
    for i in range(count):
        base2 = W2 + i * pitch2
        s = coarse[base2:base2 + span2, :] + conv(ca, base2, span2, W2, l2.at[0])
        coarse[base2:base2 + span2, :] = s
        shifted(cb, base2, jnp.where(mask2, gelu(s), 0.0))
    for i in range(count):
        base1, base2 = W1 + i * pitch1, W2 + i * pitch2
        s = coarse[base2:base2 + span2, :] + conv(cb, base2, span2, W2, l2.at[1])
        s = s.astype(bf16)
        for a in range(2):
            for b in range(2):
                g = (2 * a + b) * CH
                part = jnp.dot(s, up[:, g:g + CH], preferred_element_type=f32)
                for y in range(half):
                    rows = pl.ds(base1 + (2 * y + a) * W1 + b, W2, stride=2)
                    write(rows, read(rows) + part[y * W2:(y + 1) * W2, :])

    def enter(t, base):
        shifted(xa, base, jnp.where(mask1, gelu(read(pl.ds(base, chunk))), 0.0))
    each(enter)

    loads[5].wait()

    def layer2(t, base):
        s = read(pl.ds(base, chunk)) + conv(xa, base, chunk, W1, l1.at[2])
        write(pl.ds(base, chunk), s)
        shifted(xb, base, jnp.where(mask1, gelu(s), 0.0))
    each(layer2)

    loads[6].wait()
    lines = chunk // W1

    def layer3(t, base):
        s = read(pl.ds(base, chunk)) + conv(xb, base, chunk, W1, l1.at[3])
        score = jnp.dot(gelu(s).astype(bf16), out_k[...].astype(bf16), preferred_element_type=f32)
        i, y0 = t // per_image, (t % per_image) * lines
        for y in range(lines):
            purified[i, y0 + y] = (images[i, y0 + y] + step_size * score[y * W1:y * W1 + side, 0:3]
                                   + noise_gain * noise[i, y0 + y])
    each(layer3)


def score_call(images, noise, stem_w, l1, down, l2, up, out_w):
    count, side = images.shape[0], images.shape[1]
    rows1 = W1 + count * (side + 1) * W1
    rows2 = W2 + count * (side // 2 + 1) * W2
    vm = pl.BlockSpec(memory_space=pltpu.VMEM)
    hb = pl.BlockSpec(memory_space=pl.ANY)
    return pl.pallas_call(
        functools.partial(score_kernel, side, count),
        out_shape=jax.ShapeDtypeStruct(images.shape, f32),
        in_specs=[vm, vm, vm, hb, hb, hb, hb, vm],
        out_specs=vm,
        scratch_shapes=[
            pltpu.VMEM((rows1, 128), f32),
            pltpu.VMEM((rows1, 128), bf16),
            pltpu.VMEM((3, 128, CH), f32),
            pltpu.VMEM((CH, 128), f32),
            pltpu.VMEM((rows1, 3 * CH), bf16),
            pltpu.VMEM((rows1, 3 * CH), bf16),
            pltpu.VMEM((rows2, 3 * CH), bf16),
            pltpu.VMEM((rows2, 3 * CH), bf16),
            pltpu.VMEM((CH // 128, rows1, 128), f32),
            pltpu.VMEM((rows2, CH), f32),
            pltpu.VMEM(l1.shape, bf16),
            pltpu.VMEM(down.shape, bf16),
            pltpu.VMEM(l2.shape, bf16),
            pltpu.VMEM(up.shape, bf16),
            pltpu.SemaphoreType.DMA((7,)),
        ],
        compiler_params=pltpu.CompilerParams(vmem_limit_bytes=48 << 20),
        cost_estimate=pl.CostEstimate(flops=10_000_000_000, transcendentals=3_000_000, bytes_accessed=12_000_000),
        name="score_net",
    )(images, noise, stem_w, l1, down, l2, up, out_w)


def embed_kernel(parts, patches, weight_hbm, bias, own_hbm, mate_hbm, hidden, kept, sent,
                 weight, own, mate, field, total, sums, squares, sems):
    core = lax.axis_index("core")
    row = lax.axis_index("zh") * lax.axis_size("x") + lax.axis_index("x")
    tokens, depth = patches.shape[0], weight_hbm.shape[0]
    blocks, span, width = own_hbm.shape
    group = weight_hbm.shape[1] // parts
    loads = [pltpu.make_async_copy(weight_hbm.at[:, pl.ds(g * group, group)], weight.at[g], sems.at[g])
             for g in range(parts)]
    loads.append(pltpu.make_async_copy(own_hbm, own, sems.at[parts]))
    loads.append(pltpu.make_async_copy(mate_hbm, mate, sems.at[parts + 1]))
    for load in loads:
        load.start()
    sums[...] = jnp.zeros_like(sums)
    squares[...] = jnp.zeros_like(squares)
    pixels = patches[:, 0:depth]
    for g in range(parts):
        loads[g].wait()

        def embed(k, _, g=g):
            at = pl.multiple_of(k * span, 128)
            there = pl.multiple_of(g * group + k * span, 128)
            e = jnp.dot(pixels, weight[g, :, pl.ds(at, span)], preferred_element_type=f32)
            e = (e + bias[:, pl.ds(there, span)]).astype(bf16)
            field[:, pl.ds(there, span)] = e
            v = e.astype(f32)
            q = v * v
            a, b = sums[...], squares[...]
            for lane in range(0, span, 128):
                a += v[:, lane:lane + 128]
                b += q[:, lane:lane + 128]
            sums[...] = a
            squares[...] = b
            return 0
        lax.fori_loop(0, group // span, embed, 0)
    count = parts * group
    mean = jnp.sum(sums[...], axis=1, keepdims=True) / count
    square = jnp.sum(squares[...], axis=1, keepdims=True) / count
    scale = lax.rsqrt(square - mean * mean + ln_epsilon)
    place = lax.axis_index("zl") * lax.axis_size("y") + lax.axis_index("y")
    share = tokens // 8
    rows = pl.ds(pl.multiple_of(row * share, share), share)
    kept[...] = field[rows, pl.ds(pl.multiple_of((2 * place + core) * span, 128), span)]
    sent[...] = field[rows, pl.ds(pl.multiple_of((2 * place + 1 - core) * span, 128), span)]
    total[...] = jnp.zeros_like(total)
    loads[parts].wait()
    loads[parts + 1].wait()

    def mix(b, _):
        for block, side in ((own, core), (mate, 1 - core)):
            at = pl.multiple_of((2 * b + side) * span, 128)
            v = field[:, pl.ds(at, span)].astype(f32)
            normed = ((v - mean) * scale).astype(bf16)
            total[...] += jnp.dot(normed, block[b], preferred_element_type=f32)
        return 0
    lax.fori_loop(0, blocks, mix, 0)
    value = gelu(total[...]).astype(bf16)
    for b in range(hidden.shape[0]):
        hidden[b] = value


def embed_call(patches, weight, bias, own, mate, copies):
    tokens, blocks, span, width = patches.shape[0], *own.shape
    features = weight.shape[1]
    parts = 4
    share = tokens // 8
    vm = pl.BlockSpec(memory_space=pltpu.VMEM)
    hb = pl.BlockSpec(memory_space=pl.ANY)
    return pl.pallas_call(
        functools.partial(embed_kernel, parts),
        out_shape=(jax.ShapeDtypeStruct((copies, tokens, width), bf16),
                   jax.ShapeDtypeStruct((share, span), bf16),
                   jax.ShapeDtypeStruct((share, span), bf16)),
        in_specs=[vm, hb, vm, hb, hb],
        out_specs=(vm, vm, vm),
        scratch_shapes=[
            pltpu.VMEM((parts, weight.shape[0], features // parts), bf16),
            pltpu.VMEM(own.shape, bf16),
            pltpu.VMEM(mate.shape, bf16),
            pltpu.VMEM((tokens, features), bf16),
            pltpu.VMEM((tokens, width), f32),
            pltpu.VMEM((tokens, 128), f32),
            pltpu.VMEM((tokens, 128), f32),
            pltpu.SemaphoreType.DMA((parts + 2,)),
        ],
        compiler_params=pltpu.CompilerParams(vmem_limit_bytes=48 << 20),
        cost_estimate=pl.CostEstimate(flops=7_000_000_000, transcendentals=200_000, bytes_accessed=20_000_000),
        name="embed_mlp",
    )(patches, weight, bias, own, mate)


def mix_kernel(hidden, own, mate, out, total):
    b = pl.program_id(0)
    span = own.shape[1]

    @pl.when(b == 0)
    def _():
        total[...] = jnp.zeros_like(total)
    h = hidden[0]
    total[:, 0:span] += jnp.dot(h, own[...], preferred_element_type=f32)
    total[:, span:2 * span] += jnp.dot(h, mate[...], preferred_element_type=f32)

    @pl.when(b == pl.num_programs(0) - 1)
    def _():
        core = lax.axis_index("core")
        share = out.shape[1]
        for r in range(out.shape[0] // 2):
            rows = slice(r * share, (r + 1) * share)
            out[2 * r + core] = total[rows, 0:span].astype(bf16)
            out[2 * r + 1 - core] = total[rows, span:2 * span].astype(bf16)


def mix_call(hidden, own, mate):
    blocks, tokens, width = hidden.shape
    span = own.shape[1]
    return pl.pallas_call(
        mix_kernel,
        grid=(blocks,),
        out_shape=jax.ShapeDtypeStruct((16, tokens // 8, span), bf16),
        in_specs=[pl.BlockSpec((1, tokens, width), lambda b: (b, 0, 0)),
                  pl.BlockSpec((width, span), lambda b: (b, 0)),
                  pl.BlockSpec((width, span), lambda b: (b, 0))],
        out_specs=pl.BlockSpec((16, tokens // 8, span), lambda b: (0, 0, 0)),
        scratch_shapes=[pltpu.VMEM((tokens, 2 * span), f32)],
        compiler_params=pltpu.CompilerParams(vmem_limit_bytes=32 << 20),
        cost_estimate=pl.CostEstimate(flops=2_400_000_000, transcendentals=0, bytes_accessed=9_000_000),
        name="mlp_out",
    )(hidden, own, mate)


def split_kernel(width, whole, blocks, sems):
    loads = [pltpu.make_async_copy(whole.at[:, pl.ds(b * width, width)], blocks.at[b], sems.at[b])
             for b in range(blocks.shape[0])]
    for load in loads:
        load.start()
    for load in loads:
        load.wait()


def split_call(whole, count):
    depth, width = whole.shape[0], whole.shape[1] // count
    hb = pl.BlockSpec(memory_space=pl.ANY)
    return pl.pallas_call(
        functools.partial(split_kernel, width),
        out_shape=jax.ShapeDtypeStruct((count, depth, width), whole.dtype),
        in_specs=[hb],
        out_specs=hb,
        scratch_shapes=[pltpu.SemaphoreType.DMA((count,))],
        cost_estimate=pl.CostEstimate(flops=0, transcendentals=0, bytes_accessed=2 * whole.size * 2),
        name="split_columns",
    )(whole)


def swap(value):
    return lax.ppermute(value, "core", [(0, 1), (1, 0)])


def patchify(pixels):
    count, side = pixels.shape[0], pixels.shape[1]
    grid = side // PATCH
    blocks = pixels.reshape(count, grid, PATCH, grid, PATCH, 3).transpose(0, 1, 3, 2, 4, 5)
    return blocks.reshape(count * grid * grid, PATCH * PATCH * 3)


def on_device(images, noise_field, stem_weight, level_one, down_weight, level_two, up_weight,
              out_weight, embed_weight, embed_bias, mlp_in, mlp_out):
    span = mlp_in.shape[0]
    own_in = lax.all_to_all(split_call(mlp_in, 8), ("zl", "y"), 0, 0)
    mate_out = swap(mlp_out)

    purified = score_call(images, noise_field, stem_weight, level_one, down_weight, level_two,
                          up_weight, out_weight)
    own_in, purified = lax.optimization_barrier((own_in, purified))
    mate_in = swap(own_in)
    patches = patchify(purified.astype(bf16))
    patches = jnp.pad(patches, ((0, 0), (0, 640 - patches.shape[1])))
    every = ("zh", "x", "zl", "y")
    tokens = lax.all_to_all(jnp.broadcast_to(patches[None], (64,) + patches.shape), every, 0, 0)
    tokens = tokens.reshape(-1, tokens.shape[-1])
    hidden, kept, sent = embed_call(tokens, embed_weight, embed_bias[None], own_in, mate_in, 8)
    other = swap(sent)
    hidden = lax.all_to_all(hidden, ("zl", "y"), 0, 0)
    shares = mix_call(hidden, mlp_out, mate_out)
    shares = lax.all_to_all(shares, ("zh", "x", "core"), 0, 0)
    mixed = jnp.sum(shares.reshape(8, 2, 8, 8, span).astype(f32), axis=0)
    core = lax.axis_index("core")
    values = jnp.where(core == 0, jnp.stack([kept, other]), jnp.stack([other, kept]))
    encoded = mixed + values.reshape(2, 8, 8, span).astype(f32)
    encoded = encoded.transpose(1, 0, 2, 3).reshape(128, span).astype(bf16)
    return purified, encoded


def solution(mesh):
    fine = Mesh(mesh.devices.reshape(2, 4, 2, 4, 2), ("zh", "x", "zl", "y", "core"))
    row, col = ("zh", "x"), ("zl", "y", "core")
    images = P(row + col, None, None, None)
    placed = (images, images) + (P(),) * 8 + (P(col, row), P(row, col))
    return jax.shard_map(on_device, mesh=fine, in_specs=placed, out_specs=(images, P(row, col)),
                         check_vma=False)
```

```python
import functools
import math

import jax
import jax.numpy as jnp
from jax import lax
from jax.experimental import pallas as pl
from jax.experimental.pallas import tpu as pltpu
from jax.sharding import Mesh, PartitionSpec as P

step_size = 0.25
noise_gain = math.sqrt(0.5)
ln_epsilon = 1e-06
PATCH = 14
W1, W2 = 32, 16
CH = 256
f32, bf16 = jnp.float32, jnp.bfloat16


def gelu(v):
    inner = v * (0.7978845608028654 + 0.035677408136300125 * (v * v))
    half = 0.5 * v
    return half + half * jnp.tanh(inner)


def score_kernel(side, count, images, noise, stem_w, l1_hbm, down_hbm, l2_hbm, up_hbm, out_w,
                 purified, pix, stem_x, stem_k, out_k, xa, xb, ca, cb, stream, coarse,
                 l1, down, l2, up, sems):
    half = side // 2
    span1, span2 = side * W1, half * W2
    pitch1, pitch2 = span1 + W1, span2 + W2
    loads = [pltpu.make_async_copy(l1_hbm.at[0], l1.at[0], sems.at[0]),
             pltpu.make_async_copy(l1_hbm.at[1], l1.at[1], sems.at[1]),
             pltpu.make_async_copy(down_hbm, down, sems.at[2]),
             pltpu.make_async_copy(l2_hbm, l2, sems.at[3]),
             pltpu.make_async_copy(up_hbm, up, sems.at[4]),
             pltpu.make_async_copy(l1_hbm.at[2], l1.at[2], sems.at[5]),
             pltpu.make_async_copy(l1_hbm.at[3], l1.at[3], sems.at[6])]
    for load in loads:
        load.start()

    chunk = span1 // 2
    per_image = 2
    mask1 = (lax.broadcasted_iota(jnp.int32, (chunk, 1), 0) % W1) < side
    mask2 = (lax.broadcasted_iota(jnp.int32, (span2, 1), 0) % W2) < half

    def read(rows):
        return jnp.concatenate([stream[0, rows, :], stream[1, rows, :]], axis=1)

    def write(rows, value):
        stream[0, rows, :] = value[:, 0:128]
        stream[1, rows, :] = value[:, 128:256]

    for i in range(count + 1):
        z1 = jnp.zeros((W1, 3 * CH), bf16)
        z2 = jnp.zeros((W2, 3 * CH), bf16)
        xa[i * pitch1:i * pitch1 + W1, :] = z1
        xb[i * pitch1:i * pitch1 + W1, :] = z1
        ca[i * pitch2:i * pitch2 + W2, :] = z2
        cb[i * pitch2:i * pitch2 + W2, :] = z2
        stem_x[i * pitch1:i * pitch1 + W1, :] = jnp.zeros((W1, 128), bf16)
    pix[...] = jnp.zeros_like(pix)
    stem_k[...] = jnp.zeros_like(stem_k)
    out_k[...] = jnp.zeros_like(out_k)
    for dy in range(3):
        stem_k[dy, 0:9, :] = stem_w[9 * dy:9 * dy + 9, :].astype(f32)
    out_k[:, 0:3] = out_w[...].astype(f32)

    for i in range(count):
        def put(y, _, i=i):
            base = pl.multiple_of(W1 + i * pitch1 + y * W1, W1)
            pix[pl.ds(base, side), 0:3] = images[i, y].astype(bf16).astype(f32)
            return 0
        lax.fori_loop(0, side, put, 0)

    def shifted(ref, base, value):
        n = value.shape[0]
        ref[pl.ds(base, n), 0:CH] = pltpu.roll(value, 1, 0).astype(bf16)
        ref[pl.ds(base, n), CH:2 * CH] = value.astype(bf16)
        ref[pl.ds(base, n), 2 * CH:3 * CH] = pltpu.roll(value, n - 1, 0).astype(bf16)

    def each(body):
        def step(t, _):
            base = W1 + (t // per_image) * pitch1 + (t % per_image) * chunk
            body(t, pl.multiple_of(base, W1))
            return 0
        lax.fori_loop(0, count * per_image, step, 0)

    def conv(ref, base, n, width, weights):
        acc = jnp.dot(ref[pl.ds(base - width, n), :], weights[0:3 * CH, :], preferred_element_type=f32)
        acc += jnp.dot(ref[pl.ds(base, n), :], weights[3 * CH:6 * CH, :], preferred_element_type=f32)
        acc += jnp.dot(ref[pl.ds(base + width, n), :], weights[6 * CH:9 * CH, :], preferred_element_type=f32)
        return acc

    def stem_cols(t, base):
        v = pix[pl.ds(base, chunk), :]
        left = pltpu.roll(v, 1, 0)
        right = pltpu.roll(v, chunk - 1, 0)
        stem_x[pl.ds(base, chunk), :] = (left + pltpu.roll(v, 3, 1) + pltpu.roll(right, 6, 1)).astype(bf16)
    each(stem_cols)

    def stem_conv(t, base):
        acc = jnp.dot(stem_x[pl.ds(base - W1, chunk), :], stem_k[0].astype(bf16), preferred_element_type=f32)
        acc += jnp.dot(stem_x[pl.ds(base, chunk), :], stem_k[1].astype(bf16), preferred_element_type=f32)
        acc += jnp.dot(stem_x[pl.ds(base + W1, chunk), :], stem_k[2].astype(bf16), preferred_element_type=f32)
        write(pl.ds(base, chunk), acc)
        shifted(xa, base, jnp.where(mask1, gelu(acc), 0.0))
    each(stem_conv)

    loads[0].wait()

    def layer0(t, base):
        s = read(pl.ds(base, chunk)) + conv(xa, base, chunk, W1, l1.at[0])
        write(pl.ds(base, chunk), s)
        shifted(xb, base, jnp.where(mask1, gelu(s), 0.0))
    each(layer0)

    loads[1].wait()

    def layer1(t, base):
        write(pl.ds(base, chunk), read(pl.ds(base, chunk)) + conv(xb, base, chunk, W1, l1.at[1]))
    each(layer1)

    loads[2].wait()
    loads[3].wait()
    loads[4].wait()
    for i in range(count):
        base1, base2 = W1 + i * pitch1, W2 + i * pitch2
        acc = None
        for b in range(2):
            cols = read(pl.ds(base1 + b, span1 // 2, stride=2)).astype(bf16).reshape(half, 2, W2, CH)
            for a in range(2):
                part = jnp.dot(cols[:, a].reshape(span2, CH), down[(2 * a + b) * CH:(2 * a + b + 1) * CH, :],
                               preferred_element_type=f32)
                acc = part if acc is None else acc + part
        coarse[base2:base2 + span2, :] = acc
        shifted(ca, base2, jnp.where(mask2, gelu(acc), 0.0))
    for i in range(count):
        base2 = W2 + i * pitch2
        s = coarse[base2:base2 + span2, :] + conv(ca, base2, span2, W2, l2.at[0])
        coarse[base2:base2 + span2, :] = s
        shifted(cb, base2, jnp.where(mask2, gelu(s), 0.0))
    for i in range(count):
        base1, base2 = W1 + i * pitch1, W2 + i * pitch2
        s = coarse[base2:base2 + span2, :] + conv(cb, base2, span2, W2, l2.at[1])
        s = s.astype(bf16)
        for a in range(2):
            for b in range(2):
                g = (2 * a + b) * CH
                part = jnp.dot(s, up[:, g:g + CH], preferred_element_type=f32)
                for y in range(half):
                    rows = pl.ds(base1 + (2 * y + a) * W1 + b, W2, stride=2)
                    write(rows, read(rows) + part[y * W2:(y + 1) * W2, :])

    def enter(t, base):
        shifted(xa, base, jnp.where(mask1, gelu(read(pl.ds(base, chunk))), 0.0))
    each(enter)

    loads[5].wait()

    def layer2(t, base):
        s = read(pl.ds(base, chunk)) + conv(xa, base, chunk, W1, l1.at[2])
        write(pl.ds(base, chunk), s)
        shifted(xb, base, jnp.where(mask1, gelu(s), 0.0))
    each(layer2)

    loads[6].wait()
    lines = chunk // W1

    def layer3(t, base):
        s = read(pl.ds(base, chunk)) + conv(xb, base, chunk, W1, l1.at[3])
        score = jnp.dot(gelu(s).astype(bf16), out_k[...].astype(bf16), preferred_element_type=f32)
        i, y0 = t // per_image, (t % per_image) * lines
        for y in range(lines):
            purified[i, y0 + y] = (images[i, y0 + y] + step_size * score[y * W1:y * W1 + side, 0:3]
                                   + noise_gain * noise[i, y0 + y])
    each(layer3)


def score_call(images, noise, stem_w, l1, down, l2, up, out_w):
    count, side = images.shape[0], images.shape[1]
    rows1 = W1 + count * (side + 1) * W1
    rows2 = W2 + count * (side // 2 + 1) * W2
    vm = pl.BlockSpec(memory_space=pltpu.VMEM)
    hb = pl.BlockSpec(memory_space=pl.ANY)
    return pl.pallas_call(
        functools.partial(score_kernel, side, count),
        out_shape=jax.ShapeDtypeStruct(images.shape, f32),
        in_specs=[vm, vm, vm, hb, hb, hb, hb, vm],
        out_specs=vm,
        scratch_shapes=[
            pltpu.VMEM((rows1, 128), f32),
            pltpu.VMEM((rows1, 128), bf16),
            pltpu.VMEM((3, 128, CH), f32),
            pltpu.VMEM((CH, 128), f32),
            pltpu.VMEM((rows1, 3 * CH), bf16),
            pltpu.VMEM((rows1, 3 * CH), bf16),
            pltpu.VMEM((rows2, 3 * CH), bf16),
            pltpu.VMEM((rows2, 3 * CH), bf16),
            pltpu.VMEM((CH // 128, rows1, 128), f32),
            pltpu.VMEM((rows2, CH), f32),
            pltpu.VMEM(l1.shape, bf16),
            pltpu.VMEM(down.shape, bf16),
            pltpu.VMEM(l2.shape, bf16),
            pltpu.VMEM(up.shape, bf16),
            pltpu.SemaphoreType.DMA((7,)),
        ],
        compiler_params=pltpu.CompilerParams(vmem_limit_bytes=48 << 20),
        cost_estimate=pl.CostEstimate(flops=10_000_000_000, transcendentals=3_000_000, bytes_accessed=12_000_000),
        name="score_net",
    )(images, noise, stem_w, l1, down, l2, up, out_w)


def embed_kernel(parts, patches, weight_hbm, bias, own_hbm, mate_hbm, hidden, kept, sent,
                 weight, own, mate, field, total, sums, squares, sems):
    core = lax.axis_index("core")
    row = lax.axis_index("zh") * lax.axis_size("x") + lax.axis_index("x")
    tokens, depth = patches.shape[0], weight_hbm.shape[0]
    blocks, span, width = own_hbm.shape
    group = weight_hbm.shape[1] // parts
    loads = [pltpu.make_async_copy(weight_hbm.at[:, pl.ds(g * group, group)], weight.at[g], sems.at[g])
             for g in range(parts)]
    loads.append(pltpu.make_async_copy(own_hbm, own, sems.at[parts]))
    loads.append(pltpu.make_async_copy(mate_hbm, mate, sems.at[parts + 1]))
    for load in loads:
        load.start()
    sums[...] = jnp.zeros_like(sums)
    squares[...] = jnp.zeros_like(squares)
    pixels = patches[:, 0:depth]
    for g in range(parts):
        loads[g].wait()

        def embed(k, _, g=g):
            at = pl.multiple_of(k * span, 128)
            there = pl.multiple_of(g * group + k * span, 128)
            e = jnp.dot(pixels, weight[g, :, pl.ds(at, span)], preferred_element_type=f32)
            e = (e + bias[:, pl.ds(there, span)]).astype(bf16)
            field[:, pl.ds(there, span)] = e
            v = e.astype(f32)
            q = v * v
            a, b = sums[...], squares[...]
            for lane in range(0, span, 128):
                a += v[:, lane:lane + 128]
                b += q[:, lane:lane + 128]
            sums[...] = a
            squares[...] = b
            return 0
        lax.fori_loop(0, group // span, embed, 0)
    count = parts * group
    mean = jnp.sum(sums[...], axis=1, keepdims=True) / count
    square = jnp.sum(squares[...], axis=1, keepdims=True) / count
    scale = lax.rsqrt(square - mean * mean + ln_epsilon)
    place = lax.axis_index("zl") * lax.axis_size("y") + lax.axis_index("y")
    share = tokens // 8
    rows = pl.ds(pl.multiple_of(row * share, share), share)
    kept[...] = field[rows, pl.ds(pl.multiple_of((2 * place + core) * span, 128), span)]
    sent[...] = field[rows, pl.ds(pl.multiple_of((2 * place + 1 - core) * span, 128), span)]
    total[...] = jnp.zeros_like(total)
    loads[parts].wait()
    loads[parts + 1].wait()

    def mix(b, _):
        for block, side in ((own, core), (mate, 1 - core)):
            at = pl.multiple_of((2 * b + side) * span, 128)
            v = field[:, pl.ds(at, span)].astype(f32)
            normed = ((v - mean) * scale).astype(bf16)
            total[...] += jnp.dot(normed, block[b], preferred_element_type=f32)
        return 0
    lax.fori_loop(0, blocks, mix, 0)
    value = gelu(total[...]).astype(bf16)
    grouped = value.reshape(8, 2, 4 * 8, width)
    for side in range(2):
        part = grouped[:, side].reshape(tokens // 2, width)
        for y in range(4):
            hidden[4 * side + y] = part


def embed_call(patches, weight, bias, own, mate):
    tokens, blocks, span, width = patches.shape[0], *own.shape
    features = weight.shape[1]
    parts = 4
    share = tokens // 8
    vm = pl.BlockSpec(memory_space=pltpu.VMEM)
    hb = pl.BlockSpec(memory_space=pl.ANY)
    return pl.pallas_call(
        functools.partial(embed_kernel, parts),
        out_shape=(jax.ShapeDtypeStruct((8, tokens // 2, width), bf16),
                   jax.ShapeDtypeStruct((share, span), bf16),
                   jax.ShapeDtypeStruct((share, span), bf16)),
        in_specs=[vm, hb, vm, hb, hb],
        out_specs=(vm, vm, vm),
        scratch_shapes=[
            pltpu.VMEM((parts, weight.shape[0], features // parts), bf16),
            pltpu.VMEM(own.shape, bf16),
            pltpu.VMEM(mate.shape, bf16),
            pltpu.VMEM((tokens, features), bf16),
            pltpu.VMEM((tokens, width), f32),
            pltpu.VMEM((tokens, 128), f32),
            pltpu.VMEM((tokens, 128), f32),
            pltpu.SemaphoreType.DMA((parts + 2,)),
        ],
        compiler_params=pltpu.CompilerParams(vmem_limit_bytes=48 << 20),
        cost_estimate=pl.CostEstimate(flops=7_000_000_000, transcendentals=200_000, bytes_accessed=20_000_000),
        name="embed_mlp",
    )(patches, weight, bias, own, mate)


def mix_kernel(hidden, own, mate, far, far_mate, out, total):
    b = pl.program_id(0)
    span = own.shape[1]

    @pl.when(b == 0)
    def _():
        total[...] = jnp.zeros_like(total)
    h = hidden[0]
    for k, weight in enumerate((own, mate, far, far_mate)):
        total[:, k * span:(k + 1) * span] += jnp.dot(h, weight[...], preferred_element_type=f32)

    @pl.when(b == pl.num_programs(0) - 1)
    def _():
        core, side = lax.axis_index("core"), lax.axis_index("zl")
        share = out.shape[1]
        for r in range(out.shape[0] // 4):
            rows = slice(r * share, (r + 1) * share)
            for k in range(4):
                to_side = side if k < 2 else 1 - side
                to_core = core if k % 2 == 0 else 1 - core
                out[4 * r + 2 * to_side + to_core] = total[rows, k * span:(k + 1) * span].astype(bf16)


def mix_call(hidden, *weights):
    blocks, tokens, width = hidden.shape
    span = weights[0].shape[1]
    shape = (32, tokens // 8, span)
    return pl.pallas_call(
        mix_kernel,
        grid=(blocks,),
        out_shape=jax.ShapeDtypeStruct(shape, bf16),
        in_specs=[pl.BlockSpec((1, tokens, width), lambda b: (b, 0, 0))]
        + [pl.BlockSpec((width, span), lambda b: (b, 0))] * 4,
        out_specs=pl.BlockSpec(shape, lambda b: (0, 0, 0)),
        scratch_shapes=[pltpu.VMEM((tokens, 4 * span), f32)],
        compiler_params=pltpu.CompilerParams(vmem_limit_bytes=32 << 20),
        cost_estimate=pl.CostEstimate(flops=2_400_000_000, transcendentals=0, bytes_accessed=12_000_000),
        name="mlp_out",
    )(hidden, *weights)


def split_kernel(whole, blocks):
    blocks[0] = whole[...]


def split_call(whole, count):
    depth, width = whole.shape[0], whole.shape[1] // count
    return pl.pallas_call(
        split_kernel,
        grid=(count,),
        out_shape=jax.ShapeDtypeStruct((count, depth, width), whole.dtype),
        in_specs=[pl.BlockSpec((depth, width), lambda b: (0, b))],
        out_specs=pl.BlockSpec((1, depth, width), lambda b: (b, 0, 0)),
        cost_estimate=pl.CostEstimate(flops=0, transcendentals=0, bytes_accessed=2 * whole.size * 2),
        name="split_columns",
    )(whole)


def swap(value):
    return lax.ppermute(value, "core", [(0, 1), (1, 0)])


def patchify(pixels):
    count, side = pixels.shape[0], pixels.shape[1]
    grid = side // PATCH
    blocks = pixels.reshape(count, grid, PATCH, grid, PATCH, 3).transpose(0, 1, 3, 2, 4, 5)
    return blocks.reshape(count * grid * grid, PATCH * PATCH * 3)


def on_device(images, noise_field, stem_weight, level_one, down_weight, level_two, up_weight,
              out_weight, embed_weight, embed_bias, mlp_in, mlp_out):
    span = mlp_in.shape[0]
    own_in = lax.all_to_all(split_call(mlp_in, 8), ("zl", "y"), 0, 0)
    far_out = lax.ppermute(mlp_out, "zl", [(0, 1), (1, 0)])

    purified = score_call(images, noise_field, stem_weight, level_one, down_weight, level_two,
                          up_weight, out_weight)
    patches = patchify(purified.astype(bf16))
    patches = jnp.pad(patches, ((0, 0), (0, 640 - patches.shape[1])))
    own_in, _ = lax.optimization_barrier((own_in, patches))
    mate_in = swap(own_in)
    every = ("zh", "x", "zl", "y")
    tokens = lax.all_to_all(jnp.broadcast_to(patches[None], (64,) + patches.shape), every, 0, 0)
    tokens = tokens.reshape(-1, tokens.shape[-1])
    hidden, kept, sent = embed_call(tokens, embed_weight, embed_bias[None], own_in, mate_in)
    far_out, hidden = lax.optimization_barrier((far_out, hidden))
    mate_out, far_mate_out = swap(mlp_out), swap(far_out)
    other = swap(sent)
    hidden = lax.all_to_all(hidden, ("zl", "y"), 0, 0)
    shares = mix_call(hidden, mlp_out, mate_out, far_out, far_mate_out)
    shares = lax.all_to_all(shares, ("zh", "x", "zl", "core"), 0, 0)
    mixed = jnp.sum(shares.reshape(8, 2, 2, 4, 8, span).astype(f32), axis=0)
    mixed = mixed.transpose(1, 0, 2, 3, 4).reshape(2, 8, 8, span)
    core = lax.axis_index("core")
    values = jnp.where(core == 0, jnp.stack([kept, other]), jnp.stack([other, kept]))
    encoded = mixed + values.reshape(2, 8, 8, span).astype(f32)
    encoded = encoded.transpose(1, 0, 2, 3).reshape(128, span).astype(bf16)
    return purified, encoded


def solution(mesh):
    fine = Mesh(mesh.devices.reshape(2, 4, 2, 4, 2), ("zh", "x", "zl", "y", "core"))
    row, col = ("zh", "x"), ("zl", "y", "core")
    images = P(row + col, None, None, None)
    placed = (images, images) + (P(),) * 8 + (P(col, row), P(row, col))
    return jax.shard_map(on_device, mesh=fine, in_specs=placed, out_specs=(images, P(row, col)),
                         check_vma=False)
```

```python
import functools
import math

import jax
import jax.numpy as jnp
from jax import lax
from jax.experimental import pallas as pl
from jax.experimental.pallas import tpu as pltpu
from jax.sharding import Mesh, PartitionSpec as P

step_size = 0.25
noise_gain = math.sqrt(0.5)
ln_epsilon = 1e-06
PATCH = 14
W1, W2 = 32, 16
CH = 256
f32, bf16 = jnp.float32, jnp.bfloat16


def gelu(v):
    inner = v * (0.7978845608028654 + 0.035677408136300125 * (v * v))
    half = 0.5 * v
    return half + half * jnp.tanh(inner)


def score_kernel(side, count, images, noise, stem_w, l1_hbm, down_hbm, l2_hbm, up_hbm, out_w,
                 purified, pix, stem_x, stem_k, out_k, xa, xb, ca, cb, stream, coarse,
                 l1, down, l2, up, sems):
    half = side // 2
    span1, span2 = side * W1, half * W2
    pitch1, pitch2 = span1 + W1, span2 + W2
    loads = [pltpu.make_async_copy(l1_hbm.at[0], l1.at[0], sems.at[0]),
             pltpu.make_async_copy(l1_hbm.at[1], l1.at[1], sems.at[1]),
             pltpu.make_async_copy(down_hbm, down, sems.at[2]),
             pltpu.make_async_copy(l2_hbm, l2, sems.at[3]),
             pltpu.make_async_copy(up_hbm, up, sems.at[4]),
             pltpu.make_async_copy(l1_hbm.at[2], l1.at[2], sems.at[5]),
             pltpu.make_async_copy(l1_hbm.at[3], l1.at[3], sems.at[6])]
    for load in loads:
        load.start()

    chunk = span1 // 2
    per_image = 2
    mask1 = (lax.broadcasted_iota(jnp.int32, (chunk, 1), 0) % W1) < side
    mask2 = (lax.broadcasted_iota(jnp.int32, (span2, 1), 0) % W2) < half

    def read(rows):
        return jnp.concatenate([stream[0, rows, :], stream[1, rows, :]], axis=1)

    def write(rows, value):
        stream[0, rows, :] = value[:, 0:128]
        stream[1, rows, :] = value[:, 128:256]

    for i in range(count + 1):
        z1 = jnp.zeros((W1, 3 * CH), bf16)
        z2 = jnp.zeros((W2, 3 * CH), bf16)
        xa[i * pitch1:i * pitch1 + W1, :] = z1
        xb[i * pitch1:i * pitch1 + W1, :] = z1
        ca[i * pitch2:i * pitch2 + W2, :] = z2
        cb[i * pitch2:i * pitch2 + W2, :] = z2
        stem_x[i * pitch1:i * pitch1 + W1, :] = jnp.zeros((W1, 128), bf16)
    pix[...] = jnp.zeros_like(pix)
    stem_k[...] = jnp.zeros_like(stem_k)
    out_k[...] = jnp.zeros_like(out_k)
    for dy in range(3):
        stem_k[dy, 0:9, :] = stem_w[9 * dy:9 * dy + 9, :].astype(f32)
    out_k[:, 0:3] = out_w[...].astype(f32)

    for i in range(count):
        def put(y, _, i=i):
            base = pl.multiple_of(W1 + i * pitch1 + y * W1, W1)
            pix[pl.ds(base, side), 0:3] = images[i, y].astype(bf16).astype(f32)
            return 0
        lax.fori_loop(0, side, put, 0)

    def shifted(ref, base, value):
        n = value.shape[0]
        ref[pl.ds(base, n), 0:CH] = pltpu.roll(value, 1, 0).astype(bf16)
        ref[pl.ds(base, n), CH:2 * CH] = value.astype(bf16)
        ref[pl.ds(base, n), 2 * CH:3 * CH] = pltpu.roll(value, n - 1, 0).astype(bf16)

    def each(body):
        def step(t, _):
            base = W1 + (t // per_image) * pitch1 + (t % per_image) * chunk
            body(t, pl.multiple_of(base, W1))
            return 0
        lax.fori_loop(0, count * per_image, step, 0)

    def conv(ref, base, n, width, weights):
        acc = jnp.dot(ref[pl.ds(base - width, n), :], weights[0:3 * CH, :], preferred_element_type=f32)
        acc += jnp.dot(ref[pl.ds(base, n), :], weights[3 * CH:6 * CH, :], preferred_element_type=f32)
        acc += jnp.dot(ref[pl.ds(base + width, n), :], weights[6 * CH:9 * CH, :], preferred_element_type=f32)
        return acc

    def stem_cols(t, base):
        v = pix[pl.ds(base, chunk), :]
        left = pltpu.roll(v, 1, 0)
        right = pltpu.roll(v, chunk - 1, 0)
        stem_x[pl.ds(base, chunk), :] = (left + pltpu.roll(v, 3, 1) + pltpu.roll(right, 6, 1)).astype(bf16)
    each(stem_cols)

    def stem_conv(t, base):
        acc = jnp.dot(stem_x[pl.ds(base - W1, chunk), :], stem_k[0].astype(bf16), preferred_element_type=f32)
        acc += jnp.dot(stem_x[pl.ds(base, chunk), :], stem_k[1].astype(bf16), preferred_element_type=f32)
        acc += jnp.dot(stem_x[pl.ds(base + W1, chunk), :], stem_k[2].astype(bf16), preferred_element_type=f32)
        write(pl.ds(base, chunk), acc)
        shifted(xa, base, jnp.where(mask1, gelu(acc), 0.0))
    each(stem_conv)

    loads[0].wait()

    def layer0(t, base):
        s = read(pl.ds(base, chunk)) + conv(xa, base, chunk, W1, l1.at[0])
        write(pl.ds(base, chunk), s)
        shifted(xb, base, jnp.where(mask1, gelu(s), 0.0))
    each(layer0)

    loads[1].wait()

    def layer1(t, base):
        write(pl.ds(base, chunk), read(pl.ds(base, chunk)) + conv(xb, base, chunk, W1, l1.at[1]))
    each(layer1)

    loads[2].wait()
    loads[3].wait()
    loads[4].wait()
    for i in range(count):
        base1, base2 = W1 + i * pitch1, W2 + i * pitch2
        acc = None
        for b in range(2):
            cols = read(pl.ds(base1 + b, span1 // 2, stride=2)).astype(bf16).reshape(half, 2, W2, CH)
            for a in range(2):
                part = jnp.dot(cols[:, a].reshape(span2, CH), down[(2 * a + b) * CH:(2 * a + b + 1) * CH, :],
                               preferred_element_type=f32)
                acc = part if acc is None else acc + part
        coarse[base2:base2 + span2, :] = acc
        shifted(ca, base2, jnp.where(mask2, gelu(acc), 0.0))
    for i in range(count):
        base2 = W2 + i * pitch2
        s = coarse[base2:base2 + span2, :] + conv(ca, base2, span2, W2, l2.at[0])
        coarse[base2:base2 + span2, :] = s
        shifted(cb, base2, jnp.where(mask2, gelu(s), 0.0))
    for i in range(count):
        base1, base2 = W1 + i * pitch1, W2 + i * pitch2
        s = coarse[base2:base2 + span2, :] + conv(cb, base2, span2, W2, l2.at[1])
        s = s.astype(bf16)
        for a in range(2):
            for b in range(2):
                g = (2 * a + b) * CH
                part = jnp.dot(s, up[:, g:g + CH], preferred_element_type=f32)
                for y in range(half):
                    rows = pl.ds(base1 + (2 * y + a) * W1 + b, W2, stride=2)
                    write(rows, read(rows) + part[y * W2:(y + 1) * W2, :])

    def enter(t, base):
        shifted(xa, base, jnp.where(mask1, gelu(read(pl.ds(base, chunk))), 0.0))
    each(enter)

    loads[5].wait()

    def layer2(t, base):
        s = read(pl.ds(base, chunk)) + conv(xa, base, chunk, W1, l1.at[2])
        write(pl.ds(base, chunk), s)
        shifted(xb, base, jnp.where(mask1, gelu(s), 0.0))
    each(layer2)

    loads[6].wait()
    lines = chunk // W1

    def layer3(t, base):
        s = read(pl.ds(base, chunk)) + conv(xb, base, chunk, W1, l1.at[3])
        score = jnp.dot(gelu(s).astype(bf16), out_k[...].astype(bf16), preferred_element_type=f32)
        i, y0 = t // per_image, (t % per_image) * lines
        for y in range(lines):
            purified[i, y0 + y] = (images[i, y0 + y] + step_size * score[y * W1:y * W1 + side, 0:3]
                                   + noise_gain * noise[i, y0 + y])
    each(layer3)


def score_call(images, noise, stem_w, l1, down, l2, up, out_w):
    count, side = images.shape[0], images.shape[1]
    rows1 = W1 + count * (side + 1) * W1
    rows2 = W2 + count * (side // 2 + 1) * W2
    vm = pl.BlockSpec(memory_space=pltpu.VMEM)
    hb = pl.BlockSpec(memory_space=pl.ANY)
    return pl.pallas_call(
        functools.partial(score_kernel, side, count),
        out_shape=jax.ShapeDtypeStruct(images.shape, f32),
        in_specs=[vm, vm, vm, hb, hb, hb, hb, vm],
        out_specs=vm,
        scratch_shapes=[
            pltpu.VMEM((rows1, 128), f32),
            pltpu.VMEM((rows1, 128), bf16),
            pltpu.VMEM((3, 128, CH), f32),
            pltpu.VMEM((CH, 128), f32),
            pltpu.VMEM((rows1, 3 * CH), bf16),
            pltpu.VMEM((rows1, 3 * CH), bf16),
            pltpu.VMEM((rows2, 3 * CH), bf16),
            pltpu.VMEM((rows2, 3 * CH), bf16),
            pltpu.VMEM((CH // 128, rows1, 128), f32),
            pltpu.VMEM((rows2, CH), f32),
            pltpu.VMEM(l1.shape, bf16),
            pltpu.VMEM(down.shape, bf16),
            pltpu.VMEM(l2.shape, bf16),
            pltpu.VMEM(up.shape, bf16),
            pltpu.SemaphoreType.DMA((7,)),
        ],
        compiler_params=pltpu.CompilerParams(vmem_limit_bytes=48 << 20),
        cost_estimate=pl.CostEstimate(flops=10_000_000_000, transcendentals=3_000_000, bytes_accessed=12_000_000),
        name="score_net",
    )(images, noise, stem_w, l1, down, l2, up, out_w)


def embed_kernel(parts, patches, weight_hbm, bias, own_hbm, mate_hbm, hidden, kept, sent,
                 weight, mixer, total, sums, squares, sems, own_sems, mate_sems):
    core = lax.axis_index("core")
    row = lax.axis_index("zh") * lax.axis_size("x") + lax.axis_index("x")
    place = lax.axis_index("zl") * lax.axis_size("y") + lax.axis_index("y")
    tokens, depth = patches.shape[0], weight_hbm.shape[0]
    blocks, span, width = own_hbm.shape
    group = weight_hbm.shape[1] // parts
    count = parts * group
    step = 512

    def piece(b, side, source, sem):
        at = pl.multiple_of((2 * b + side) * span, span)
        return pltpu.make_async_copy(source.at[b], mixer.at[pl.ds(at, span), :], sem.at[b])

    loads = [pltpu.make_async_copy(weight_hbm.at[:, pl.ds(g * group, group)], weight.at[g], sems.at[g])
             for g in range(parts)]
    pieces = [(piece(b, core, own_hbm, own_sems), piece(b, 1 - core, mate_hbm, mate_sems)) for b in range(blocks)]
    loads[0].start()
    for pair in pieces[:2]:
        pair[0].start()
        pair[1].start()
    for load in loads[1:]:
        load.start()
    for pair in pieces[2:]:
        pair[0].start()
        pair[1].start()
    pixels = patches[:, 0:depth]
    ones = jnp.ones((16, step), bf16)
    ready = 0
    for c in range(count // step):
        g, at = (c * step) // group, (c * step) % group
        if at == 0:
            loads[g].wait()
        e = jnp.dot(pixels, weight[g, :, at:at + step], preferred_element_type=f32)
        e = (e + bias[:, c * step:(c + 1) * step]).astype(bf16)
        v = e.astype(f32)
        q = v * v
        a = v[:, 0:128] + v[:, 128:256] + v[:, 256:384] + v[:, 384:512]
        b = q[:, 0:128] + q[:, 128:256] + q[:, 256:384] + q[:, 384:512]
        sums[...] = a if c == 0 else sums[...] + a
        squares[...] = b if c == 0 else squares[...] + b
        while ready * 2 * span < (c + 1) * step:
            pieces[ready][0].wait()
            pieces[ready][1].wait()
            ready += 1
        part = jnp.dot(jnp.concatenate([e, ones], axis=0), mixer[c * step:(c + 1) * step, :],
                       preferred_element_type=f32)
        total[...] = part if c == 0 else total[...] + part
    share = tokens // 8
    mine = patches[pl.ds(pl.multiple_of(row * share, share), share), 0:depth]
    for out, side in ((kept, core), (sent, 1 - core)):
        first = 2 * place + side
        g, at = first // (group // span), first % (group // span)
        e = jnp.dot(mine, weight[g, :, pl.ds(pl.multiple_of(at * span, 128), span)], preferred_element_type=f32)
        out[...] = (e + bias[:, pl.ds(pl.multiple_of(first * span, 128), span)]).astype(bf16)
    mean = jnp.sum(sums[...], axis=1, keepdims=True) / count
    square = jnp.sum(squares[...], axis=1, keepdims=True) / count
    scale = lax.rsqrt(square - mean * mean + ln_epsilon)
    column = total[tokens:tokens + 1, :]
    value = gelu((total[0:tokens, :] - mean * column) * scale).astype(bf16)
    for b in range(hidden.shape[0]):
        hidden[b] = value


def embed_call(patches, weight, bias, own, mate):
    tokens = patches.shape[0]
    _, span, width = own.shape
    features = weight.shape[1]
    parts = 4
    share = tokens // 8
    vm = pl.BlockSpec(memory_space=pltpu.VMEM)
    hb = pl.BlockSpec(memory_space=pl.ANY)
    return pl.pallas_call(
        functools.partial(embed_kernel, parts),
        out_shape=(jax.ShapeDtypeStruct((8, tokens, width), bf16),
                   jax.ShapeDtypeStruct((share, span), bf16),
                   jax.ShapeDtypeStruct((share, span), bf16)),
        in_specs=[vm, hb, vm, hb, hb],
        out_specs=(vm, vm, vm),
        scratch_shapes=[
            pltpu.VMEM((parts, weight.shape[0], features // parts), bf16),
            pltpu.VMEM((features, width), bf16),
            pltpu.VMEM((tokens + 16, width), f32),
            pltpu.VMEM((tokens, 128), f32),
            pltpu.VMEM((tokens, 128), f32),
            pltpu.SemaphoreType.DMA((parts,)),
            pltpu.SemaphoreType.DMA((8,)),
            pltpu.SemaphoreType.DMA((8,)),
        ],
        compiler_params=pltpu.CompilerParams(vmem_limit_bytes=40 << 20),
        cost_estimate=pl.CostEstimate(flops=7_000_000_000, transcendentals=200_000, bytes_accessed=20_000_000),
        name="embed_mlp",
    )(patches, weight, bias, own, mate)


def mix_kernel(hidden_hbm, own_hbm, mate_hbm, out, hidden, weight, total, sems):
    core = lax.axis_index("core")
    blocks, tokens, width = hidden_hbm.shape
    span = own_hbm.shape[1]
    parts = blocks // 2
    deep = 2 * width
    loads = []
    for k in range(parts):
        rows = pl.ds(k * deep, deep)
        pairs = [(own_hbm.at[rows, :], weight.at[rows, pl.ds(0, span)]),
                 (mate_hbm.at[rows, :], weight.at[rows, pl.ds(span, span)])]
        pairs += [(hidden_hbm.at[b], hidden.at[:, pl.ds(b * width, width)]) for b in (2 * k, 2 * k + 1)]
        loads.append([pltpu.make_async_copy(a, b, sems.at[k, n]) for n, (a, b) in enumerate(pairs)])
        for load in loads[-1]:
            load.start()
    for k in range(parts):
        for load in loads[k]:
            load.wait()
        at = slice(k * deep, (k + 1) * deep)
        part = jnp.dot(hidden[:, at], weight[at, :], preferred_element_type=f32)
        if k == 0:
            total[...] = part
        elif k < parts - 1:
            total[...] += part
        else:
            done = (total[...] + part).astype(bf16)
    share = out.shape[1]
    for r in range(tokens // share):
        rows = slice(r * share, (r + 1) * share)
        out[2 * r + core] = done[rows, 0:span]
        out[2 * r + 1 - core] = done[rows, span:2 * span]


def mix_call(hidden, own, mate):
    blocks, tokens, width = hidden.shape
    depth, span = own.shape
    hb = pl.BlockSpec(memory_space=pl.ANY)
    return pl.pallas_call(
        mix_kernel,
        out_shape=jax.ShapeDtypeStruct((16, tokens // 8, span), bf16),
        in_specs=[hb, hb, hb],
        out_specs=pl.BlockSpec(memory_space=pltpu.VMEM),
        scratch_shapes=[
            pltpu.VMEM((tokens, depth), bf16),
            pltpu.VMEM((depth, 2 * span), bf16),
            pltpu.VMEM((tokens, 2 * span), f32),
            pltpu.SemaphoreType.DMA((blocks // 2, 4)),
        ],
        compiler_params=pltpu.CompilerParams(vmem_limit_bytes=24 << 20),
        cost_estimate=pl.CostEstimate(flops=2_400_000_000, transcendentals=0, bytes_accessed=9_000_000),
        name="mlp_out",
    )(hidden, own, mate)


def split_kernel(whole, blocks):
    width = blocks.shape[2]
    for b in range(blocks.shape[0]):
        blocks[b] = whole[:, b * width:(b + 1) * width]


def split_call(whole, count):
    depth, width = whole.shape[0], whole.shape[1] // count
    return pl.pallas_call(
        split_kernel,
        grid=(count // 2,),
        out_shape=jax.ShapeDtypeStruct((count, depth, width), whole.dtype),
        in_specs=[pl.BlockSpec((depth, 2 * width), lambda b: (0, b))],
        out_specs=pl.BlockSpec((2, depth, width), lambda b: (b, 0, 0)),
        cost_estimate=pl.CostEstimate(flops=0, transcendentals=0, bytes_accessed=2 * whole.size * 2),
        name="split_columns",
    )(whole)


def swap(value):
    return lax.ppermute(value, "core", [(0, 1), (1, 0)])


def patchify(pixels):
    count, side = pixels.shape[0], pixels.shape[1]
    grid = side // PATCH
    blocks = pixels.reshape(count, grid, PATCH, grid, PATCH, 3).transpose(0, 1, 3, 2, 4, 5)
    return blocks.reshape(count * grid * grid, PATCH * PATCH * 3)


def on_device(images, noise_field, stem_weight, level_one, down_weight, level_two, up_weight,
              out_weight, embed_weight, embed_bias, mlp_in, mlp_out):
    span = mlp_in.shape[0]
    own_in = lax.all_to_all(split_call(mlp_in, 8), ("zl", "y"), 0, 0)
    mate_out = swap(mlp_out)

    purified = score_call(images, noise_field, stem_weight, level_one, down_weight, level_two,
                          up_weight, out_weight)
    patches = patchify(purified.astype(bf16))
    patches = jnp.pad(patches, ((0, 0), (0, 640 - patches.shape[1])))
    own_in, mate_out, _ = lax.optimization_barrier((own_in, mate_out, patches))
    mate_in = swap(own_in)
    every = ("zh", "x", "zl", "y")
    tokens = lax.all_to_all(jnp.broadcast_to(patches[None], (64,) + patches.shape), every, 0, 0)
    tokens = tokens.reshape(-1, tokens.shape[-1])
    hidden, kept, sent = embed_call(tokens, embed_weight, embed_bias[None], own_in, mate_in)
    other = swap(sent)
    hidden = lax.all_to_all(hidden, ("zl", "y"), 0, 0)
    shares = mix_call(hidden, mlp_out, mate_out)
    shares = lax.all_to_all(shares, ("zh", "x", "core"), 0, 0)
    mixed = jnp.sum(shares.reshape(8, 2, 8, 8, span).astype(f32), axis=0)
    core = lax.axis_index("core")
    values = jnp.where(core == 0, jnp.stack([kept, other]), jnp.stack([other, kept]))
    encoded = mixed + values.reshape(2, 8, 8, span).astype(f32)
    encoded = encoded.transpose(1, 0, 2, 3).reshape(128, span).astype(bf16)
    return purified, encoded


def solution(mesh):
    fine = Mesh(mesh.devices.reshape(2, 4, 2, 4, 2), ("zh", "x", "zl", "y", "core"))
    row, col = ("zh", "x"), ("zl", "y", "core")
    images = P(row + col, None, None, None)
    placed = (images, images) + (P(),) * 8 + (P(col, row), P(row, col))
    return jax.shard_map(on_device, mesh=fine, in_specs=placed, out_specs=(images, P(row, col)),
                         check_vma=False)
```

```python
import functools
import math

import jax
import jax.numpy as jnp
from jax import lax
from jax.experimental import pallas as pl
from jax.experimental.pallas import tpu as pltpu
from jax.sharding import Mesh, PartitionSpec as P

step_size = 0.25
noise_gain = math.sqrt(0.5)
ln_epsilon = 1e-06
PATCH = 14
W1, W2 = 32, 16
CH = 256
f32, bf16 = jnp.float32, jnp.bfloat16


def gelu(v):
    inner = v * (0.7978845608028654 + 0.035677408136300125 * (v * v))
    half = 0.5 * v
    return half + half * jnp.tanh(inner)


def score_kernel(side, count, images, noise, stem_w, l1_hbm, down_hbm, l2_hbm, up_hbm, out_w,
                 purified, patches, raw, extra, pix, stem_x, stem_k, out_k, xa, xb, ca, cb, stream, coarse,
                 l1, down, l2, up, sems):
    half = side // 2
    span1, span2 = side * W1, half * W2
    pitch1, pitch2 = span1 + W1, span2 + W2
    loads = [pltpu.make_async_copy(l1_hbm.at[0], l1.at[0], sems.at[0]),
             pltpu.make_async_copy(l1_hbm.at[1], l1.at[1], sems.at[1]),
             pltpu.make_async_copy(down_hbm, down, sems.at[2]),
             pltpu.make_async_copy(l2_hbm, l2, sems.at[3]),
             pltpu.make_async_copy(up_hbm, up, sems.at[4]),
             pltpu.make_async_copy(l1_hbm.at[2], l1.at[2], sems.at[5]),
             pltpu.make_async_copy(l1_hbm.at[3], l1.at[3], sems.at[6])]
    for load in loads:
        load.start()

    mask1 = (lax.broadcasted_iota(jnp.int32, (span1, 1), 0) % W1) < side
    mask2 = (lax.broadcasted_iota(jnp.int32, (span2, 1), 0) % W2) < half

    def read(rows):
        return jnp.concatenate([stream[0, rows, :], stream[1, rows, :]], axis=1)

    def write(rows, value):
        stream[0, rows, :] = value[:, 0:128]
        stream[1, rows, :] = value[:, 128:256]

    for i in range(count + 1):
        z1 = jnp.zeros((W1, 3 * CH), bf16)
        z2 = jnp.zeros((W2, 3 * CH), bf16)
        xa[i * pitch1:i * pitch1 + W1, :] = z1
        xb[i * pitch1:i * pitch1 + W1, :] = z1
        ca[i * pitch2:i * pitch2 + W2, :] = z2
        cb[i * pitch2:i * pitch2 + W2, :] = z2
    raw[...] = jnp.zeros_like(raw)
    extra[...] = jnp.zeros_like(extra)
    stem_k[...] = jnp.zeros_like(stem_k)
    stem = stem_w[...].astype(f32)
    for dy in range(3):
        for dx in range(3):
            for c in range(3):
                k = (3 * dy + dx) * 3 + c
                at = 128 * dx + W1 * c + dy
                stem_k[at:at + 1, :] = stem[k:k + 1, :]
    column = lax.broadcasted_iota(jnp.int32, (8, 128), 1)
    colour = lax.broadcasted_iota(jnp.int32, (8, 128), 0)
    place = ((column == W1 * colour) & (colour < 3)).astype(bf16)
    out_k[...] = jnp.dot(out_w[...], place[0:3, :], preferred_element_type=f32).astype(bf16)

    for y in range(side):
        for c in range(3):
            at = W1 * c + y
            v, n = images[y, c], noise[y, c]
            for i in range(count):
                raw[i, at:at + 1, 0:side] = v[i:i + 1, :]
                extra[i, at:at + 1, 0:side] = n[i:i + 1, :]

    def shifted(ref, base, value):
        n, wide = value.shape
        ref[pl.ds(base, n), 0:wide] = pltpu.roll(value, 1, 0).astype(bf16)
        ref[pl.ds(base, n), wide:2 * wide] = value.astype(bf16)
        ref[pl.ds(base, n), 2 * wide:3 * wide] = pltpu.roll(value, n - 1, 0).astype(bf16)

    def each(body):
        def step(i, _):
            body(i, pl.multiple_of(W1 + i * pitch1, W1))
            return 0
        lax.fori_loop(0, count, step, 0)

    def conv(ref, base, n, width, weights):
        near = jnp.concatenate([ref[pl.ds(base - width, n), :], ref[pl.ds(base, n), :],
                                ref[pl.ds(base + width, n), :]], axis=1)
        return jnp.dot(near, weights[...], preferred_element_type=f32)

    def begin(i, base):
        across = jnp.transpose(raw[i].astype(bf16).astype(f32))[0:W1, :]
        for y in range(side):
            pix[y * W1:(y + 1) * W1, :] = pltpu.roll(across, (1 - y) % 128, 1)
        shifted(stem_x, 0, pix[...])
        acc = jnp.dot(stem_x[...], stem_k[...].astype(bf16), preferred_element_type=f32)
        write(pl.ds(base, span1), acc)
        shifted(xa, base, jnp.where(mask1, gelu(acc), 0.0))
    each(begin)

    loads[0].wait()

    def layer0(i, base):
        s = read(pl.ds(base, span1)) + conv(xa, base, span1, W1, l1.at[0])
        write(pl.ds(base, span1), s)
        shifted(xb, base, jnp.where(mask1, gelu(s), 0.0))
    each(layer0)

    loads[1].wait()

    def layer1(i, base):
        write(pl.ds(base, span1), read(pl.ds(base, span1)) + conv(xb, base, span1, W1, l1.at[1]))
    each(layer1)

    loads[2].wait()
    loads[3].wait()
    loads[4].wait()
    for i in range(count):
        base1, base2 = W1 + i * pitch1, W2 + i * pitch2
        cols = [read(pl.ds(base1 + b, span1 // 2, stride=2)).astype(bf16).reshape(half, 2, W2, CH) for b in range(2)]
        cells = jnp.concatenate([cols[b][:, a].reshape(span2, CH) for a in range(2) for b in range(2)], axis=1)
        acc = jnp.dot(cells, down[...], preferred_element_type=f32)
        coarse[base2:base2 + span2, :] = acc
        shifted(ca, base2, jnp.where(mask2, gelu(acc), 0.0))
    for i in range(count):
        base2 = W2 + i * pitch2
        s = coarse[base2:base2 + span2, :] + conv(ca, base2, span2, W2, l2.at[0])
        coarse[base2:base2 + span2, :] = s
        shifted(cb, base2, jnp.where(mask2, gelu(s), 0.0))
    for i in range(count):
        base1, base2 = W1 + i * pitch1, W2 + i * pitch2
        s = coarse[base2:base2 + span2, :] + conv(cb, base2, span2, W2, l2.at[1])
        s = s.astype(bf16)
        for a in range(2):
            for b in range(2):
                g = (2 * a + b) * CH
                part = jnp.dot(s, up[:, g:g + CH], preferred_element_type=f32)
                for y in range(half):
                    rows = pl.ds(base1 + (2 * y + a) * W1 + b, W2, stride=2)
                    write(rows, read(rows) + part[y * W2:(y + 1) * W2, :])

    def enter(i, base):
        shifted(xa, base, jnp.where(mask1, gelu(read(pl.ds(base, span1))), 0.0))
    each(enter)

    loads[5].wait()

    def layer2(i, base):
        s = read(pl.ds(base, span1)) + conv(xa, base, span1, W1, l1.at[2])
        write(pl.ds(base, span1), s)
        shifted(xb, base, jnp.where(mask1, gelu(s), 0.0))
    each(layer2)

    loads[6].wait()

    def layer3(i, base):
        s = read(pl.ds(base, span1)) + conv(xb, base, span1, W1, l1.at[3])
        score = jnp.dot(gelu(s).astype(bf16), out_k[...], preferred_element_type=f32)
        across = score[0:W1, :]
        for y in range(1, side):
            across += pltpu.roll(score[y * W1:(y + 1) * W1, :], y, 1)
        across = jnp.concatenate([across, jnp.zeros((128 - W1, 128), f32)], axis=0)
        raw[i] = raw[i] + step_size * jnp.transpose(across) + noise_gain * extra[i]
    each(layer3)

    for y in range(side):
        for c in range(3):
            at = W1 * c + y
            purified[y, c] = jnp.concatenate([raw[i, at:at + 1, 0:side] for i in range(count)], axis=0)

    lane = lax.broadcasted_iota(jnp.int32, (128, 128), 1)
    line = lax.broadcasted_iota(jnp.int32, (128, 128), 0)
    wide = []
    for i in range(count):
        rows = None
        for c in range(3):
            spread = ((lane == 3 * line + c) & (line < side)).astype(bf16)
            part = jnp.dot(raw[i, W1 * c:W1 * (c + 1), :].astype(bf16), spread, preferred_element_type=f32)
            rows = part if rows is None else rows + part
        wide.append(rows)
    wide = jnp.concatenate(wide, axis=0).astype(bf16)
    many, run = 4 * count, 3 * PATCH
    token = lax.broadcasted_iota(jnp.int32, (many, count * W1), 0)
    source = lax.broadcasted_iota(jnp.int32, (many, count * W1), 1)
    first = (token // 4) * W1 + ((token // 2) % 2) * PATCH
    lanes = lax.broadcasted_iota(jnp.int32, (many, 128), 1)
    second = (lax.broadcasted_iota(jnp.int32, (many, 128), 0) % 2) == 1
    pieces = [jnp.zeros((many, 128), f32) for _ in range(5)]
    for r in range(PATCH):
        z = jnp.dot((source == first + r).astype(bf16), wide, preferred_element_type=f32)
        z = jnp.where(second, pltpu.roll(z, 128 - run, 1), z)
        z = jnp.where(lanes < run, z, 0.0)
        k, at = (run * r) // 128, (run * r) % 128
        z = pltpu.roll(z, at, 1) if at else z
        pieces[k] += jnp.where(lanes >= at, z, 0.0)
        if at + run > 128:
            pieces[k + 1] += jnp.where(lanes < at, z, 0.0)
    tokens = jnp.concatenate(pieces, axis=1).astype(bf16)
    for k in range(patches.shape[0]):
        patches[k] = tokens


def score_call(images, noise, stem_w, l1, down, l2, up, out_w, copies):
    count, side = images.shape[0], images.shape[1]
    rows1 = W1 + count * (side + 1) * W1
    rows2 = W2 + count * (side // 2 + 1) * W2
    images, noise = images.transpose(1, 3, 0, 2), noise.transpose(1, 3, 0, 2)
    vm = pl.BlockSpec(memory_space=pltpu.VMEM)
    hb = pl.BlockSpec(memory_space=pltpu.HBM)
    purified, patches = pl.pallas_call(
        functools.partial(score_kernel, side, count),
        out_shape=(jax.ShapeDtypeStruct(images.shape, f32), jax.ShapeDtypeStruct((copies, 4 * count, 640), bf16)),
        in_specs=[vm, vm, vm, hb, hb, hb, hb, vm],
        out_specs=(vm, vm),
        scratch_shapes=[
            pltpu.VMEM((count, 128, 128), f32),
            pltpu.VMEM((count, 128, 128), f32),
            pltpu.VMEM((side * W1, 128), f32),
            pltpu.VMEM((side * W1, 3 * 128), bf16),
            pltpu.VMEM((3 * 128, CH), f32),
            pltpu.VMEM((CH, 128), bf16),
            pltpu.VMEM((rows1, 3 * CH), bf16),
            pltpu.VMEM((rows1, 3 * CH), bf16),
            pltpu.VMEM((rows2, 3 * CH), bf16),
            pltpu.VMEM((rows2, 3 * CH), bf16),
            pltpu.VMEM((CH // 128, rows1, 128), f32),
            pltpu.VMEM((rows2, CH), f32),
            pltpu.VMEM(l1.shape, bf16),
            pltpu.VMEM(down.shape, bf16),
            pltpu.VMEM(l2.shape, bf16),
            pltpu.VMEM(up.shape, bf16),
            pltpu.SemaphoreType.DMA((7,)),
        ],
        compiler_params=pltpu.CompilerParams(vmem_limit_bytes=58 << 20),
        cost_estimate=pl.CostEstimate(flops=10_000_000_000, transcendentals=3_000_000, bytes_accessed=12_000_000),
        name="score_net",
    )(images, noise, stem_w, l1, down, l2, up, out_w)
    return purified.transpose(2, 0, 3, 1), patches


def embed_kernel(parts, patches, weight_hbm, bias, own_hbm, mate_hbm, hidden, kept, sent,
                 weight, mixer, total, sums, squares, sems, own_sems, mate_sems):
    core = lax.axis_index("core")
    row = lax.axis_index("zh") * lax.axis_size("x") + lax.axis_index("x")
    place = lax.axis_index("zl") * lax.axis_size("y") + lax.axis_index("y")
    tokens, depth = patches.shape[0], weight_hbm.shape[0]
    blocks, span, width = own_hbm.shape
    group = weight_hbm.shape[1] // parts
    count = parts * group
    step = 512

    def piece(b, side, source, sem):
        at = pl.multiple_of((2 * b + side) * span, span)
        return pltpu.make_async_copy(source.at[b], mixer.at[pl.ds(at, span), :], sem.at[b])

    loads = [pltpu.make_async_copy(weight_hbm.at[:, pl.ds(g * group, group)], weight.at[g], sems.at[g])
             for g in range(parts)]
    pieces = [(piece(b, core, own_hbm, own_sems), piece(b, 1 - core, mate_hbm, mate_sems)) for b in range(blocks)]
    loads[0].start()
    for pair in pieces[:2]:
        pair[0].start()
        pair[1].start()
    for load in loads[1:]:
        load.start()
    for pair in pieces[2:]:
        pair[0].start()
        pair[1].start()
    pixels = patches[:, 0:depth]
    ones = jnp.ones((16, step), bf16)
    ready = 0
    for c in range(count // step):
        g, at = (c * step) // group, (c * step) % group
        if at == 0:
            loads[g].wait()
        e = jnp.dot(pixels, weight[g, :, at:at + step], preferred_element_type=f32)
        e = (e + bias[:, c * step:(c + 1) * step]).astype(bf16)
        v = e.astype(f32)
        q = v * v
        a = v[:, 0:128] + v[:, 128:256] + v[:, 256:384] + v[:, 384:512]
        b = q[:, 0:128] + q[:, 128:256] + q[:, 256:384] + q[:, 384:512]
        sums[...] = a if c == 0 else sums[...] + a
        squares[...] = b if c == 0 else squares[...] + b
        while ready * 2 * span < (c + 1) * step:
            pieces[ready][0].wait()
            pieces[ready][1].wait()
            ready += 1
        part = jnp.dot(jnp.concatenate([e, ones], axis=0), mixer[c * step:(c + 1) * step, :],
                       preferred_element_type=f32)
        total[...] = part if c == 0 else total[...] + part
    share = tokens // 8
    mine = patches[pl.ds(pl.multiple_of(row * share, share), share), 0:depth]
    for out, side in ((kept, core), (sent, 1 - core)):
        first = 2 * place + side
        g, at = first // (group // span), first % (group // span)
        e = jnp.dot(mine, weight[g, :, pl.ds(pl.multiple_of(at * span, 128), span)], preferred_element_type=f32)
        out[...] = (e + bias[:, pl.ds(pl.multiple_of(first * span, 128), span)]).astype(bf16)
    mean = jnp.sum(sums[...], axis=1, keepdims=True) / count
    square = jnp.sum(squares[...], axis=1, keepdims=True) / count
    scale = lax.rsqrt(square - mean * mean + ln_epsilon)
    column = total[tokens:tokens + 1, :]
    value = gelu((total[0:tokens, :] - mean * column) * scale).astype(bf16)
    for b in range(hidden.shape[0]):
        hidden[b] = value


def embed_call(patches, weight, bias, own, mate):
    tokens = patches.shape[0]
    _, span, width = own.shape
    features = weight.shape[1]
    parts = 4
    share = tokens // 8
    vm = pl.BlockSpec(memory_space=pltpu.VMEM)
    hb = pl.BlockSpec(memory_space=pltpu.HBM)
    return pl.pallas_call(
        functools.partial(embed_kernel, parts),
        out_shape=(jax.ShapeDtypeStruct((8, tokens, width), bf16),
                   jax.ShapeDtypeStruct((share, span), bf16),
                   jax.ShapeDtypeStruct((share, span), bf16)),
        in_specs=[vm, hb, vm, hb, hb],
        out_specs=(vm, vm, vm),
        scratch_shapes=[
            pltpu.VMEM((parts, weight.shape[0], features // parts), bf16),
            pltpu.VMEM((features, width), bf16),
            pltpu.VMEM((tokens + 16, width), f32),
            pltpu.VMEM((tokens, 128), f32),
            pltpu.VMEM((tokens, 128), f32),
            pltpu.SemaphoreType.DMA((parts,)),
            pltpu.SemaphoreType.DMA((8,)),
            pltpu.SemaphoreType.DMA((8,)),
        ],
        compiler_params=pltpu.CompilerParams(vmem_limit_bytes=58 << 20),
        cost_estimate=pl.CostEstimate(flops=7_000_000_000, transcendentals=200_000, bytes_accessed=20_000_000),
        name="embed_mlp",
    )(patches, weight, bias, own, mate)


def mix_kernel(hidden_hbm, own_hbm, mate_hbm, out, hidden, weight, total, sems):
    core = lax.axis_index("core")
    blocks, tokens, width = hidden_hbm.shape
    span = own_hbm.shape[1]
    parts = blocks // 2
    deep = 2 * width
    loads = []
    for k in range(parts):
        rows = pl.ds(k * deep, deep)
        pairs = [(own_hbm.at[rows, :], weight.at[rows, pl.ds(0, span)]),
                 (mate_hbm.at[rows, :], weight.at[rows, pl.ds(span, span)])]
        pairs += [(hidden_hbm.at[b], hidden.at[:, pl.ds(b * width, width)]) for b in (2 * k, 2 * k + 1)]
        loads.append([pltpu.make_async_copy(a, b, sems.at[k, n]) for n, (a, b) in enumerate(pairs)])
        for load in loads[-1]:
            load.start()
    for k in range(parts):
        for load in loads[k]:
            load.wait()
        at = slice(k * deep, (k + 1) * deep)
        part = jnp.dot(hidden[:, at], weight[at, :], preferred_element_type=f32)
        if k == 0:
            total[...] = part
        elif k < parts - 1:
            total[...] += part
        else:
            done = (total[...] + part).astype(bf16)
    share = out.shape[1]
    for r in range(tokens // share):
        rows = slice(r * share, (r + 1) * share)
        out[2 * r + core] = done[rows, 0:span]
        out[2 * r + 1 - core] = done[rows, span:2 * span]


def mix_call(hidden, own, mate):
    blocks, tokens, width = hidden.shape
    depth, span = own.shape
    hb = pl.BlockSpec(memory_space=pltpu.HBM)
    return pl.pallas_call(
        mix_kernel,
        out_shape=jax.ShapeDtypeStruct((16, tokens // 8, span), bf16),
        in_specs=[hb, hb, hb],
        out_specs=pl.BlockSpec(memory_space=pltpu.VMEM),
        scratch_shapes=[
            pltpu.VMEM((tokens, depth), bf16),
            pltpu.VMEM((depth, 2 * span), bf16),
            pltpu.VMEM((tokens, 2 * span), f32),
            pltpu.SemaphoreType.DMA((blocks // 2, 4)),
        ],
        compiler_params=pltpu.CompilerParams(vmem_limit_bytes=58 << 20),
        cost_estimate=pl.CostEstimate(flops=2_400_000_000, transcendentals=0, bytes_accessed=9_000_000),
        name="mlp_out",
    )(hidden, own, mate)


def split_kernel(whole, blocks, sems):
    width = blocks.shape[2]
    loads = [pltpu.make_async_copy(whole.at[:, pl.ds(b * width, width)], blocks.at[b], sems.at[b])
             for b in range(blocks.shape[0])]
    for load in loads:
        load.start()
    for load in loads:
        load.wait()


def split_call(whole, count):
    depth, width = whole.shape[0], whole.shape[1] // count
    return pl.pallas_call(
        split_kernel,
        out_shape=jax.ShapeDtypeStruct((count, depth, width), whole.dtype),
        in_specs=[pl.BlockSpec(memory_space=pltpu.HBM)],
        out_specs=pl.BlockSpec(memory_space=pltpu.VMEM),
        scratch_shapes=[pltpu.SemaphoreType.DMA((count,))],
        compiler_params=pltpu.CompilerParams(vmem_limit_bytes=58 << 20),
        cost_estimate=pl.CostEstimate(flops=0, transcendentals=0, bytes_accessed=2 * whole.size * 2),
        name="split_columns",
    )(whole)


def swap(value):
    return lax.ppermute(value, "core", [(0, 1), (1, 0)])


def on_device(images, noise_field, stem_weight, level_one, down_weight, level_two, up_weight,
              out_weight, embed_weight, embed_bias, mlp_in, mlp_out):
    span = mlp_in.shape[0]
    own_in = lax.all_to_all(split_call(mlp_in, 8), ("zl", "y"), 0, 0)
    mate_out = swap(mlp_out)

    purified, patches = score_call(images, noise_field, stem_weight, level_one, down_weight, level_two,
                                   up_weight, out_weight, 64)
    own_in, mate_out, _ = lax.optimization_barrier((own_in, mate_out, purified))
    mate_in = swap(own_in)
    tokens = lax.all_to_all(patches, ("zh", "x", "zl", "y"), 0, 0)
    tokens = tokens.reshape(-1, tokens.shape[-1])
    hidden, kept, sent = embed_call(tokens, embed_weight, embed_bias[None], own_in, mate_in)
    other = swap(sent)
    hidden = lax.all_to_all(hidden, ("zl", "y"), 0, 0)
    shares = mix_call(hidden, mlp_out, mate_out)
    shares = lax.all_to_all(shares, ("zh", "x", "core"), 0, 0)
    mixed = jnp.sum(shares.reshape(8, 2, 8, 8, span).astype(f32), axis=0)
    core = lax.axis_index("core")
    values = jnp.where(core == 0, jnp.stack([kept, other]), jnp.stack([other, kept]))
    encoded = mixed + values.reshape(2, 8, 8, span).astype(f32)
    encoded = encoded.transpose(1, 0, 2, 3).reshape(128, span).astype(bf16)
    return purified, encoded


def solution(mesh):
    fine = Mesh(mesh.devices.reshape(2, 4, 2, 4, 2), ("zh", "x", "zl", "y", "core"))
    row, col = ("zh", "x"), ("zl", "y", "core")
    images = P(row + col, None, None, None)
    placed = (images, images) + (P(),) * 8 + (P(col, row), P(row, col))
    return jax.shard_map(on_device, mesh=fine, in_specs=placed, out_specs=(images, P(row, col)),
                         check_vma=False)
```

```python
import functools
import math

import jax
import jax.numpy as jnp
from jax import lax
from jax.experimental import pallas as pl
from jax.experimental.pallas import tpu as pltpu
from jax.sharding import Mesh, PartitionSpec as P

step_size = 0.25
noise_gain = math.sqrt(0.5)
ln_epsilon = 1e-06
PATCH = 14
W1, W2 = 32, 16
CH = 256
f32, bf16 = jnp.float32, jnp.bfloat16


def gelu(v):
    inner = v * (0.7978845608028654 + 0.035677408136300125 * (v * v))
    half = 0.5 * v
    return half + half * jnp.tanh(inner)


def score_kernel(side, count, images, noise, stem_w, l1_hbm, down_hbm, l2_hbm, up_hbm, out_w,
                 purified, patches, raw, extra, pix, stem_x, stem_k, out_k, xa, xb, ca, cb, stream, coarse,
                 l1, down, l2, up, sems):
    half = side // 2
    span1, span2 = side * W1, half * W2
    pitch1, pitch2 = span1 + W1, span2 + W2
    loads = [pltpu.make_async_copy(l1_hbm.at[0], l1.at[0], sems.at[0]),
             pltpu.make_async_copy(l1_hbm.at[1], l1.at[1], sems.at[1]),
             pltpu.make_async_copy(down_hbm, down, sems.at[2]),
             pltpu.make_async_copy(l2_hbm, l2, sems.at[3]),
             pltpu.make_async_copy(up_hbm, up, sems.at[4]),
             pltpu.make_async_copy(l1_hbm.at[2], l1.at[2], sems.at[5]),
             pltpu.make_async_copy(l1_hbm.at[3], l1.at[3], sems.at[6])]
    for load in loads:
        load.start()

    mask1 = (lax.broadcasted_iota(jnp.int32, (span1, 1), 0) % W1) < side
    mask2 = (lax.broadcasted_iota(jnp.int32, (span2, 1), 0) % W2) < half

    def read(rows):
        return jnp.concatenate([stream[0, rows, :], stream[1, rows, :]], axis=1)

    def write(rows, value):
        stream[0, rows, :] = value[:, 0:128]
        stream[1, rows, :] = value[:, 128:256]

    for i in range(count + 1):
        z1 = jnp.zeros((W1, 3 * CH), bf16)
        z2 = jnp.zeros((W2, 3 * CH), bf16)
        xa[i * pitch1:i * pitch1 + W1, :] = z1
        xb[i * pitch1:i * pitch1 + W1, :] = z1
        ca[i * pitch2:i * pitch2 + W2, :] = z2
        cb[i * pitch2:i * pitch2 + W2, :] = z2
    raw[...] = jnp.zeros_like(raw)
    extra[...] = jnp.zeros_like(extra)
    stem_k[...] = jnp.zeros_like(stem_k)
    stem = stem_w[...].astype(f32)
    for dy in range(3):
        for dx in range(3):
            for c in range(3):
                k = (3 * dy + dx) * 3 + c
                at = 128 * dx + W1 * c + dy
                stem_k[at:at + 1, :] = stem[k:k + 1, :]
    column = lax.broadcasted_iota(jnp.int32, (8, 128), 1)
    colour = lax.broadcasted_iota(jnp.int32, (8, 128), 0)
    place = ((column == W1 * colour) & (colour < 3)).astype(bf16)
    out_k[...] = jnp.dot(out_w[...], place[0:3, :], preferred_element_type=f32).astype(bf16)

    for y in range(side):
        for c in range(3):
            at = W1 * c + y
            v, n = images[y, c], noise[y, c]
            for i in range(count):
                raw[i, at:at + 1, 0:side] = v[i:i + 1, :]
                extra[i, at:at + 1, 0:side] = n[i:i + 1, :]

    def shifted(ref, base, value):
        n, wide = value.shape
        ref[pl.ds(base, n), 0:wide] = pltpu.roll(value, 1, 0).astype(bf16)
        ref[pl.ds(base, n), wide:2 * wide] = value.astype(bf16)
        ref[pl.ds(base, n), 2 * wide:3 * wide] = pltpu.roll(value, n - 1, 0).astype(bf16)

    def each(body):
        def step(i, _):
            body(i, pl.multiple_of(W1 + i * pitch1, W1))
            return 0
        lax.fori_loop(0, count, step, 0)

    def conv(ref, base, n, width, weights):
        near = jnp.concatenate([ref[pl.ds(base - width, n), :], ref[pl.ds(base, n), :],
                                ref[pl.ds(base + width, n), :]], axis=1)
        return jnp.dot(near, weights[...], preferred_element_type=f32)

    def begin(i, base):
        across = jnp.transpose(raw[i].astype(bf16).astype(f32))[0:W1, :]
        for y in range(side):
            pix[y * W1:(y + 1) * W1, :] = pltpu.roll(across, (1 - y) % 128, 1)
        shifted(stem_x, 0, pix[...])
        acc = jnp.dot(stem_x[...], stem_k[...].astype(bf16), preferred_element_type=f32)
        write(pl.ds(base, span1), acc)
        shifted(xa, base, jnp.where(mask1, gelu(acc), 0.0))
    each(begin)

    loads[0].wait()

    def layer0(i, base):
        s = read(pl.ds(base, span1)) + conv(xa, base, span1, W1, l1.at[0])
        write(pl.ds(base, span1), s)
        shifted(xb, base, jnp.where(mask1, gelu(s), 0.0))
    each(layer0)

    loads[1].wait()

    def layer1(i, base):
        write(pl.ds(base, span1), read(pl.ds(base, span1)) + conv(xb, base, span1, W1, l1.at[1]))
    each(layer1)

    loads[2].wait()
    loads[3].wait()
    loads[4].wait()
    for i in range(count):
        base1, base2 = W1 + i * pitch1, W2 + i * pitch2
        cols = [read(pl.ds(base1 + b, span1 // 2, stride=2)).astype(bf16).reshape(half, 2, W2, CH) for b in range(2)]
        cells = jnp.concatenate([cols[b][:, a].reshape(span2, CH) for a in range(2) for b in range(2)], axis=1)
        acc = jnp.dot(cells, down[...], preferred_element_type=f32)
        coarse[base2:base2 + span2, :] = acc
        shifted(ca, base2, jnp.where(mask2, gelu(acc), 0.0))
    for i in range(count):
        base2 = W2 + i * pitch2
        s = coarse[base2:base2 + span2, :] + conv(ca, base2, span2, W2, l2.at[0])
        coarse[base2:base2 + span2, :] = s
        shifted(cb, base2, jnp.where(mask2, gelu(s), 0.0))
    for i in range(count):
        base1, base2 = W1 + i * pitch1, W2 + i * pitch2
        s = coarse[base2:base2 + span2, :] + conv(cb, base2, span2, W2, l2.at[1])
        s = s.astype(bf16)
        for a in range(2):
            for b in range(2):
                g = (2 * a + b) * CH
                part = jnp.dot(s, up[:, g:g + CH], preferred_element_type=f32)
                for y in range(half):
                    rows = pl.ds(base1 + (2 * y + a) * W1 + b, W2, stride=2)
                    write(rows, read(rows) + part[y * W2:(y + 1) * W2, :])

    def enter(i, base):
        shifted(xa, base, jnp.where(mask1, gelu(read(pl.ds(base, span1))), 0.0))
    each(enter)

    loads[5].wait()

    def layer2(i, base):
        s = read(pl.ds(base, span1)) + conv(xa, base, span1, W1, l1.at[2])
        write(pl.ds(base, span1), s)
        shifted(xb, base, jnp.where(mask1, gelu(s), 0.0))
    each(layer2)

    loads[6].wait()

    def layer3(i, base):
        s = read(pl.ds(base, span1)) + conv(xb, base, span1, W1, l1.at[3])
        score = jnp.dot(gelu(s).astype(bf16), out_k[...], preferred_element_type=f32)
        across = score[0:W1, :]
        for y in range(1, side):
            across += pltpu.roll(score[y * W1:(y + 1) * W1, :], y, 1)
        across = jnp.concatenate([across, jnp.zeros((128 - W1, 128), f32)], axis=0)
        raw[i] = raw[i] + step_size * jnp.transpose(across) + noise_gain * extra[i]
    each(layer3)

    for y in range(side):
        for c in range(3):
            at = W1 * c + y
            purified[y, c] = jnp.concatenate([raw[i, at:at + 1, 0:side] for i in range(count)], axis=0)

    lane = lax.broadcasted_iota(jnp.int32, (128, 128), 1)
    line = lax.broadcasted_iota(jnp.int32, (128, 128), 0)
    wide = []
    for i in range(count):
        rows = None
        for c in range(3):
            spread = ((lane == 3 * line + c) & (line < side)).astype(bf16)
            part = jnp.dot(raw[i, W1 * c:W1 * (c + 1), :].astype(bf16), spread, preferred_element_type=f32)
            rows = part if rows is None else rows + part
        wide.append(rows)
    wide = jnp.concatenate(wide, axis=0).astype(bf16)
    many, run = 4 * count, 3 * PATCH
    token = lax.broadcasted_iota(jnp.int32, (many, count * W1), 0)
    source = lax.broadcasted_iota(jnp.int32, (many, count * W1), 1)
    first = (token // 4) * W1 + ((token // 2) % 2) * PATCH
    lanes = lax.broadcasted_iota(jnp.int32, (many, 128), 1)
    second = (lax.broadcasted_iota(jnp.int32, (many, 128), 0) % 2) == 1
    pieces = [jnp.zeros((many, 128), f32) for _ in range(5)]
    for r in range(PATCH):
        z = jnp.dot((source == first + r).astype(bf16), wide, preferred_element_type=f32)
        z = jnp.where(second, pltpu.roll(z, 128 - run, 1), z)
        z = jnp.where(lanes < run, z, 0.0)
        k, at = (run * r) // 128, (run * r) % 128
        z = pltpu.roll(z, at, 1) if at else z
        pieces[k] += jnp.where(lanes >= at, z, 0.0)
        if at + run > 128:
            pieces[k + 1] += jnp.where(lanes < at, z, 0.0)
    tokens = jnp.concatenate(pieces, axis=1).astype(bf16)
    for k in range(patches.shape[0]):
        patches[k] = tokens


def score_call(images, noise, stem_w, l1, down, l2, up, out_w, copies):
    count, side = images.shape[0], images.shape[1]
    rows1 = W1 + count * (side + 1) * W1
    rows2 = W2 + count * (side // 2 + 1) * W2
    images, noise = images.transpose(1, 3, 0, 2), noise.transpose(1, 3, 0, 2)
    vm = pl.BlockSpec(memory_space=pltpu.VMEM)
    hb = pl.BlockSpec(memory_space=pltpu.HBM)
    purified, patches = pl.pallas_call(
        functools.partial(score_kernel, side, count),
        out_shape=(jax.ShapeDtypeStruct(images.shape, f32), jax.ShapeDtypeStruct((copies, 4 * count, 640), bf16)),
        in_specs=[vm, vm, vm, hb, hb, hb, hb, vm],
        out_specs=(vm, vm),
        scratch_shapes=[
            pltpu.VMEM((count, 128, 128), f32),
            pltpu.VMEM((count, 128, 128), f32),
            pltpu.VMEM((side * W1, 128), f32),
            pltpu.VMEM((side * W1, 3 * 128), bf16),
            pltpu.VMEM((3 * 128, CH), f32),
            pltpu.VMEM((CH, 128), bf16),
            pltpu.VMEM((rows1, 3 * CH), bf16),
            pltpu.VMEM((rows1, 3 * CH), bf16),
            pltpu.VMEM((rows2, 3 * CH), bf16),
            pltpu.VMEM((rows2, 3 * CH), bf16),
            pltpu.VMEM((CH // 128, rows1, 128), f32),
            pltpu.VMEM((rows2, CH), f32),
            pltpu.VMEM(l1.shape, bf16),
            pltpu.VMEM(down.shape, bf16),
            pltpu.VMEM(l2.shape, bf16),
            pltpu.VMEM(up.shape, bf16),
            pltpu.SemaphoreType.DMA((7,)),
        ],
        compiler_params=pltpu.CompilerParams(vmem_limit_bytes=58 << 20),
        cost_estimate=pl.CostEstimate(flops=10_000_000_000, transcendentals=3_000_000, bytes_accessed=12_000_000),
        name="score_net",
    )(images, noise, stem_w, l1, down, l2, up, out_w)
    return purified.transpose(2, 0, 3, 1), patches


def embed_kernel(flip, patches, weight_hbm, bias, mixer_hbm, *refs):
    if flip:
        (total_in, sums_in, squares_in, hidden, sent, total, sums, squares,
         weight, offset, mixer, sems, mixer_sems) = refs
    else:
        total, sums, squares, sent, weight, offset, mixer, sems, mixer_sems = refs
    core = lax.axis_index("core")
    side = 1 - core if flip else core
    row = lax.axis_index("zh") * lax.axis_size("x") + lax.axis_index("x")
    place = lax.axis_index("zl") * lax.axis_size("y") + lax.axis_index("y")
    depth, features = weight_hbm.shape
    blocks, span, width = mixer_hbm.shape
    tokens = patches.shape[0]
    step = 1024

    def first(b):
        return pl.multiple_of((2 * b + side) * span, 128)
    loads = [pltpu.make_async_copy(weight_hbm.at[:, pl.ds(first(b), span)], weight.at[:, pl.ds(b * span, span)], sems.at[b])
             for b in range(blocks)]
    mixes = [pltpu.make_async_copy(mixer_hbm.at[b], mixer.at[pl.ds(b * span, span), :], mixer_sems.at[b])
             for b in range(blocks)]
    for b in range(blocks):
        loads[b].start()
        mixes[b].start()
    for b in range(blocks):
        offset[:, b * span:(b + 1) * span] = bias[:, pl.ds(first(b), span)]
    pixels = patches[:, 0:depth]
    ones = jnp.ones((16, step), bf16)
    ready = 0
    for c in range(blocks * span // step):
        at = slice(c * step, (c + 1) * step)
        while ready * span < (c + 1) * step:
            loads[ready].wait()
            mixes[ready].wait()
            ready += 1
        e = jnp.dot(pixels, weight[:, at], preferred_element_type=f32)
        e = (e + offset[:, at]).astype(bf16)
        v = e.astype(f32)
        q = v * v
        a = sum(v[:, k:k + 128] for k in range(128, step, 128)) + v[:, 0:128]
        b = sum(q[:, k:k + 128] for k in range(128, step, 128)) + q[:, 0:128]
        part = jnp.dot(jnp.concatenate([e, ones], axis=0), mixer[at, :], preferred_element_type=f32)
        if c:
            a, b, part = a + sums[...], b + squares[...], part + total[...]
        elif flip:
            a, b, part = a + sums_in[...], b + squares_in[...], part + total_in[...]
        sums[...], squares[...], total[...] = a, b, part
    share = tokens // 8
    mine = patches[pl.ds(pl.multiple_of(row * share, share), share), 0:depth]
    at = pl.ds(pl.multiple_of(place * span, 128), span)
    sent[...] = (jnp.dot(mine, weight[:, at], preferred_element_type=f32) + offset[:, at]).astype(bf16)
    if flip:
        mean = jnp.sum(sums[...], axis=1, keepdims=True) / features
        square = jnp.sum(squares[...], axis=1, keepdims=True) / features
        scale = lax.rsqrt(square - mean * mean + ln_epsilon)
        column = total[tokens:tokens + 1, :]
        value = gelu((total[0:tokens, :] - mean * column) * scale).astype(bf16)
        for b in range(hidden.shape[0]):
            hidden[b] = value


def embed_call(patches, weight, bias, mixer, carry):
    tokens, depth = patches.shape[0], weight.shape[0]
    blocks, span, width = mixer.shape
    flip = 1 if carry else 0
    sent = jax.ShapeDtypeStruct((tokens // 8, span), bf16)
    state = [(tokens + 16, width), (tokens, 128), (tokens, 128)]
    vm = pl.BlockSpec(memory_space=pltpu.VMEM)
    hb = pl.BlockSpec(memory_space=pltpu.HBM)
    if flip:
        shapes = (jax.ShapeDtypeStruct((8, tokens, width), bf16), sent)
        scratch = [pltpu.VMEM(shape, f32) for shape in state]
    else:
        shapes = tuple(jax.ShapeDtypeStruct(shape, f32) for shape in state) + (sent,)
        scratch = []
    return pl.pallas_call(
        functools.partial(embed_kernel, flip),
        out_shape=shapes,
        in_specs=[vm, hb, vm, hb] + [vm] * len(carry),
        out_specs=(vm,) * len(shapes),
        scratch_shapes=scratch + [
            pltpu.VMEM((depth, blocks * span), bf16),
            pltpu.VMEM((1, blocks * span), f32),
            pltpu.VMEM((blocks * span, width), bf16),
            pltpu.SemaphoreType.DMA((blocks,)),
            pltpu.SemaphoreType.DMA((blocks,)),
        ],
        compiler_params=pltpu.CompilerParams(vmem_limit_bytes=58 << 20),
        cost_estimate=pl.CostEstimate(flops=3_500_000_000, transcendentals=100_000, bytes_accessed=8_000_000),
        name="embed_mate" if flip else "embed_own",
    )(patches, weight, bias, mixer, *carry)


def mix_kernel(hidden_hbm, own_hbm, mate_hbm, out, hidden, weight, total, sems):
    core = lax.axis_index("core")
    blocks, tokens, width = hidden_hbm.shape
    span = own_hbm.shape[1]
    parts = blocks // 2
    deep = 2 * width
    loads = []
    for k in range(parts):
        rows = pl.ds(k * deep, deep)
        pairs = [(own_hbm.at[rows, :], weight.at[rows, pl.ds(0, span)]),
                 (mate_hbm.at[rows, :], weight.at[rows, pl.ds(span, span)])]
        pairs += [(hidden_hbm.at[b], hidden.at[:, pl.ds(b * width, width)]) for b in (2 * k, 2 * k + 1)]
        loads.append([pltpu.make_async_copy(a, b, sems.at[k, n]) for n, (a, b) in enumerate(pairs)])
        for load in loads[-1]:
            load.start()
    for k in range(parts):
        for load in loads[k]:
            load.wait()
        at = slice(k * deep, (k + 1) * deep)
        part = jnp.dot(hidden[:, at], weight[at, :], preferred_element_type=f32)
        if k == 0:
            total[...] = part
        elif k < parts - 1:
            total[...] += part
        else:
            done = (total[...] + part).astype(bf16)
    share = out.shape[1]
    for r in range(tokens // share):
        rows = slice(r * share, (r + 1) * share)
        out[2 * r + core] = done[rows, 0:span]
        out[2 * r + 1 - core] = done[rows, span:2 * span]


def mix_call(hidden, own, mate):
    blocks, tokens, width = hidden.shape
    depth, span = own.shape
    hb = pl.BlockSpec(memory_space=pltpu.HBM)
    return pl.pallas_call(
        mix_kernel,
        out_shape=jax.ShapeDtypeStruct((16, tokens // 8, span), bf16),
        in_specs=[hb, hb, hb],
        out_specs=pl.BlockSpec(memory_space=pltpu.VMEM),
        scratch_shapes=[
            pltpu.VMEM((tokens, depth), bf16),
            pltpu.VMEM((depth, 2 * span), bf16),
            pltpu.VMEM((tokens, 2 * span), f32),
            pltpu.SemaphoreType.DMA((blocks // 2, 4)),
        ],
        compiler_params=pltpu.CompilerParams(vmem_limit_bytes=58 << 20),
        cost_estimate=pl.CostEstimate(flops=2_400_000_000, transcendentals=0, bytes_accessed=9_000_000),
        name="mlp_out",
    )(hidden, own, mate)


def split_kernel(whole, blocks, sems):
    width = blocks.shape[2]
    loads = [pltpu.make_async_copy(whole.at[:, pl.ds(b * width, width)], blocks.at[b], sems.at[b])
             for b in range(blocks.shape[0])]
    for load in loads:
        load.start()
    for load in loads:
        load.wait()


def split_call(whole, count):
    depth, width = whole.shape[0], whole.shape[1] // count
    return pl.pallas_call(
        split_kernel,
        out_shape=jax.ShapeDtypeStruct((count, depth, width), whole.dtype),
        in_specs=[pl.BlockSpec(memory_space=pltpu.HBM)],
        out_specs=pl.BlockSpec(memory_space=pltpu.VMEM),
        scratch_shapes=[pltpu.SemaphoreType.DMA((count,))],
        compiler_params=pltpu.CompilerParams(vmem_limit_bytes=58 << 20),
        cost_estimate=pl.CostEstimate(flops=0, transcendentals=0, bytes_accessed=2 * whole.size * 2),
        name="split_columns",
    )(whole)


def swap(value):
    return lax.ppermute(value, "core", [(0, 1), (1, 0)])


def on_device(images, noise_field, stem_weight, level_one, down_weight, level_two, up_weight,
              out_weight, embed_weight, embed_bias, mlp_in, mlp_out):
    span = mlp_in.shape[0]
    own_in = lax.all_to_all(split_call(mlp_in, 8), ("zl", "y"), 0, 0)
    mate_out = swap(mlp_out)

    purified, patches = score_call(images, noise_field, stem_weight, level_one, down_weight, level_two,
                                   up_weight, out_weight, 64)
    mate_out, patches = lax.optimization_barrier((mate_out, patches))
    tokens = lax.all_to_all(patches, ("zh", "x", "zl", "y"), 0, 0)
    own_in, tokens = lax.optimization_barrier((own_in, tokens))
    tokens = tokens.reshape(-1, tokens.shape[-1])
    mate_in = swap(own_in)
    *carry, kept = embed_call(tokens, embed_weight, embed_bias[None], own_in, ())
    hidden, sent = embed_call(tokens, embed_weight, embed_bias[None], mate_in, tuple(carry))
    other = swap(sent)
    hidden = lax.all_to_all(hidden, ("zl", "y"), 0, 0)
    shares = mix_call(hidden, mlp_out, mate_out)
    shares = lax.all_to_all(shares, ("zh", "x", "core"), 0, 0)
    mixed = jnp.sum(shares.reshape(8, 2, 8, 8, span).astype(f32), axis=0)
    core = lax.axis_index("core")
    values = jnp.where(core == 0, jnp.stack([kept, other]), jnp.stack([other, kept]))
    encoded = mixed + values.reshape(2, 8, 8, span).astype(f32)
    encoded = encoded.transpose(1, 0, 2, 3).reshape(128, span).astype(bf16)
    return purified, encoded


def solution(mesh):
    fine = Mesh(mesh.devices.reshape(2, 4, 2, 4, 2), ("zh", "x", "zl", "y", "core"))
    row, col = ("zh", "x"), ("zl", "y", "core")
    images = P(row + col, None, None, None)
    placed = (images, images) + (P(),) * 8 + (P(col, row), P(row, col))
    return jax.shard_map(on_device, mesh=fine, in_specs=placed, out_specs=(images, P(row, col)),
                         check_vma=False)
```

```python
import functools
import math

import jax
import jax.numpy as jnp
from jax import lax
from jax.experimental import pallas as pl
from jax.experimental.pallas import tpu as pltpu
from jax.sharding import Mesh, PartitionSpec as P

step_size = 0.25
noise_gain = math.sqrt(0.5)
ln_epsilon = 1e-06
PATCH = 14
W1, W2 = 32, 16
CH = 256
f32, bf16 = jnp.float32, jnp.bfloat16


def gelu(v):
    inner = v * (0.7978845608028654 + 0.035677408136300125 * (v * v))
    half = 0.5 * v
    return half + half * jnp.tanh(inner)


def score_kernel(side, count, images, noise, stem_w, l1_hbm, down_hbm, l2_hbm, up_hbm, out_w,
                 purified, patches, raw, extra, pix, stem_x, stem_k, out_k, xa, xb, ca, cb, stream, coarse,
                 l1, down, l2, up, sems):
    half = side // 2
    span1, span2 = side * W1, half * W2
    pitch1, pitch2 = span1 + W1, span2 + W2
    loads = [pltpu.make_async_copy(l1_hbm.at[0], l1.at[0], sems.at[0]),
             pltpu.make_async_copy(l1_hbm.at[1], l1.at[1], sems.at[1]),
             pltpu.make_async_copy(down_hbm, down, sems.at[2]),
             pltpu.make_async_copy(l2_hbm, l2, sems.at[3]),
             pltpu.make_async_copy(up_hbm, up, sems.at[4]),
             pltpu.make_async_copy(l1_hbm.at[2], l1.at[2], sems.at[5]),
             pltpu.make_async_copy(l1_hbm.at[3], l1.at[3], sems.at[6])]
    for load in loads:
        load.start()

    mask1 = (lax.broadcasted_iota(jnp.int32, (span1, 1), 0) % W1) < side
    mask2 = (lax.broadcasted_iota(jnp.int32, (span2, 1), 0) % W2) < half

    def read(rows):
        return jnp.concatenate([stream[0, rows, :], stream[1, rows, :]], axis=1)

    def write(rows, value):
        stream[0, rows, :] = value[:, 0:128]
        stream[1, rows, :] = value[:, 128:256]

    for i in range(count + 1):
        z1 = jnp.zeros((W1, 3 * CH), bf16)
        z2 = jnp.zeros((W2, 3 * CH), bf16)
        xa[i * pitch1:i * pitch1 + W1, :] = z1
        xb[i * pitch1:i * pitch1 + W1, :] = z1
        ca[i * pitch2:i * pitch2 + W2, :] = z2
        cb[i * pitch2:i * pitch2 + W2, :] = z2
    raw[...] = jnp.zeros_like(raw)
    extra[...] = jnp.zeros_like(extra)
    stem_k[...] = jnp.zeros_like(stem_k)
    stem = stem_w[...].astype(f32)
    for dy in range(3):
        for dx in range(3):
            for c in range(3):
                k = (3 * dy + dx) * 3 + c
                at = 128 * dx + W1 * c + dy
                stem_k[at:at + 1, :] = stem[k:k + 1, :]
    column = lax.broadcasted_iota(jnp.int32, (8, 128), 1)
    colour = lax.broadcasted_iota(jnp.int32, (8, 128), 0)
    place = ((column == W1 * colour) & (colour < 3)).astype(bf16)
    out_k[...] = jnp.dot(out_w[...], place[0:3, :], preferred_element_type=f32).astype(bf16)

    for y in range(side):
        for c in range(3):
            at = W1 * c + y
            v, n = images[y, c], noise[y, c]
            for i in range(count):
                raw[i, at:at + 1, 0:side] = v[i:i + 1, :]
                extra[i, at:at + 1, 0:side] = n[i:i + 1, :]

    def shifted(ref, base, value):
        n, wide = value.shape
        ref[pl.ds(base, n), 0:wide] = pltpu.roll(value, 1, 0).astype(bf16)
        ref[pl.ds(base, n), wide:2 * wide] = value.astype(bf16)
        ref[pl.ds(base, n), 2 * wide:3 * wide] = pltpu.roll(value, n - 1, 0).astype(bf16)

    def each(body):
        def step(i, _):
            body(i, pl.multiple_of(W1 + i * pitch1, W1))
            return 0
        lax.fori_loop(0, count, step, 0)

    def conv(ref, base, n, width, weights):
        near = jnp.concatenate([ref[pl.ds(base - width, n), :], ref[pl.ds(base, n), :],
                                ref[pl.ds(base + width, n), :]], axis=1)
        return jnp.dot(near, weights[...], preferred_element_type=f32)

    def begin(i, base):
        across = jnp.transpose(raw[i].astype(bf16).astype(f32))[0:W1, :]
        for y in range(side):
            pix[y * W1:(y + 1) * W1, :] = pltpu.roll(across, (1 - y) % 128, 1)
        shifted(stem_x, 0, pix[...])
        acc = jnp.dot(stem_x[...], stem_k[...].astype(bf16), preferred_element_type=f32)
        write(pl.ds(base, span1), acc)
        shifted(xa, base, jnp.where(mask1, gelu(acc), 0.0))
    each(begin)

    loads[0].wait()

    def layer0(i, base):
        s = read(pl.ds(base, span1)) + conv(xa, base, span1, W1, l1.at[0])
        write(pl.ds(base, span1), s)
        shifted(xb, base, jnp.where(mask1, gelu(s), 0.0))
    each(layer0)

    loads[1].wait()

    def layer1(i, base):
        write(pl.ds(base, span1), read(pl.ds(base, span1)) + conv(xb, base, span1, W1, l1.at[1]))
    each(layer1)

    loads[2].wait()
    loads[3].wait()
    loads[4].wait()
    for i in range(count):
        base1, base2 = W1 + i * pitch1, W2 + i * pitch2
        cols = [read(pl.ds(base1 + b, span1 // 2, stride=2)).astype(bf16).reshape(half, 2, W2, CH) for b in range(2)]
        cells = jnp.concatenate([cols[b][:, a].reshape(span2, CH) for a in range(2) for b in range(2)], axis=1)
        acc = jnp.dot(cells, down[...], preferred_element_type=f32)
        coarse[base2:base2 + span2, :] = acc
        shifted(ca, base2, jnp.where(mask2, gelu(acc), 0.0))
    for i in range(count):
        base2 = W2 + i * pitch2
        s = coarse[base2:base2 + span2, :] + conv(ca, base2, span2, W2, l2.at[0])
        coarse[base2:base2 + span2, :] = s
        shifted(cb, base2, jnp.where(mask2, gelu(s), 0.0))
    for i in range(count):
        base1, base2 = W1 + i * pitch1, W2 + i * pitch2
        s = coarse[base2:base2 + span2, :] + conv(cb, base2, span2, W2, l2.at[1])
        s = s.astype(bf16)
        for a in range(2):
            for b in range(2):
                g = (2 * a + b) * CH
                part = jnp.dot(s, up[:, g:g + CH], preferred_element_type=f32)
                for y in range(half):
                    rows = pl.ds(base1 + (2 * y + a) * W1 + b, W2, stride=2)
                    write(rows, read(rows) + part[y * W2:(y + 1) * W2, :])

    def enter(i, base):
        shifted(xa, base, jnp.where(mask1, gelu(read(pl.ds(base, span1))), 0.0))
    each(enter)

    loads[5].wait()

    def layer2(i, base):
        s = read(pl.ds(base, span1)) + conv(xa, base, span1, W1, l1.at[2])
        write(pl.ds(base, span1), s)
        shifted(xb, base, jnp.where(mask1, gelu(s), 0.0))
    each(layer2)

    loads[6].wait()

    def layer3(i, base):
        s = read(pl.ds(base, span1)) + conv(xb, base, span1, W1, l1.at[3])
        score = jnp.dot(gelu(s).astype(bf16), out_k[...], preferred_element_type=f32)
        across = score[0:W1, :]
        for y in range(1, side):
            across += pltpu.roll(score[y * W1:(y + 1) * W1, :], y, 1)
        across = jnp.concatenate([across, jnp.zeros((128 - W1, 128), f32)], axis=0)
        raw[i] = raw[i] + step_size * jnp.transpose(across) + noise_gain * extra[i]
    each(layer3)

    for y in range(side):
        for c in range(3):
            at = W1 * c + y
            purified[y, c] = jnp.concatenate([raw[i, at:at + 1, 0:side] for i in range(count)], axis=0)

    lane = lax.broadcasted_iota(jnp.int32, (128, 128), 1)
    line = lax.broadcasted_iota(jnp.int32, (128, 128), 0)
    wide = []
    for i in range(count):
        rows = None
        for c in range(3):
            spread = ((lane == 3 * line + c) & (line < side)).astype(bf16)
            part = jnp.dot(raw[i, W1 * c:W1 * (c + 1), :].astype(bf16), spread, preferred_element_type=f32)
            rows = part if rows is None else rows + part
        wide.append(rows)
    wide = jnp.concatenate(wide, axis=0).astype(bf16)
    many, run = 4 * count, 3 * PATCH
    token = lax.broadcasted_iota(jnp.int32, (many, count * W1), 0)
    source = lax.broadcasted_iota(jnp.int32, (many, count * W1), 1)
    first = (token // 4) * W1 + ((token // 2) % 2) * PATCH
    lanes = lax.broadcasted_iota(jnp.int32, (many, 128), 1)
    second = (lax.broadcasted_iota(jnp.int32, (many, 128), 0) % 2) == 1
    pieces = [jnp.zeros((many, 128), f32) for _ in range(5)]
    for r in range(PATCH):
        z = jnp.dot((source == first + r).astype(bf16), wide, preferred_element_type=f32)
        z = jnp.where(second, pltpu.roll(z, 128 - run, 1), z)
        z = jnp.where(lanes < run, z, 0.0)
        k, at = (run * r) // 128, (run * r) % 128
        z = pltpu.roll(z, at, 1) if at else z
        pieces[k] += jnp.where(lanes >= at, z, 0.0)
        if at + run > 128:
            pieces[k + 1] += jnp.where(lanes < at, z, 0.0)
    tokens = jnp.concatenate(pieces, axis=1).astype(bf16)
    patches[...] = tokens


def score_call(images, noise, stem_w, l1, down, l2, up, out_w):
    count, side = images.shape[0], images.shape[1]
    rows1 = W1 + count * (side + 1) * W1
    rows2 = W2 + count * (side // 2 + 1) * W2
    images, noise = images.transpose(1, 3, 0, 2), noise.transpose(1, 3, 0, 2)
    vm = pl.BlockSpec(memory_space=pltpu.VMEM)
    hb = pl.BlockSpec(memory_space=pltpu.HBM)
    purified, patches = pl.pallas_call(
        functools.partial(score_kernel, side, count),
        out_shape=(jax.ShapeDtypeStruct(images.shape, f32), jax.ShapeDtypeStruct((4 * count, 640), bf16)),
        in_specs=[vm, vm, vm, hb, hb, hb, hb, vm],
        out_specs=(vm, vm),
        scratch_shapes=[
            pltpu.VMEM((count, 128, 128), f32),
            pltpu.VMEM((count, 128, 128), f32),
            pltpu.VMEM((side * W1, 128), f32),
            pltpu.VMEM((side * W1, 3 * 128), bf16),
            pltpu.VMEM((3 * 128, CH), f32),
            pltpu.VMEM((CH, 128), bf16),
            pltpu.VMEM((rows1, 3 * CH), bf16),
            pltpu.VMEM((rows1, 3 * CH), bf16),
            pltpu.VMEM((rows2, 3 * CH), bf16),
            pltpu.VMEM((rows2, 3 * CH), bf16),
            pltpu.VMEM((CH // 128, rows1, 128), f32),
            pltpu.VMEM((rows2, CH), f32),
            pltpu.VMEM(l1.shape, bf16),
            pltpu.VMEM(down.shape, bf16),
            pltpu.VMEM(l2.shape, bf16),
            pltpu.VMEM(up.shape, bf16),
            pltpu.SemaphoreType.DMA((7,)),
        ],
        compiler_params=pltpu.CompilerParams(vmem_limit_bytes=58 << 20),
        cost_estimate=pl.CostEstimate(flops=10_000_000_000, transcendentals=3_000_000, bytes_accessed=12_000_000),
        name="score_net",
    )(images, noise, stem_w, l1, down, l2, up, out_w)
    return purified.transpose(2, 0, 3, 1), patches


def embed_kernel(flip, piece0, piece1, piece2, piece3, weight_hbm, bias, mixer_hbm, *refs):
    if flip:
        (total_in, sums_in, squares_in, hidden, sent, total, sums, squares,
         patches, weight, offset, mixer, sems, mixer_sems, piece_sems) = refs
    else:
        total, sums, squares, sent, patches, weight, offset, mixer, sems, mixer_sems, piece_sems = refs
    core = lax.axis_index("core")
    side = 1 - core if flip else core
    level, line, lines = lax.axis_index("zl"), lax.axis_index("y"), lax.axis_size("y")
    place = level * lines + line
    depth, features = weight_hbm.shape
    blocks, span, width = mixer_hbm.shape
    tokens = patches.shape[0]
    step = 1024

    def first(b):
        return pl.multiple_of((2 * b + side) * span, 128)
    loads = [pltpu.make_async_copy(weight_hbm.at[:, pl.ds(first(b), span)], weight.at[:, pl.ds(b * span, span)], sems.at[b])
             for b in range(blocks)]
    mixes = [pltpu.make_async_copy(mixer_hbm.at[b], mixer.at[pl.ds(b * span, span), :], mixer_sems.at[b])
             for b in range(blocks)]
    share = tokens // 8
    moves = []
    for k, piece in enumerate((piece0, piece1, piece2, piece3)):
        for part in range(2):
            to = (level + part) % 2 * lines + (line + lines - k) % lines
            moves.append(pltpu.make_async_copy(
                piece.at[pl.ds(part * share, share), :],
                patches.at[pl.ds(pl.multiple_of(to * share, share), share), :], piece_sems.at[2 * k + part]))
    for move in moves:
        move.start()
    for b in range(blocks):
        loads[b].start()
        mixes[b].start()
    for b in range(blocks):
        offset[:, b * span:(b + 1) * span] = bias[:, pl.ds(first(b), span)]
    for move in moves:
        move.wait()
    pixels = patches[:, 0:depth]
    ones = jnp.ones((16, step), bf16)
    ready = 0
    for c in range(blocks * span // step):
        at = slice(c * step, (c + 1) * step)
        while ready * span < (c + 1) * step:
            loads[ready].wait()
            mixes[ready].wait()
            ready += 1
        e = jnp.dot(pixels, weight[:, at], preferred_element_type=f32)
        e = (e + offset[:, at]).astype(bf16)
        v = e.astype(f32)
        q = v * v
        a = sum(v[:, k:k + 128] for k in range(128, step, 128)) + v[:, 0:128]
        b = sum(q[:, k:k + 128] for k in range(128, step, 128)) + q[:, 0:128]
        part = jnp.dot(jnp.concatenate([e, ones], axis=0), mixer[at, :], preferred_element_type=f32)
        if c:
            a, b, part = a + sums[...], b + squares[...], part + total[...]
        elif flip:
            a, b, part = a + sums_in[...], b + squares_in[...], part + total_in[...]
        sums[...], squares[...], total[...] = a, b, part
    mine = jnp.concatenate([patches[b * share:b * share + 8, 0:depth].astype(f32) for b in range(8)], axis=0).astype(bf16)
    at = pl.ds(pl.multiple_of(place * span, 128), span)
    sent[...] = (jnp.dot(mine, weight[:, at], preferred_element_type=f32) + offset[:, at]).astype(bf16)
    if flip:
        mean = jnp.sum(sums[...], axis=1, keepdims=True) / features
        square = jnp.sum(squares[...], axis=1, keepdims=True) / features
        scale = lax.rsqrt(square - mean * mean + ln_epsilon)
        column = total[tokens:tokens + 1, :]
        value = gelu((total[0:tokens, :] - mean * column) * scale).astype(bf16)
        for b in range(hidden.shape[0]):
            hidden[b] = value


def embed_call(pieces, weight, bias, mixer, carry):
    tokens, depth = 4 * pieces[0].shape[0], weight.shape[0]
    blocks, span, width = mixer.shape
    flip = 1 if carry else 0
    free = pl.BlockSpec(memory_space=pl.ANY)
    sent = jax.ShapeDtypeStruct((tokens // 8, span), bf16)
    state = [(tokens + 16, width), (tokens, 128), (tokens, 128)]
    vm = pl.BlockSpec(memory_space=pltpu.VMEM)
    hb = pl.BlockSpec(memory_space=pltpu.HBM)
    if flip:
        shapes = (jax.ShapeDtypeStruct((8, tokens, width), bf16), sent)
        scratch = [pltpu.VMEM(shape, f32) for shape in state]
    else:
        shapes = tuple(jax.ShapeDtypeStruct(shape, f32) for shape in state) + (sent,)
        scratch = []
    return pl.pallas_call(
        functools.partial(embed_kernel, flip),
        out_shape=shapes,
        in_specs=[free] * 4 + [hb, vm, free] + [vm] * len(carry),
        out_specs=(vm,) * len(shapes),
        scratch_shapes=scratch + [
            pltpu.VMEM((tokens, pieces[0].shape[1]), bf16),
            pltpu.VMEM((depth, blocks * span), bf16),
            pltpu.VMEM((1, blocks * span), f32),
            pltpu.VMEM((blocks * span, width), bf16),
            pltpu.SemaphoreType.DMA((blocks,)),
            pltpu.SemaphoreType.DMA((blocks,)),
            pltpu.SemaphoreType.DMA((8,)),
        ],
        compiler_params=pltpu.CompilerParams(vmem_limit_bytes=58 << 20),
        cost_estimate=pl.CostEstimate(flops=3_500_000_000, transcendentals=100_000, bytes_accessed=8_000_000),
        name="embed_mate" if flip else "embed_own",
    )(*pieces, weight, bias, mixer, *carry)


def mix_kernel(hidden_hbm, own_hbm, mate_hbm, out, hidden, weight, total, sems):
    core = lax.axis_index("core")
    blocks, tokens, width = hidden_hbm.shape
    span = own_hbm.shape[1]
    parts = blocks // 2
    deep = 2 * width
    loads = []
    for k in range(parts):
        rows = pl.ds(k * deep, deep)
        pairs = [(own_hbm.at[rows, :], weight.at[rows, pl.ds(0, span)]),
                 (mate_hbm.at[rows, :], weight.at[rows, pl.ds(span, span)])]
        pairs += [(hidden_hbm.at[b], hidden.at[:, pl.ds(b * width, width)]) for b in (2 * k, 2 * k + 1)]
        loads.append([pltpu.make_async_copy(a, b, sems.at[k, n]) for n, (a, b) in enumerate(pairs)])
        for load in loads[-1]:
            load.start()
    for k in range(parts):
        for load in loads[k]:
            load.wait()
        at = slice(k * deep, (k + 1) * deep)
        part = jnp.dot(hidden[:, at], weight[at, :], preferred_element_type=f32)
        if k == 0:
            total[...] = part
        elif k < parts - 1:
            total[...] += part
        else:
            done = total[...] + part
    share = out.shape[1]
    high, across, size = lax.axis_index("zh"), lax.axis_index("x"), lax.axis_size("x")
    for q in range(tokens // share):
        rows = jnp.concatenate([done[b * share + q * 8:b * share + q * 8 + 8, :] for b in range(8)], axis=0).astype(bf16)
        r = (high + q // size) % 2 * size + (across + size - q % size) % size
        out[2 * r + core] = rows[:, 0:span]
        out[2 * r + 1 - core] = rows[:, span:2 * span]


def mix_call(hidden, own, mate):
    blocks, tokens, width = hidden.shape
    depth, span = own.shape
    hb = pl.BlockSpec(memory_space=pltpu.HBM)
    return pl.pallas_call(
        mix_kernel,
        out_shape=jax.ShapeDtypeStruct((16, tokens // 8, span), bf16),
        in_specs=[hb, hb, hb],
        out_specs=pl.BlockSpec(memory_space=pltpu.VMEM),
        scratch_shapes=[
            pltpu.VMEM((tokens, depth), bf16),
            pltpu.VMEM((depth, 2 * span), bf16),
            pltpu.VMEM((tokens, 2 * span), f32),
            pltpu.SemaphoreType.DMA((blocks // 2, 4)),
        ],
        compiler_params=pltpu.CompilerParams(vmem_limit_bytes=58 << 20),
        cost_estimate=pl.CostEstimate(flops=2_400_000_000, transcendentals=0, bytes_accessed=9_000_000),
        name="mlp_out",
    )(hidden, own, mate)


def split_kernel(whole, blocks, sems):
    width = blocks.shape[2]
    loads = [pltpu.make_async_copy(whole.at[:, pl.ds(b * width, width)], blocks.at[b], sems.at[b])
             for b in range(blocks.shape[0])]
    for load in loads:
        load.start()
    for load in loads:
        load.wait()


def split_call(whole, count):
    depth, width = whole.shape[0], whole.shape[1] // count
    return pl.pallas_call(
        split_kernel,
        out_shape=jax.ShapeDtypeStruct((count, depth, width), whole.dtype),
        in_specs=[pl.BlockSpec(memory_space=pltpu.HBM)],
        out_specs=pl.BlockSpec(memory_space=pltpu.VMEM),
        scratch_shapes=[pltpu.SemaphoreType.DMA((count,))],
        compiler_params=pltpu.CompilerParams(vmem_limit_bytes=58 << 20),
        cost_estimate=pl.CostEstimate(flops=0, transcendentals=0, bytes_accessed=2 * whole.size * 2),
        name="split_columns",
    )(whole)


def shift(value, axis, k):
    n = lax.axis_size(axis)
    return lax.ppermute(value, axis, [(i, (i + k) % n) for i in range(n)])


def swap(value):
    return lax.ppermute(value, "core", [(0, 1), (1, 0)])


def on_device(images, noise_field, stem_weight, level_one, down_weight, level_two, up_weight,
              out_weight, embed_weight, embed_bias, mlp_in, mlp_out):
    span = mlp_in.shape[0]
    own_in = lax.all_to_all(split_call(mlp_in, 8), ("zl", "y"), 0, 0)
    mate_out = swap(mlp_out)

    purified, patches = score_call(images, noise_field, stem_weight, level_one, down_weight, level_two,
                                   up_weight, out_weight)
    mate_out, patches = lax.optimization_barrier((mate_out, patches))
    patches = jnp.concatenate([patches] + [shift(patches, "x", k) for k in (1, 2, 3)], axis=0)
    patches = jnp.concatenate([patches, shift(patches, "zh", 1)], axis=0)
    patches = jnp.concatenate([patches, shift(patches, "zl", 1)], axis=0)
    pieces = [patches] + [shift(patches, "y", k) for k in (1, 2, 3)]
    own_in, *pieces = lax.optimization_barrier((own_in, *pieces))
    mate_in = swap(own_in)
    *carry, kept = embed_call(pieces, embed_weight, embed_bias[None], own_in, ())
    hidden, sent = embed_call(pieces, embed_weight, embed_bias[None], mate_in, tuple(carry))
    other = swap(sent)
    hidden = lax.all_to_all(hidden, ("zl", "y"), 0, 0)
    shares = mix_call(hidden, mlp_out, mate_out)
    shares = lax.all_to_all(shares, ("zh", "x", "core"), 0, 0)
    mixed = jnp.sum(shares.reshape(8, 2, 8, 8, span).astype(f32), axis=0)
    core = lax.axis_index("core")
    values = jnp.where(core == 0, jnp.stack([kept, other]), jnp.stack([other, kept]))
    encoded = mixed + values.reshape(2, 8, 8, span).astype(f32)
    encoded = encoded.transpose(1, 0, 2, 3).reshape(128, span).astype(bf16)
    return purified, encoded


def solution(mesh):
    fine = Mesh(mesh.devices.reshape(2, 4, 2, 4, 2), ("zh", "x", "zl", "y", "core"))
    row, col = ("zh", "x"), ("zl", "y", "core")
    images = P(row + col, None, None, None)
    placed = (images, images) + (P(),) * 8 + (P(col, row), P(row, col))
    return jax.shard_map(on_device, mesh=fine, in_specs=placed, out_specs=(images, P(row, col)),
                         check_vma=False)
```

```python
import functools
import math

import jax
import jax.numpy as jnp
from jax import lax
from jax.experimental import pallas as pl
from jax.experimental.pallas import tpu as pltpu
from jax.sharding import Mesh, PartitionSpec as P

step_size = 0.25
noise_gain = math.sqrt(0.5)
ln_epsilon = 1e-06
PATCH = 14
W1, W2 = 32, 16
CH = 256
f32, bf16 = jnp.float32, jnp.bfloat16


def gelu(v):
    inner = v * (0.7978845608028654 + 0.035677408136300125 * (v * v))
    half = 0.5 * v
    return half + half * jnp.tanh(inner)


def score_kernel(side, count, images, noise, stem_w, l1_hbm, down_hbm, l2_hbm, up_hbm, out_w,
                 purified, patches, raw, extra, pix, stem_x, stem_k, out_k, xa, xb, ca, cb, stream, coarse,
                 l1, down, l2, up, sems):
    half = side // 2
    span1, span2 = side * W1, half * W2
    pitch1, pitch2 = span1 + W1, span2 + W2
    loads = [pltpu.make_async_copy(l1_hbm.at[0], l1.at[0], sems.at[0]),
             pltpu.make_async_copy(l1_hbm.at[1], l1.at[1], sems.at[1]),
             pltpu.make_async_copy(down_hbm, down, sems.at[2]),
             pltpu.make_async_copy(l2_hbm, l2, sems.at[3]),
             pltpu.make_async_copy(up_hbm, up, sems.at[4]),
             pltpu.make_async_copy(l1_hbm.at[2], l1.at[2], sems.at[5]),
             pltpu.make_async_copy(l1_hbm.at[3], l1.at[3], sems.at[6])]
    for load in loads:
        load.start()

    mask1 = (lax.broadcasted_iota(jnp.int32, (span1, 1), 0) % W1) < side
    mask2 = (lax.broadcasted_iota(jnp.int32, (span2, 1), 0) % W2) < half

    def read(rows):
        return jnp.concatenate([stream[0, rows, :], stream[1, rows, :]], axis=1)

    def write(rows, value):
        stream[0, rows, :] = value[:, 0:128]
        stream[1, rows, :] = value[:, 128:256]

    for i in range(count + 1):
        z1 = jnp.zeros((W1, 3 * CH), bf16)
        z2 = jnp.zeros((W2, 3 * CH), bf16)
        xa[i * pitch1:i * pitch1 + W1, :] = z1
        xb[i * pitch1:i * pitch1 + W1, :] = z1
        ca[i * pitch2:i * pitch2 + W2, :] = z2
        cb[i * pitch2:i * pitch2 + W2, :] = z2
    raw[...] = jnp.zeros_like(raw)
    extra[...] = jnp.zeros_like(extra)
    stem_k[...] = jnp.zeros_like(stem_k)
    stem = stem_w[...].astype(f32)
    for dy in range(3):
        for dx in range(3):
            for c in range(3):
                k = (3 * dy + dx) * 3 + c
                at = 128 * dx + W1 * c + dy
                stem_k[at:at + 1, :] = stem[k:k + 1, :]
    column = lax.broadcasted_iota(jnp.int32, (8, 128), 1)
    colour = lax.broadcasted_iota(jnp.int32, (8, 128), 0)
    place = ((column == W1 * colour) & (colour < 3)).astype(bf16)
    out_k[...] = jnp.dot(out_w[...], place[0:3, :], preferred_element_type=f32).astype(bf16)

    for y in range(side):
        for c in range(3):
            at = W1 * c + y
            v, n = images[y, c], noise[y, c]
            for i in range(count):
                raw[i, at:at + 1, 0:side] = v[i:i + 1, :]
                extra[i, at:at + 1, 0:side] = n[i:i + 1, :]

    def shifted(ref, base, value):
        n, wide = value.shape
        ref[pl.ds(base, n), 0:wide] = pltpu.roll(value, 1, 0).astype(bf16)
        ref[pl.ds(base, n), wide:2 * wide] = value.astype(bf16)
        ref[pl.ds(base, n), 2 * wide:3 * wide] = pltpu.roll(value, n - 1, 0).astype(bf16)

    def each(body):
        def step(i, _):
            body(i, pl.multiple_of(W1 + i * pitch1, W1))
            return 0
        lax.fori_loop(0, count, step, 0)

    def conv(ref, base, n, width, weights):
        near = jnp.concatenate([ref[pl.ds(base - width, n), :], ref[pl.ds(base, n), :],
                                ref[pl.ds(base + width, n), :]], axis=1)
        return jnp.dot(near, weights[...], preferred_element_type=f32)

    def begin(i, base):
        across = jnp.transpose(raw[i].astype(bf16).astype(f32))[0:W1, :]
        for y in range(side):
            pix[y * W1:(y + 1) * W1, :] = pltpu.roll(across, (1 - y) % 128, 1)
        shifted(stem_x, 0, pix[...])
        acc = jnp.dot(stem_x[...], stem_k[...].astype(bf16), preferred_element_type=f32)
        write(pl.ds(base, span1), acc)
        shifted(xa, base, jnp.where(mask1, gelu(acc), 0.0))
    each(begin)

    loads[0].wait()

    def layer0(i, base):
        s = read(pl.ds(base, span1)) + conv(xa, base, span1, W1, l1.at[0])
        write(pl.ds(base, span1), s)
        shifted(xb, base, jnp.where(mask1, gelu(s), 0.0))
    each(layer0)

    loads[1].wait()

    def layer1(i, base):
        write(pl.ds(base, span1), read(pl.ds(base, span1)) + conv(xb, base, span1, W1, l1.at[1]))
    each(layer1)

    loads[2].wait()
    loads[3].wait()
    loads[4].wait()
    for i in range(count):
        base1, base2 = W1 + i * pitch1, W2 + i * pitch2
        cols = [read(pl.ds(base1 + b, span1 // 2, stride=2)).astype(bf16).reshape(half, 2, W2, CH) for b in range(2)]
        cells = jnp.concatenate([cols[b][:, a].reshape(span2, CH) for a in range(2) for b in range(2)], axis=1)
        acc = jnp.dot(cells, down[...], preferred_element_type=f32)
        coarse[base2:base2 + span2, :] = acc
        shifted(ca, base2, jnp.where(mask2, gelu(acc), 0.0))
    for i in range(count):
        base2 = W2 + i * pitch2
        s = coarse[base2:base2 + span2, :] + conv(ca, base2, span2, W2, l2.at[0])
        coarse[base2:base2 + span2, :] = s
        shifted(cb, base2, jnp.where(mask2, gelu(s), 0.0))
    for i in range(count):
        base1, base2 = W1 + i * pitch1, W2 + i * pitch2
        s = coarse[base2:base2 + span2, :] + conv(cb, base2, span2, W2, l2.at[1])
        s = s.astype(bf16)
        for a in range(2):
            for b in range(2):
                g = (2 * a + b) * CH
                part = jnp.dot(s, up[:, g:g + CH], preferred_element_type=f32)
                for y in range(half):
                    rows = pl.ds(base1 + (2 * y + a) * W1 + b, W2, stride=2)
                    write(rows, read(rows) + part[y * W2:(y + 1) * W2, :])

    def enter(i, base):
        shifted(xa, base, jnp.where(mask1, gelu(read(pl.ds(base, span1))), 0.0))
    each(enter)

    loads[5].wait()

    def layer2(i, base):
        s = read(pl.ds(base, span1)) + conv(xa, base, span1, W1, l1.at[2])
        write(pl.ds(base, span1), s)
        shifted(xb, base, jnp.where(mask1, gelu(s), 0.0))
    each(layer2)

    loads[6].wait()

    def layer3(i, base):
        s = read(pl.ds(base, span1)) + conv(xb, base, span1, W1, l1.at[3])
        score = jnp.dot(gelu(s).astype(bf16), out_k[...], preferred_element_type=f32)
        across = score[0:W1, :]
        for y in range(1, side):
            across += pltpu.roll(score[y * W1:(y + 1) * W1, :], y, 1)
        across = jnp.concatenate([across, jnp.zeros((128 - W1, 128), f32)], axis=0)
        raw[i] = raw[i] + step_size * jnp.transpose(across) + noise_gain * extra[i]
    each(layer3)

    for y in range(side):
        for c in range(3):
            at = W1 * c + y
            purified[y, c] = jnp.concatenate([raw[i, at:at + 1, 0:side] for i in range(count)], axis=0)

    lane = lax.broadcasted_iota(jnp.int32, (128, 128), 1)
    line = lax.broadcasted_iota(jnp.int32, (128, 128), 0)
    wide = []
    for i in range(count):
        rows = None
        for c in range(3):
            spread = ((lane == 3 * line + c) & (line < side)).astype(bf16)
            part = jnp.dot(raw[i, W1 * c:W1 * (c + 1), :].astype(bf16), spread, preferred_element_type=f32)
            rows = part if rows is None else rows + part
        wide.append(rows)
    wide = jnp.concatenate(wide, axis=0).astype(bf16)
    many, run = 4 * count, 3 * PATCH
    token = lax.broadcasted_iota(jnp.int32, (many, count * W1), 0)
    source = lax.broadcasted_iota(jnp.int32, (many, count * W1), 1)
    first = (token // 4) * W1 + ((token // 2) % 2) * PATCH
    lanes = lax.broadcasted_iota(jnp.int32, (many, 128), 1)
    second = (lax.broadcasted_iota(jnp.int32, (many, 128), 0) % 2) == 1
    pieces = [jnp.zeros((many, 128), f32) for _ in range(5)]
    for r in range(PATCH):
        z = jnp.dot((source == first + r).astype(bf16), wide, preferred_element_type=f32)
        z = jnp.where(second, pltpu.roll(z, 128 - run, 1), z)
        z = jnp.where(lanes < run, z, 0.0)
        k, at = (run * r) // 128, (run * r) % 128
        z = pltpu.roll(z, at, 1) if at else z
        pieces[k] += jnp.where(lanes >= at, z, 0.0)
        if at + run > 128:
            pieces[k + 1] += jnp.where(lanes < at, z, 0.0)
    tokens = jnp.concatenate(pieces, axis=1).astype(bf16)
    patches[...] = tokens


def score_call(images, noise, stem_w, l1, down, l2, up, out_w):
    count, side = images.shape[0], images.shape[1]
    rows1 = W1 + count * (side + 1) * W1
    rows2 = W2 + count * (side // 2 + 1) * W2
    images, noise = images.transpose(1, 3, 0, 2), noise.transpose(1, 3, 0, 2)
    vm = pl.BlockSpec(memory_space=pltpu.VMEM)
    hb = pl.BlockSpec(memory_space=pltpu.HBM)
    purified, patches = pl.pallas_call(
        functools.partial(score_kernel, side, count),
        out_shape=(jax.ShapeDtypeStruct(images.shape, f32), jax.ShapeDtypeStruct((4 * count, 640), bf16)),
        in_specs=[vm, vm, vm, hb, hb, hb, hb, vm],
        out_specs=(vm, vm),
        scratch_shapes=[
            pltpu.VMEM((count, 128, 128), f32),
            pltpu.VMEM((count, 128, 128), f32),
            pltpu.VMEM((side * W1, 128), f32),
            pltpu.VMEM((side * W1, 3 * 128), bf16),
            pltpu.VMEM((3 * 128, CH), f32),
            pltpu.VMEM((CH, 128), bf16),
            pltpu.VMEM((rows1, 3 * CH), bf16),
            pltpu.VMEM((rows1, 3 * CH), bf16),
            pltpu.VMEM((rows2, 3 * CH), bf16),
            pltpu.VMEM((rows2, 3 * CH), bf16),
            pltpu.VMEM((CH // 128, rows1, 128), f32),
            pltpu.VMEM((rows2, CH), f32),
            pltpu.VMEM(l1.shape, bf16),
            pltpu.VMEM(down.shape, bf16),
            pltpu.VMEM(l2.shape, bf16),
            pltpu.VMEM(up.shape, bf16),
            pltpu.SemaphoreType.DMA((7,)),
        ],
        compiler_params=pltpu.CompilerParams(vmem_limit_bytes=58 << 20),
        cost_estimate=pl.CostEstimate(flops=10_000_000_000, transcendentals=3_000_000, bytes_accessed=12_000_000),
        name="score_net",
    )(images, noise, stem_w, l1, down, l2, up, out_w)
    return purified.transpose(2, 0, 3, 1), patches


def embed_kernel(flip, piece0, piece1, piece2, piece3, weight_hbm, bias, mixer_hbm, *refs):
    if flip:
        (total_in, sums_in, squares_in, hidden, sent, total, sums, squares,
         patches, weight, offset, mixer, sems, mixer_sems, piece_sems) = refs
    else:
        total, sums, squares, sent, patches, weight, offset, mixer, sems, mixer_sems, piece_sems = refs
    core = lax.axis_index("core")
    side = 1 - core if flip else core
    level, line, lines = lax.axis_index("zl"), lax.axis_index("y"), lax.axis_size("y")
    place = level * lines + line
    depth, features = weight_hbm.shape
    blocks, span, width = mixer_hbm.shape
    tokens = patches.shape[0]
    step = 1024

    def first(b):
        return pl.multiple_of((2 * b + side) * span, 128)
    loads = [pltpu.make_async_copy(weight_hbm.at[:, pl.ds(first(b), span)], weight.at[:, pl.ds(b * span, span)], sems.at[b])
             for b in range(blocks)]
    mixes = [pltpu.make_async_copy(mixer_hbm.at[b], mixer.at[pl.ds(b * span, span), :], mixer_sems.at[b])
             for b in range(blocks)]
    share = tokens // 8
    moves = []
    for k, piece in enumerate((piece0, piece1, piece2, piece3)):
        for part in range(2):
            to = (level + part) % 2 * lines + (line + lines - k) % lines
            moves.append(pltpu.make_async_copy(
                piece.at[pl.ds(part * share, share), :],
                patches.at[pl.ds(pl.multiple_of(to * share, share), share), :], piece_sems.at[2 * k + part]))
    for move in moves:
        move.start()
    for b in range(blocks):
        loads[b].start()
        mixes[b].start()
    for b in range(blocks):
        offset[:, b * span:(b + 1) * span] = bias[:, pl.ds(first(b), span)]
    for move in moves:
        move.wait()
    pixels = patches[:, 0:depth]
    ones = jnp.ones((16, step), bf16)
    ready = 0
    for c in range(blocks * span // step):
        at = slice(c * step, (c + 1) * step)
        while ready * span < (c + 1) * step:
            loads[ready].wait()
            mixes[ready].wait()
            ready += 1
        e = jnp.dot(pixels, weight[:, at], preferred_element_type=f32)
        e = (e + offset[:, at]).astype(bf16)
        v = e.astype(f32)
        q = v * v
        a = sum(v[:, k:k + 128] for k in range(128, step, 128)) + v[:, 0:128]
        b = sum(q[:, k:k + 128] for k in range(128, step, 128)) + q[:, 0:128]
        part = jnp.dot(jnp.concatenate([e, ones], axis=0), mixer[at, :], preferred_element_type=f32)
        if c:
            a, b, part = a + sums[...], b + squares[...], part + total[...]
        elif flip:
            a, b, part = a + sums_in[...], b + squares_in[...], part + total_in[...]
        sums[...], squares[...], total[...] = a, b, part
    mine = jnp.concatenate([patches[b * share:b * share + 8, 0:depth].astype(f32) for b in range(8)], axis=0).astype(bf16)
    at = pl.ds(pl.multiple_of(place * span, 128), span)
    sent[...] = (jnp.dot(mine, weight[:, at], preferred_element_type=f32) + offset[:, at]).astype(bf16)
    if flip:
        mean = jnp.sum(sums[...], axis=1, keepdims=True) / features
        square = jnp.sum(squares[...], axis=1, keepdims=True) / features
        scale = lax.rsqrt(square - mean * mean + ln_epsilon)
        column = total[tokens:tokens + 1, :]
        value = gelu((total[0:tokens, :] - mean * column) * scale).astype(bf16)
        for b in range(hidden.shape[0]):
            hidden[b] = value


def embed_call(pieces, weight, bias, mixer, carry):
    tokens, depth = 4 * pieces[0].shape[0], weight.shape[0]
    blocks, span, width = mixer.shape
    flip = 1 if carry else 0
    free = pl.BlockSpec(memory_space=pl.ANY)
    sent = jax.ShapeDtypeStruct((tokens // 8, span), bf16)
    state = [(tokens + 16, width), (tokens, 128), (tokens, 128)]
    vm = pl.BlockSpec(memory_space=pltpu.VMEM)
    hb = pl.BlockSpec(memory_space=pltpu.HBM)
    if flip:
        shapes = (jax.ShapeDtypeStruct((8, tokens, width), bf16), sent)
        scratch = [pltpu.VMEM(shape, f32) for shape in state]
    else:
        shapes = tuple(jax.ShapeDtypeStruct(shape, f32) for shape in state) + (sent,)
        scratch = []
    return pl.pallas_call(
        functools.partial(embed_kernel, flip),
        out_shape=shapes,
        in_specs=[free] * 4 + [hb, vm, free] + [vm] * len(carry),
        out_specs=(vm,) * len(shapes),
        scratch_shapes=scratch + [
            pltpu.VMEM((tokens, pieces[0].shape[1]), bf16),
            pltpu.VMEM((depth, blocks * span), bf16),
            pltpu.VMEM((1, blocks * span), f32),
            pltpu.VMEM((blocks * span, width), bf16),
            pltpu.SemaphoreType.DMA((blocks,)),
            pltpu.SemaphoreType.DMA((blocks,)),
            pltpu.SemaphoreType.DMA((8,)),
        ],
        compiler_params=pltpu.CompilerParams(vmem_limit_bytes=40 << 20),
        cost_estimate=pl.CostEstimate(flops=3_500_000_000, transcendentals=100_000, bytes_accessed=8_000_000),
        name="embed_mate" if flip else "embed_own",
    )(*pieces, weight, bias, mixer, *carry)


def mix_kernel(hidden_hbm, own_hbm, mate_hbm, out, hidden, weight, total, sems):
    core = lax.axis_index("core")
    blocks, tokens, width = hidden_hbm.shape
    span = own_hbm.shape[1]
    parts = blocks // 2
    deep = 2 * width
    loads = []
    for k in range(parts):
        rows = pl.ds(k * deep, deep)
        pairs = [(own_hbm.at[rows, :], weight.at[rows, pl.ds(0, span)]),
                 (mate_hbm.at[rows, :], weight.at[rows, pl.ds(span, span)])]
        pairs += [(hidden_hbm.at[b], hidden.at[:, pl.ds(b * width, width)]) for b in (2 * k, 2 * k + 1)]
        loads.append([pltpu.make_async_copy(a, b, sems.at[k, n]) for n, (a, b) in enumerate(pairs)])
        for load in loads[-1]:
            load.start()
    for k in range(parts):
        for load in loads[k]:
            load.wait()
        at = slice(k * deep, (k + 1) * deep)
        part = jnp.dot(hidden[:, at], weight[at, :], preferred_element_type=f32)
        if k == 0:
            total[...] = part
        elif k < parts - 1:
            total[...] += part
        else:
            done = total[...] + part
    share = out.shape[1]
    high, across, size = lax.axis_index("zh"), lax.axis_index("x"), lax.axis_size("x")
    for q in range(tokens // share):
        rows = jnp.concatenate([done[b * share + q * 8:b * share + q * 8 + 8, :] for b in range(8)], axis=0).astype(bf16)
        r = (high + q // size) % 2 * size + (across + size - q % size) % size
        out[2 * r + core] = rows[:, 0:span]
        out[2 * r + 1 - core] = rows[:, span:2 * span]


def mix_call(hidden, own, mate):
    blocks, tokens, width = hidden.shape
    depth, span = own.shape
    hb = pl.BlockSpec(memory_space=pltpu.HBM)
    return pl.pallas_call(
        mix_kernel,
        out_shape=jax.ShapeDtypeStruct((16, tokens // 8, span), bf16),
        in_specs=[hb, hb, hb],
        out_specs=pl.BlockSpec(memory_space=pltpu.VMEM),
        scratch_shapes=[
            pltpu.VMEM((tokens, depth), bf16),
            pltpu.VMEM((depth, 2 * span), bf16),
            pltpu.VMEM((tokens, 2 * span), f32),
            pltpu.SemaphoreType.DMA((blocks // 2, 4)),
        ],
        compiler_params=pltpu.CompilerParams(vmem_limit_bytes=24 << 20),
        cost_estimate=pl.CostEstimate(flops=2_400_000_000, transcendentals=0, bytes_accessed=9_000_000),
        name="mlp_out",
    )(hidden, own, mate)


def split_kernel(whole, blocks, sems):
    width = blocks.shape[2]
    loads = [pltpu.make_async_copy(whole.at[:, pl.ds(b * width, width)], blocks.at[b], sems.at[b])
             for b in range(blocks.shape[0])]
    for load in loads:
        load.start()
    for load in loads:
        load.wait()


def split_call(whole, count):
    depth, width = whole.shape[0], whole.shape[1] // count
    return pl.pallas_call(
        split_kernel,
        out_shape=jax.ShapeDtypeStruct((count, depth, width), whole.dtype),
        in_specs=[pl.BlockSpec(memory_space=pltpu.HBM)],
        out_specs=pl.BlockSpec(memory_space=pltpu.VMEM),
        scratch_shapes=[pltpu.SemaphoreType.DMA((count,))],
        compiler_params=pltpu.CompilerParams(vmem_limit_bytes=58 << 20),
        cost_estimate=pl.CostEstimate(flops=0, transcendentals=0, bytes_accessed=2 * whole.size * 2),
        name="split_columns",
    )(whole)


def shift(value, axis, k):
    n = lax.axis_size(axis)
    return lax.ppermute(value, axis, [(i, (i + k) % n) for i in range(n)])


def swap(value):
    return lax.ppermute(value, "core", [(0, 1), (1, 0)])


def on_device(images, noise_field, stem_weight, level_one, down_weight, level_two, up_weight,
              out_weight, embed_weight, embed_bias, mlp_in, mlp_out):
    span = mlp_in.shape[0]
    own_in = lax.all_to_all(split_call(mlp_in, 8), ("zl", "y"), 0, 0)
    mate_out = swap(mlp_out)

    purified, patches = score_call(images, noise_field, stem_weight, level_one, down_weight, level_two,
                                   up_weight, out_weight)
    mate_out, patches = lax.optimization_barrier((mate_out, patches))
    patches = jnp.concatenate([patches] + [shift(patches, "x", k) for k in (1, 2, 3)], axis=0)
    patches = jnp.concatenate([patches, shift(patches, "zh", 1)], axis=0)
    patches = jnp.concatenate([patches, shift(patches, "zl", 1)], axis=0)
    pieces = [patches] + [shift(patches, "y", k) for k in (1, 2, 3)]
    own_in, *pieces = lax.optimization_barrier((own_in, *pieces))
    mate_in = swap(own_in)
    *carry, kept = embed_call(pieces, embed_weight, embed_bias[None], own_in, ())
    hidden, sent = embed_call(pieces, embed_weight, embed_bias[None], mate_in, tuple(carry))
    other = swap(sent)
    hidden = lax.all_to_all(hidden, ("zl", "y"), 0, 0)
    shares = mix_call(hidden, mlp_out, mate_out)
    shares = lax.all_to_all(shares, ("zh", "x", "core"), 0, 0)
    mixed = jnp.sum(shares.reshape(8, 2, 8, 8, span).astype(f32), axis=0)
    core = lax.axis_index("core")
    values = jnp.where(core == 0, jnp.stack([kept, other]), jnp.stack([other, kept]))
    encoded = mixed + values.reshape(2, 8, 8, span).astype(f32)
    encoded = encoded.transpose(1, 0, 2, 3).reshape(128, span).astype(bf16)
    return purified, encoded


def solution(mesh):
    fine = Mesh(mesh.devices.reshape(2, 4, 2, 4, 2), ("zh", "x", "zl", "y", "core"))
    row, col = ("zh", "x"), ("zl", "y", "core")
    images = P(row + col, None, None, None)
    placed = (images, images) + (P(),) * 8 + (P(col, row), P(row, col))
    return jax.shard_map(on_device, mesh=fine, in_specs=placed, out_specs=(images, P(row, col)),
                         check_vma=False)
```

```python
import functools
import math

import jax
import jax.numpy as jnp
from jax import lax
from jax.experimental import pallas as pl
from jax.experimental.pallas import tpu as pltpu
from jax.sharding import Mesh, PartitionSpec as P

step_size = 0.25
noise_gain = math.sqrt(0.5)
ln_epsilon = 1e-06
PATCH = 14
W1, W2 = 32, 16
CH = 256
f32, bf16 = jnp.float32, jnp.bfloat16


def gelu(v):
    inner = v * (0.7978845608028654 + 0.035677408136300125 * (v * v))
    half = 0.5 * v
    return half + half * jnp.tanh(inner)


def score_kernel(side, count, images, noise, stem_w, l1_hbm, down_hbm, l2_hbm, up_hbm, out_w,
                 purified, patches, raw, extra, pix, stem_x, stem_k, out_k, xa, xb, ca, cb, stream, coarse,
                 l1, down, l2, up, sems):
    half = side // 2
    span1, span2 = side * W1, half * W2
    pitch1, pitch2 = span1 + W1, span2 + W2
    loads = [pltpu.make_async_copy(l1_hbm.at[0], l1.at[0], sems.at[0]),
             pltpu.make_async_copy(l1_hbm.at[1], l1.at[1], sems.at[1]),
             pltpu.make_async_copy(down_hbm, down, sems.at[2]),
             pltpu.make_async_copy(l2_hbm, l2, sems.at[3]),
             pltpu.make_async_copy(up_hbm, up, sems.at[4]),
             pltpu.make_async_copy(l1_hbm.at[2], l1.at[2], sems.at[5]),
             pltpu.make_async_copy(l1_hbm.at[3], l1.at[3], sems.at[6])]
    for load in loads:
        load.start()

    mask1 = (lax.broadcasted_iota(jnp.int32, (span1, 1), 0) % W1) < side
    mask2 = (lax.broadcasted_iota(jnp.int32, (span2, 1), 0) % W2) < half

    def read(rows):
        return jnp.concatenate([stream[0, rows, :], stream[1, rows, :]], axis=1)

    def write(rows, value):
        stream[0, rows, :] = value[:, 0:128]
        stream[1, rows, :] = value[:, 128:256]

    for i in range(count + 1):
        z1 = jnp.zeros((W1, 3 * CH), bf16)
        z2 = jnp.zeros((W2, 3 * CH), bf16)
        xa[i * pitch1:i * pitch1 + W1, :] = z1
        xb[i * pitch1:i * pitch1 + W1, :] = z1
        ca[i * pitch2:i * pitch2 + W2, :] = z2
        cb[i * pitch2:i * pitch2 + W2, :] = z2
    raw[...] = jnp.zeros_like(raw)
    extra[...] = jnp.zeros_like(extra)
    stem_k[...] = jnp.zeros_like(stem_k)
    stem = stem_w[...].astype(f32)
    for dy in range(3):
        for dx in range(3):
            for c in range(3):
                k = (3 * dy + dx) * 3 + c
                at = 128 * dx + W1 * c + dy
                stem_k[at:at + 1, :] = stem[k:k + 1, :]
    column = lax.broadcasted_iota(jnp.int32, (8, 128), 1)
    colour = lax.broadcasted_iota(jnp.int32, (8, 128), 0)
    place = ((column == W1 * colour) & (colour < 3)).astype(bf16)
    out_k[...] = jnp.dot(out_w[...], place[0:3, :], preferred_element_type=f32).astype(bf16)

    for y in range(side):
        for c in range(3):
            at = W1 * c + y
            v, n = images[y, c], noise[y, c]
            for i in range(count):
                raw[i, at:at + 1, 0:side] = v[i:i + 1, :]
                extra[i, at:at + 1, 0:side] = n[i:i + 1, :]

    def shifted(ref, base, value):
        n, wide = value.shape
        ref[pl.ds(base, n), 0:wide] = pltpu.roll(value, 1, 0).astype(bf16)
        ref[pl.ds(base, n), wide:2 * wide] = value.astype(bf16)
        ref[pl.ds(base, n), 2 * wide:3 * wide] = pltpu.roll(value, n - 1, 0).astype(bf16)

    def each(body):
        def step(i, _):
            body(i, pl.multiple_of(W1 + i * pitch1, W1))
            return 0
        lax.fori_loop(0, count, step, 0)

    def conv(ref, base, n, width, weights):
        near = jnp.concatenate([ref[pl.ds(base - width, n), :], ref[pl.ds(base, n), :],
                                ref[pl.ds(base + width, n), :]], axis=1)
        return jnp.dot(near, weights[...], preferred_element_type=f32)

    def begin(i, base):
        across = jnp.transpose(raw[i].astype(bf16).astype(f32))[0:W1, :]
        for y in range(side):
            pix[y * W1:(y + 1) * W1, :] = pltpu.roll(across, (1 - y) % 128, 1)
        shifted(stem_x, 0, pix[...])
        acc = jnp.dot(stem_x[...], stem_k[...].astype(bf16), preferred_element_type=f32)
        write(pl.ds(base, span1), acc)
        shifted(xa, base, jnp.where(mask1, gelu(acc), 0.0))
    each(begin)

    loads[0].wait()

    def layer0(i, base):
        s = read(pl.ds(base, span1)) + conv(xa, base, span1, W1, l1.at[0])
        write(pl.ds(base, span1), s)
        shifted(xb, base, jnp.where(mask1, gelu(s), 0.0))
    each(layer0)

    loads[1].wait()

    def layer1(i, base):
        write(pl.ds(base, span1), read(pl.ds(base, span1)) + conv(xb, base, span1, W1, l1.at[1]))
    each(layer1)

    loads[2].wait()
    loads[3].wait()
    loads[4].wait()
    for i in range(count):
        base1, base2 = W1 + i * pitch1, W2 + i * pitch2
        cols = [read(pl.ds(base1 + b, span1 // 2, stride=2)).astype(bf16).reshape(half, 2, W2, CH) for b in range(2)]
        cells = jnp.concatenate([cols[b][:, a].reshape(span2, CH) for a in range(2) for b in range(2)], axis=1)
        acc = jnp.dot(cells, down[...], preferred_element_type=f32)
        coarse[base2:base2 + span2, :] = acc
        shifted(ca, base2, jnp.where(mask2, gelu(acc), 0.0))
    for i in range(count):
        base2 = W2 + i * pitch2
        s = coarse[base2:base2 + span2, :] + conv(ca, base2, span2, W2, l2.at[0])
        coarse[base2:base2 + span2, :] = s
        shifted(cb, base2, jnp.where(mask2, gelu(s), 0.0))
    for i in range(count):
        base1, base2 = W1 + i * pitch1, W2 + i * pitch2
        s = coarse[base2:base2 + span2, :] + conv(cb, base2, span2, W2, l2.at[1])
        s = s.astype(bf16)
        for a in range(2):
            for b in range(2):
                g = (2 * a + b) * CH
                part = jnp.dot(s, up[:, g:g + CH], preferred_element_type=f32)
                for y in range(half):
                    rows = pl.ds(base1 + (2 * y + a) * W1 + b, W2, stride=2)
                    write(rows, read(rows) + part[y * W2:(y + 1) * W2, :])

    def enter(i, base):
        shifted(xa, base, jnp.where(mask1, gelu(read(pl.ds(base, span1))), 0.0))
    each(enter)

    loads[5].wait()

    def layer2(i, base):
        s = read(pl.ds(base, span1)) + conv(xa, base, span1, W1, l1.at[2])
        write(pl.ds(base, span1), s)
        shifted(xb, base, jnp.where(mask1, gelu(s), 0.0))
    each(layer2)

    loads[6].wait()

    def layer3(i, base):
        s = read(pl.ds(base, span1)) + conv(xb, base, span1, W1, l1.at[3])
        score = jnp.dot(gelu(s).astype(bf16), out_k[...], preferred_element_type=f32)
        across = score[0:W1, :]
        for y in range(1, side):
            across += pltpu.roll(score[y * W1:(y + 1) * W1, :], y, 1)
        across = jnp.concatenate([across, jnp.zeros((128 - W1, 128), f32)], axis=0)
        raw[i] = raw[i] + step_size * jnp.transpose(across) + noise_gain * extra[i]
    each(layer3)

    for y in range(side):
        for c in range(3):
            at = W1 * c + y
            purified[y, c] = jnp.concatenate([raw[i, at:at + 1, 0:side] for i in range(count)], axis=0)

    lane = lax.broadcasted_iota(jnp.int32, (128, 128), 1)
    line = lax.broadcasted_iota(jnp.int32, (128, 128), 0)
    wide = []
    for i in range(count):
        rows = None
        for c in range(3):
            spread = ((lane == 3 * line + c) & (line < side)).astype(bf16)
            part = jnp.dot(raw[i, W1 * c:W1 * (c + 1), :].astype(bf16), spread, preferred_element_type=f32)
            rows = part if rows is None else rows + part
        wide.append(rows)
    wide = jnp.concatenate(wide, axis=0).astype(bf16)
    many, run = 4 * count, 3 * PATCH
    token = lax.broadcasted_iota(jnp.int32, (many, count * W1), 0)
    source = lax.broadcasted_iota(jnp.int32, (many, count * W1), 1)
    first = (token // 4) * W1 + ((token // 2) % 2) * PATCH
    lanes = lax.broadcasted_iota(jnp.int32, (many, 128), 1)
    second = (lax.broadcasted_iota(jnp.int32, (many, 128), 0) % 2) == 1
    pieces = [jnp.zeros((many, 128), f32) for _ in range(5)]
    for r in range(PATCH):
        z = jnp.dot((source == first + r).astype(bf16), wide, preferred_element_type=f32)
        z = jnp.where(second, pltpu.roll(z, 128 - run, 1), z)
        z = jnp.where(lanes < run, z, 0.0)
        k, at = (run * r) // 128, (run * r) % 128
        z = pltpu.roll(z, at, 1) if at else z
        pieces[k] += jnp.where(lanes >= at, z, 0.0)
        if at + run > 128:
            pieces[k + 1] += jnp.where(lanes < at, z, 0.0)
    tokens = jnp.concatenate(pieces, axis=1).astype(bf16)
    patches[...] = tokens


def score_call(images, noise, stem_w, l1, down, l2, up, out_w):
    count, side = images.shape[0], images.shape[1]
    rows1 = W1 + count * (side + 1) * W1
    rows2 = W2 + count * (side // 2 + 1) * W2
    images, noise = images.transpose(1, 3, 0, 2), noise.transpose(1, 3, 0, 2)
    vm = pl.BlockSpec(memory_space=pltpu.VMEM)
    hb = pl.BlockSpec(memory_space=pltpu.HBM)
    purified, patches = pl.pallas_call(
        functools.partial(score_kernel, side, count),
        out_shape=(jax.ShapeDtypeStruct(images.shape, f32), jax.ShapeDtypeStruct((4 * count, 640), bf16)),
        in_specs=[vm, vm, vm, hb, hb, hb, hb, vm],
        out_specs=(vm, vm),
        scratch_shapes=[
            pltpu.VMEM((count, 128, 128), f32),
            pltpu.VMEM((count, 128, 128), f32),
            pltpu.VMEM((side * W1, 128), f32),
            pltpu.VMEM((side * W1, 3 * 128), bf16),
            pltpu.VMEM((3 * 128, CH), f32),
            pltpu.VMEM((CH, 128), bf16),
            pltpu.VMEM((rows1, 3 * CH), bf16),
            pltpu.VMEM((rows1, 3 * CH), bf16),
            pltpu.VMEM((rows2, 3 * CH), bf16),
            pltpu.VMEM((rows2, 3 * CH), bf16),
            pltpu.VMEM((CH // 128, rows1, 128), f32),
            pltpu.VMEM((rows2, CH), f32),
            pltpu.VMEM(l1.shape, bf16),
            pltpu.VMEM(down.shape, bf16),
            pltpu.VMEM(l2.shape, bf16),
            pltpu.VMEM(up.shape, bf16),
            pltpu.SemaphoreType.DMA((7,)),
        ],
        compiler_params=pltpu.CompilerParams(vmem_limit_bytes=58 << 20),
        cost_estimate=pl.CostEstimate(flops=10_000_000_000, transcendentals=3_000_000, bytes_accessed=12_000_000),
        name="score_net",
    )(images, noise, stem_w, l1, down, l2, up, out_w)
    return purified.transpose(2, 0, 3, 1), patches


def embed_kernel(flip, piece0, piece1, piece2, piece3, weight_hbm, bias, mixer_hbm, *refs):
    if flip:
        (total_in, sums_in, squares_in, hidden, sent, total, sums, squares,
         patches, weight, offset, mixer, sems, mixer_sems, piece_sems) = refs
    else:
        total, sums, squares, sent, patches, weight, offset, mixer, sems, mixer_sems, piece_sems = refs
    core = lax.axis_index("core")
    side = 1 - core if flip else core
    level, line, lines = lax.axis_index("zl"), lax.axis_index("y"), lax.axis_size("y")
    place = level * lines + line
    depth, features = weight_hbm.shape
    blocks, span, width = mixer_hbm.shape
    tokens = patches.shape[0]
    step = 1024

    def first(b):
        return pl.multiple_of((2 * b + side) * span, 128)
    loads = [pltpu.make_async_copy(weight_hbm.at[:, pl.ds(first(b), span)], weight.at[:, pl.ds(b * span, span)], sems.at[b])
             for b in range(blocks)]
    mixes = [pltpu.make_async_copy(mixer_hbm.at[b], mixer.at[pl.ds(b * span, span), :], mixer_sems.at[b])
             for b in range(blocks)]
    share = tokens // 8
    moves = []
    for k, piece in enumerate((piece0, piece1, piece2, piece3)):
        for part in range(2):
            to = (level + part) % 2 * lines + (line + lines - k) % lines
            moves.append(pltpu.make_async_copy(
                piece.at[pl.ds(part * share, share), :],
                patches.at[pl.ds(pl.multiple_of(to * share, share), share), :], piece_sems.at[2 * k + part]))
    for move in moves:
        move.start()
    for b in range(blocks):
        loads[b].start()
        mixes[b].start()
    for b in range(blocks):
        offset[:, b * span:(b + 1) * span] = bias[:, pl.ds(first(b), span)]
    for move in moves:
        move.wait()
    pixels = patches[:, 0:depth]
    ones = jnp.ones((16, step), bf16)
    ready = 0
    for c in range(blocks * span // step):
        at = slice(c * step, (c + 1) * step)
        while ready * span < (c + 1) * step:
            loads[ready].wait()
            mixes[ready].wait()
            ready += 1
        e = jnp.dot(pixels, weight[:, at], preferred_element_type=f32)
        e = (e + offset[:, at]).astype(bf16)
        v = e.astype(f32)
        q = v * v
        a = sum(v[:, k:k + 128] for k in range(128, step, 128)) + v[:, 0:128]
        b = sum(q[:, k:k + 128] for k in range(128, step, 128)) + q[:, 0:128]
        part = jnp.dot(jnp.concatenate([e, ones], axis=0), mixer[at, :], preferred_element_type=f32)
        if c:
            a, b, part = a + sums[...], b + squares[...], part + total[...]
        elif flip:
            a, b, part = a + sums_in[...], b + squares_in[...], part + total_in[...]
        sums[...], squares[...], total[...] = a, b, part
    mine = jnp.concatenate([patches[b * share:b * share + 8, 0:depth].astype(f32) for b in range(8)], axis=0).astype(bf16)
    at = pl.ds(pl.multiple_of(place * span, 128), span)
    sent[...] = (jnp.dot(mine, weight[:, at], preferred_element_type=f32) + offset[:, at]).astype(bf16)
    if flip:
        mean = jnp.sum(sums[...], axis=1, keepdims=True) / features
        square = jnp.sum(squares[...], axis=1, keepdims=True) / features
        scale = lax.rsqrt(square - mean * mean + ln_epsilon)
        column = total[tokens:tokens + 1, :]
        value = gelu((total[0:tokens, :] - mean * column) * scale).astype(bf16)
        hidden[...] = value


def embed_call(pieces, weight, bias, mixer, carry):
    tokens, depth = 4 * pieces[0].shape[0], weight.shape[0]
    blocks, span, width = mixer.shape
    flip = 1 if carry else 0
    free = pl.BlockSpec(memory_space=pl.ANY)
    sent = jax.ShapeDtypeStruct((tokens // 8, span), bf16)
    state = [(tokens + 16, width), (tokens, 128), (tokens, 128)]
    vm = pl.BlockSpec(memory_space=pltpu.VMEM)
    hb = pl.BlockSpec(memory_space=pltpu.HBM)
    if flip:
        shapes = (jax.ShapeDtypeStruct((tokens, width), bf16), sent)
        scratch = [pltpu.VMEM(shape, f32) for shape in state]
    else:
        shapes = tuple(jax.ShapeDtypeStruct(shape, f32) for shape in state) + (sent,)
        scratch = []
    return pl.pallas_call(
        functools.partial(embed_kernel, flip),
        out_shape=shapes,
        in_specs=[free] * 4 + [hb, vm, free] + [vm] * len(carry),
        out_specs=(vm,) * len(shapes),
        scratch_shapes=scratch + [
            pltpu.VMEM((tokens, pieces[0].shape[1]), bf16),
            pltpu.VMEM((depth, blocks * span), bf16),
            pltpu.VMEM((1, blocks * span), f32),
            pltpu.VMEM((blocks * span, width), bf16),
            pltpu.SemaphoreType.DMA((blocks,)),
            pltpu.SemaphoreType.DMA((blocks,)),
            pltpu.SemaphoreType.DMA((8,)),
        ],
        compiler_params=pltpu.CompilerParams(vmem_limit_bytes=40 << 20),
        cost_estimate=pl.CostEstimate(flops=3_500_000_000, transcendentals=100_000, bytes_accessed=8_000_000),
        name="embed_mate" if flip else "embed_own",
    )(*pieces, weight, bias, mixer, *carry)


def mix_kernel(places, begin, end, *refs):
    refs = list(refs)
    total_in = None if begin else refs.pop(0)
    hidden = [refs.pop(0) for _ in places]
    own_hbm, mate_hbm, out, weight, sems = refs
    core = lax.axis_index("core")
    level, line, lines = lax.axis_index("zl"), lax.axis_index("y"), lax.axis_size("y")
    span = own_hbm.shape[1]
    width = hidden[0].shape[1]
    loads = []
    for n, (z, y) in enumerate(places):
        at = ((level + z) % 2 * lines + (line + y) % lines) * width
        for k, source in enumerate((own_hbm, mate_hbm)):
            loads.append(pltpu.make_async_copy(source.at[pl.ds(pl.multiple_of(at, width), width), :],
                                               weight.at[pl.ds(n * width, width), pl.ds(k * span, span)], sems.at[n, k]))
            loads[-1].start()
    for load in loads:
        load.wait()
    h = jnp.concatenate([block[...] for block in hidden], axis=1)
    done = jnp.dot(h, weight[...], preferred_element_type=f32)
    if not begin:
        done += total_in[...]
    if not end:
        out[...] = done
        return
    share = out.shape[1]
    tokens = done.shape[0]
    high, across, size = lax.axis_index("zh"), lax.axis_index("x"), lax.axis_size("x")
    for q in range(tokens // share):
        rows = jnp.concatenate([done[b * share + q * 8:b * share + q * 8 + 8, :] for b in range(8)], axis=0).astype(bf16)
        r = (high + q // size) % 2 * size + (across + size - q % size) % size
        out[2 * r + core] = rows[:, 0:span]
        out[2 * r + 1 - core] = rows[:, span:2 * span]


def mix_call(total, blocks, own, mate, end=False):
    places = tuple(place for place, _ in blocks)
    hidden = [block for _, block in blocks]
    tokens, width = hidden[0].shape
    span = own.shape[1]
    begin = total is None
    shape = jax.ShapeDtypeStruct((16, tokens // 8, span), bf16) if end else jax.ShapeDtypeStruct((tokens, 2 * span), f32)
    vm = pl.BlockSpec(memory_space=pltpu.VMEM)
    hb = pl.BlockSpec(memory_space=pltpu.HBM)
    return pl.pallas_call(
        functools.partial(mix_kernel, places, begin, end),
        out_shape=shape,
        in_specs=[vm] * (len(hidden) + (not begin)) + [hb, hb],
        out_specs=vm,
        scratch_shapes=[
            pltpu.VMEM((len(places) * width, 2 * span), bf16),
            pltpu.SemaphoreType.DMA((len(places), 2)),
        ],
        compiler_params=pltpu.CompilerParams(vmem_limit_bytes=24 << 20),
        cost_estimate=pl.CostEstimate(flops=2 * len(places) * tokens * width * 2 * span, transcendentals=0,
                                      bytes_accessed=len(places) * (tokens + 2 * span) * width * 2 + tokens * span * 8),
        name="mlp_out_" + str(len(places)),
    )(*([] if begin else [total]), *hidden, own, mate)


def split_kernel(whole, blocks, sems):
    width = blocks.shape[2]
    loads = [pltpu.make_async_copy(whole.at[:, pl.ds(b * width, width)], blocks.at[b], sems.at[b])
             for b in range(blocks.shape[0])]
    for load in loads:
        load.start()
    for load in loads:
        load.wait()


def split_call(whole, count):
    depth, width = whole.shape[0], whole.shape[1] // count
    return pl.pallas_call(
        split_kernel,
        out_shape=jax.ShapeDtypeStruct((count, depth, width), whole.dtype),
        in_specs=[pl.BlockSpec(memory_space=pltpu.HBM)],
        out_specs=pl.BlockSpec(memory_space=pltpu.VMEM),
        scratch_shapes=[pltpu.SemaphoreType.DMA((count,))],
        compiler_params=pltpu.CompilerParams(vmem_limit_bytes=58 << 20),
        cost_estimate=pl.CostEstimate(flops=0, transcendentals=0, bytes_accessed=2 * whole.size * 2),
        name="split_columns",
    )(whole)


def shift(value, axis, k):
    n = lax.axis_size(axis)
    return lax.ppermute(value, axis, [(i, (i + k) % n) for i in range(n)])


def swap(value):
    return lax.ppermute(value, "core", [(0, 1), (1, 0)])


def on_device(images, noise_field, stem_weight, level_one, down_weight, level_two, up_weight,
              out_weight, embed_weight, embed_bias, mlp_in, mlp_out):
    span = mlp_in.shape[0]
    own_in = lax.all_to_all(split_call(mlp_in, 8), ("zl", "y"), 0, 0)
    mate_out = swap(mlp_out)

    purified, patches = score_call(images, noise_field, stem_weight, level_one, down_weight, level_two,
                                   up_weight, out_weight)
    mate_out, patches = lax.optimization_barrier((mate_out, patches))
    patches = jnp.concatenate([patches] + [shift(patches, "x", k) for k in (1, 2, 3)], axis=0)
    patches = jnp.concatenate([patches, shift(patches, "zh", 1)], axis=0)
    patches = jnp.concatenate([patches, shift(patches, "zl", 1)], axis=0)
    pieces = [patches] + [shift(patches, "y", k) for k in (1, 2, 3)]
    own_in, *pieces = lax.optimization_barrier((own_in, *pieces))
    mate_in = swap(own_in)
    *carry, kept = embed_call(pieces, embed_weight, embed_bias[None], own_in, ())
    hidden, sent = embed_call(pieces, embed_weight, embed_bias[None], mate_in, tuple(carry))
    other = swap(sent)
    far = shift(hidden, "zl", 1)
    below = shift(hidden, "y", 1)
    above = shift(hidden, "y", 3)
    across = shift(below, "y", 1)
    far_above = shift(far, "y", 3)
    far_below = shift(below, "zl", 1)
    total = mix_call(None, [((0, 0), hidden), ((1, 0), far), ((0, 3), below), ((0, 1), above)], mlp_out, mate_out)
    half = hidden.shape[0] // 2
    last = jnp.concatenate([shift(far_below[:half], "y", 1), shift(far_above[half:], "y", 3)], axis=0)
    total = mix_call(total, [((0, 2), across), ((1, 1), far_above), ((1, 3), far_below)], mlp_out, mate_out)
    shares = mix_call(total, [((1, 2), last)], mlp_out, mate_out, end=True)
    shares = lax.all_to_all(shares, ("zh", "x", "core"), 0, 0)
    mixed = jnp.sum(shares.reshape(8, 2, 8, 8, span).astype(f32), axis=0)
    core = lax.axis_index("core")
    values = jnp.where(core == 0, jnp.stack([kept, other]), jnp.stack([other, kept]))
    encoded = mixed + values.reshape(2, 8, 8, span).astype(f32)
    encoded = encoded.transpose(1, 0, 2, 3).reshape(128, span).astype(bf16)
    return purified, encoded


def solution(mesh):
    fine = Mesh(mesh.devices.reshape(2, 4, 2, 4, 2), ("zh", "x", "zl", "y", "core"))
    row, col = ("zh", "x"), ("zl", "y", "core")
    images = P(row + col, None, None, None)
    placed = (images, images) + (P(),) * 8 + (P(col, row), P(row, col))
    return jax.shard_map(on_device, mesh=fine, in_specs=placed, out_specs=(images, P(row, col)),
                         check_vma=False)
```

```python
import functools
import math

import jax
import jax.numpy as jnp
from jax import lax
from jax.experimental import pallas as pl
from jax.experimental.pallas import tpu as pltpu
from jax.sharding import Mesh, PartitionSpec as P

step_size = 0.25
noise_gain = math.sqrt(0.5)
ln_epsilon = 1e-06
PATCH = 14
W1, W2 = 32, 16
CH = 256
f32, bf16 = jnp.float32, jnp.bfloat16


def gelu(v):
    inner = v * (0.7978845608028654 + 0.035677408136300125 * (v * v))
    half = 0.5 * v
    return half + half * jnp.tanh(inner)


def score_kernel(side, count, images, noise, stem_w, l1_hbm, down_hbm, l2_hbm, up_hbm, out_w,
                 purified, patches, raw, extra, pix, stem_x, stem_k, out_k, xa, xb, ca, cb, stream, coarse,
                 l1, down, l2, up, sems):
    half = side // 2
    span1, span2 = side * W1, half * W2
    pitch1, pitch2 = span1 + W1, span2 + W2
    loads = [pltpu.make_async_copy(l1_hbm.at[0], l1.at[0], sems.at[0]),
             pltpu.make_async_copy(l1_hbm.at[1], l1.at[1], sems.at[1]),
             pltpu.make_async_copy(down_hbm, down, sems.at[2]),
             pltpu.make_async_copy(l2_hbm, l2, sems.at[3]),
             pltpu.make_async_copy(up_hbm, up, sems.at[4]),
             pltpu.make_async_copy(l1_hbm.at[2], l1.at[2], sems.at[5]),
             pltpu.make_async_copy(l1_hbm.at[3], l1.at[3], sems.at[6])]
    for load in loads:
        load.start()

    mask1 = (lax.broadcasted_iota(jnp.int32, (span1, 1), 0) % W1) < side
    mask2 = (lax.broadcasted_iota(jnp.int32, (span2, 1), 0) % W2) < half

    def read(rows):
        return jnp.concatenate([stream[0, rows, :], stream[1, rows, :]], axis=1)

    def write(rows, value):
        stream[0, rows, :] = value[:, 0:128]
        stream[1, rows, :] = value[:, 128:256]

    for i in range(count + 1):
        z1 = jnp.zeros((W1, 3 * CH), bf16)
        z2 = jnp.zeros((W2, 3 * CH), bf16)
        xa[i * pitch1:i * pitch1 + W1, :] = z1
        xb[i * pitch1:i * pitch1 + W1, :] = z1
        ca[i * pitch2:i * pitch2 + W2, :] = z2
        cb[i * pitch2:i * pitch2 + W2, :] = z2
    raw[...] = jnp.zeros_like(raw)
    extra[...] = jnp.zeros_like(extra)
    stem_k[...] = jnp.zeros_like(stem_k)
    stem = stem_w[...].astype(f32)
    for dy in range(3):
        for dx in range(3):
            for c in range(3):
                k = (3 * dy + dx) * 3 + c
                at = 128 * dx + W1 * c + dy
                stem_k[at:at + 1, :] = stem[k:k + 1, :]
    column = lax.broadcasted_iota(jnp.int32, (8, 128), 1)
    colour = lax.broadcasted_iota(jnp.int32, (8, 128), 0)
    place = ((column == W1 * colour) & (colour < 3)).astype(bf16)
    out_k[...] = lax.dot_general(out_w[...], place[0:3, :], (((0,), (0,)), ((), ())), preferred_element_type=f32).astype(bf16)

    for y in range(side):
        for c in range(3):
            at = W1 * c + y
            v, n = images[y, c], noise[y, c]
            for i in range(count):
                raw[i, at:at + 1, 0:side] = v[i:i + 1, :]
                extra[i, at:at + 1, 0:side] = n[i:i + 1, :]

    def shifted(ref, base, value):
        n, wide = value.shape
        ref[pl.ds(base, n), 0:wide] = pltpu.roll(value, 1, 0).astype(bf16)
        ref[pl.ds(base, n), wide:2 * wide] = value.astype(bf16)
        ref[pl.ds(base, n), 2 * wide:3 * wide] = pltpu.roll(value, n - 1, 0).astype(bf16)

    def each(body):
        def step(i, _):
            body(i, pl.multiple_of(W1 + i * pitch1, W1))
            return 0
        lax.fori_loop(0, count, step, 0)

    def conv(ref, base, n, width, weights):
        near = jnp.concatenate([ref[pl.ds(base - width, n), :], ref[pl.ds(base, n), :],
                                ref[pl.ds(base + width, n), :]], axis=1)
        return jnp.dot(near, weights[...], preferred_element_type=f32)

    def begin(i, base):
        across = jnp.transpose(raw[i].astype(bf16).astype(f32))[0:W1, :]
        for y in range(side):
            pix[y * W1:(y + 1) * W1, :] = pltpu.roll(across, (1 - y) % 128, 1)
        shifted(stem_x, 0, pix[...])
        acc = jnp.dot(stem_x[...], stem_k[...].astype(bf16), preferred_element_type=f32)
        write(pl.ds(base, span1), acc)
        shifted(xa, base, jnp.where(mask1, gelu(acc), 0.0))
    each(begin)

    loads[0].wait()

    def layer0(i, base):
        s = read(pl.ds(base, span1)) + conv(xa, base, span1, W1, l1.at[0])
        write(pl.ds(base, span1), s)
        shifted(xb, base, jnp.where(mask1, gelu(s), 0.0))
    each(layer0)

    loads[1].wait()

    def layer1(i, base):
        write(pl.ds(base, span1), read(pl.ds(base, span1)) + conv(xb, base, span1, W1, l1.at[1]))
    each(layer1)

    loads[2].wait()
    loads[3].wait()
    loads[4].wait()
    for i in range(count):
        base1, base2 = W1 + i * pitch1, W2 + i * pitch2
        cols = [read(pl.ds(base1 + b, span1 // 2, stride=2)).astype(bf16).reshape(half, 2, W2, CH) for b in range(2)]
        cells = jnp.concatenate([cols[b][:, a].reshape(span2, CH) for a in range(2) for b in range(2)], axis=1)
        acc = jnp.dot(cells, down[...], preferred_element_type=f32)
        coarse[base2:base2 + span2, :] = acc
        shifted(ca, base2, jnp.where(mask2, gelu(acc), 0.0))
    for i in range(count):
        base2 = W2 + i * pitch2
        s = coarse[base2:base2 + span2, :] + conv(ca, base2, span2, W2, l2.at[0])
        coarse[base2:base2 + span2, :] = s
        shifted(cb, base2, jnp.where(mask2, gelu(s), 0.0))
    for i in range(count):
        base1, base2 = W1 + i * pitch1, W2 + i * pitch2
        s = coarse[base2:base2 + span2, :] + conv(cb, base2, span2, W2, l2.at[1])
        s = s.astype(bf16)
        for a in range(2):
            for b in range(2):
                g = (2 * a + b) * CH
                part = jnp.dot(s, up[:, g:g + CH], preferred_element_type=f32)
                for y in range(half):
                    rows = pl.ds(base1 + (2 * y + a) * W1 + b, W2, stride=2)
                    write(rows, read(rows) + part[y * W2:(y + 1) * W2, :])

    def enter(i, base):
        shifted(xa, base, jnp.where(mask1, gelu(read(pl.ds(base, span1))), 0.0))
    each(enter)

    loads[5].wait()

    def layer2(i, base):
        s = read(pl.ds(base, span1)) + conv(xa, base, span1, W1, l1.at[2])
        write(pl.ds(base, span1), s)
        shifted(xb, base, jnp.where(mask1, gelu(s), 0.0))
    each(layer2)

    loads[6].wait()

    def layer3(i, base):
        s = read(pl.ds(base, span1)) + conv(xb, base, span1, W1, l1.at[3])
        score = jnp.dot(gelu(s).astype(bf16), out_k[...], preferred_element_type=f32)
        across = score[0:W1, :]
        for y in range(1, side):
            across += pltpu.roll(score[y * W1:(y + 1) * W1, :], y, 1)
        across = jnp.concatenate([across, jnp.zeros((128 - W1, 128), f32)], axis=0)
        raw[i] = raw[i] + step_size * jnp.transpose(across) + noise_gain * extra[i]
    each(layer3)

    for y in range(side):
        for c in range(3):
            at = W1 * c + y
            purified[y, c] = jnp.concatenate([raw[i, at:at + 1, 0:side] for i in range(count)], axis=0)

    lane = lax.broadcasted_iota(jnp.int32, (128, 128), 1)
    line = lax.broadcasted_iota(jnp.int32, (128, 128), 0)
    wide = []
    for i in range(count):
        rows = None
        for c in range(3):
            spread = ((lane == 3 * line + c) & (line < side)).astype(bf16)
            part = jnp.dot(raw[i, W1 * c:W1 * (c + 1), :].astype(bf16), spread, preferred_element_type=f32)
            rows = part if rows is None else rows + part
        wide.append(rows)
    wide = jnp.concatenate(wide, axis=0).astype(bf16)
    many, run = 4 * count, 3 * PATCH
    token = lax.broadcasted_iota(jnp.int32, (many, count * W1), 0)
    source = lax.broadcasted_iota(jnp.int32, (many, count * W1), 1)
    first = (token // 4) * W1 + ((token // 2) % 2) * PATCH
    lanes = lax.broadcasted_iota(jnp.int32, (many, 128), 1)
    second = (lax.broadcasted_iota(jnp.int32, (many, 128), 0) % 2) == 1
    pieces = [jnp.zeros((many, 128), f32) for _ in range(5)]
    for r in range(PATCH):
        z = jnp.dot((source == first + r).astype(bf16), wide, preferred_element_type=f32)
        z = jnp.where(second, pltpu.roll(z, 128 - run, 1), z)
        z = jnp.where(lanes < run, z, 0.0)
        k, at = (run * r) // 128, (run * r) % 128
        z = pltpu.roll(z, at, 1) if at else z
        pieces[k] += jnp.where(lanes >= at, z, 0.0)
        if at + run > 128:
            pieces[k + 1] += jnp.where(lanes < at, z, 0.0)
    tokens = jnp.concatenate(pieces, axis=1).astype(bf16)
    patches[...] = tokens


def score_call(images, noise, stem_w, l1, down, l2, up, out_w):
    count, side = images.shape[0], images.shape[1]
    rows1 = W1 + count * (side + 1) * W1
    rows2 = W2 + count * (side // 2 + 1) * W2
    images, noise = images.transpose(1, 3, 0, 2), noise.transpose(1, 3, 0, 2)
    vm = pl.BlockSpec(memory_space=pltpu.VMEM)
    hb = pl.BlockSpec(memory_space=pltpu.HBM)
    purified, patches = pl.pallas_call(
        functools.partial(score_kernel, side, count),
        out_shape=(jax.ShapeDtypeStruct(images.shape, f32), jax.ShapeDtypeStruct((4 * count, 640), bf16)),
        in_specs=[vm, vm, vm, hb, hb, hb, hb, vm],
        out_specs=(vm, vm),
        scratch_shapes=[
            pltpu.VMEM((count, 128, 128), f32),
            pltpu.VMEM((count, 128, 128), f32),
            pltpu.VMEM((side * W1, 128), f32),
            pltpu.VMEM((side * W1, 3 * 128), bf16),
            pltpu.VMEM((3 * 128, CH), f32),
            pltpu.VMEM((CH, 128), bf16),
            pltpu.VMEM((rows1, 3 * CH), bf16),
            pltpu.VMEM((rows1, 3 * CH), bf16),
            pltpu.VMEM((rows2, 3 * CH), bf16),
            pltpu.VMEM((rows2, 3 * CH), bf16),
            pltpu.VMEM((CH // 128, rows1, 128), f32),
            pltpu.VMEM((rows2, CH), f32),
            pltpu.VMEM(l1.shape, bf16),
            pltpu.VMEM(down.shape, bf16),
            pltpu.VMEM(l2.shape, bf16),
            pltpu.VMEM(up.shape, bf16),
            pltpu.SemaphoreType.DMA((7,)),
        ],
        compiler_params=pltpu.CompilerParams(vmem_limit_bytes=58 << 20),
        cost_estimate=pl.CostEstimate(flops=10_000_000_000, transcendentals=3_000_000, bytes_accessed=12_000_000),
        name="score_net",
    )(images, noise, stem_w, l1, down, l2, up, out_w.T)
    return purified.transpose(2, 0, 3, 1), patches


def embed_kernel(flip, piece0, piece1, piece2, piece3, weight_hbm, bias, mixer_hbm, *refs):
    if flip:
        (total_in, sums_in, squares_in, hidden, sent, total, sums, squares,
         patches, weight, offset, mixer, sems, mixer_sems, piece_sems) = refs
    else:
        total, sums, squares, sent, patches, weight, offset, mixer, sems, mixer_sems, piece_sems = refs
    core = lax.axis_index("core")
    side = 1 - core if flip else core
    level, line, lines = lax.axis_index("zl"), lax.axis_index("y"), lax.axis_size("y")
    place = level * lines + line
    depth, features = weight_hbm.shape
    blocks, span, width = mixer_hbm.shape
    tokens = patches.shape[0]
    step = 1024

    def first(b):
        return pl.multiple_of((2 * b + side) * span, 128)
    loads = [pltpu.make_async_copy(weight_hbm.at[:, pl.ds(first(b), span)], weight.at[:, pl.ds(b * span, span)], sems.at[b])
             for b in range(blocks)]
    mixes = [pltpu.make_async_copy(mixer_hbm.at[b], mixer.at[pl.ds(b * span, span), :], mixer_sems.at[b])
             for b in range(blocks)]
    share = tokens // 8
    moves = []
    for k, piece in enumerate((piece0, piece1, piece2, piece3)):
        for part in range(2):
            to = (level + part) % 2 * lines + (line + lines - k) % lines
            moves.append(pltpu.make_async_copy(
                piece.at[pl.ds(part * share, share), :],
                patches.at[pl.ds(pl.multiple_of(to * share, share), share), :], piece_sems.at[2 * k + part]))
    for move in moves:
        move.start()
    for b in range(blocks):
        loads[b].start()
        mixes[b].start()
    for b in range(blocks):
        offset[:, b * span:(b + 1) * span] = bias[:, pl.ds(first(b), span)]
    for move in moves:
        move.wait()
    pixels = patches[:, 0:depth]
    ones = jnp.ones((16, step), bf16)
    ready = 0
    for c in range(blocks * span // step):
        at = slice(c * step, (c + 1) * step)
        while ready * span < (c + 1) * step:
            loads[ready].wait()
            mixes[ready].wait()
            ready += 1
        e = jnp.dot(pixels, weight[:, at], preferred_element_type=f32)
        e = (e + offset[:, at]).astype(bf16)
        v = e.astype(f32)
        q = v * v
        a = sum(v[:, k:k + 128] for k in range(128, step, 128)) + v[:, 0:128]
        b = sum(q[:, k:k + 128] for k in range(128, step, 128)) + q[:, 0:128]
        part = jnp.dot(jnp.concatenate([e, ones], axis=0), mixer[at, :], preferred_element_type=f32)
        if c:
            a, b, part = a + sums[...], b + squares[...], part + total[...]
        elif flip:
            a, b, part = a + sums_in[...], b + squares_in[...], part + total_in[...]
        sums[...], squares[...], total[...] = a, b, part
    mine = jnp.concatenate([patches[b * share:b * share + 8, 0:depth].astype(f32) for b in range(8)], axis=0).astype(bf16)
    at = pl.ds(pl.multiple_of(place * span, 128), span)
    sent[...] = (jnp.dot(mine, weight[:, at], preferred_element_type=f32) + offset[:, at]).astype(bf16)
    if flip:
        mean = jnp.sum(sums[...], axis=1, keepdims=True) / features
        square = jnp.sum(squares[...], axis=1, keepdims=True) / features
        scale = lax.rsqrt(square - mean * mean + ln_epsilon)
        column = total[tokens:tokens + 1, :]
        value = gelu((total[0:tokens, :] - mean * column) * scale).astype(bf16)
        hidden[...] = value


def embed_call(pieces, weight, bias, mixer, carry):
    tokens, depth = 4 * pieces[0].shape[0], weight.shape[0]
    blocks, span, width = mixer.shape
    flip = 1 if carry else 0
    free = pl.BlockSpec(memory_space=pl.ANY)
    sent = jax.ShapeDtypeStruct((tokens // 8, span), bf16)
    state = [(tokens + 16, width), (tokens, 128), (tokens, 128)]
    vm = pl.BlockSpec(memory_space=pltpu.VMEM)
    hb = pl.BlockSpec(memory_space=pltpu.HBM)
    if flip:
        shapes = (jax.ShapeDtypeStruct((tokens, width), bf16), sent)
        scratch = [pltpu.VMEM(shape, f32) for shape in state]
    else:
        shapes = tuple(jax.ShapeDtypeStruct(shape, f32) for shape in state) + (sent,)
        scratch = []
    return pl.pallas_call(
        functools.partial(embed_kernel, flip),
        out_shape=shapes,
        in_specs=[free] * 4 + [hb, vm, free] + [vm] * len(carry),
        out_specs=(vm,) * len(shapes),
        scratch_shapes=scratch + [
            pltpu.VMEM((tokens, pieces[0].shape[1]), bf16),
            pltpu.VMEM((depth, blocks * span), bf16),
            pltpu.VMEM((1, blocks * span), f32),
            pltpu.VMEM((blocks * span, width), bf16),
            pltpu.SemaphoreType.DMA((blocks,)),
            pltpu.SemaphoreType.DMA((blocks,)),
            pltpu.SemaphoreType.DMA((8,)),
        ],
        compiler_params=pltpu.CompilerParams(vmem_limit_bytes=40 << 20),
        cost_estimate=pl.CostEstimate(flops=3_500_000_000, transcendentals=100_000, bytes_accessed=8_000_000),
        name="embed_mate" if flip else "embed_own",
    )(*pieces, weight, bias, mixer, *carry)


def mix_kernel(places, begin, end, *refs):
    refs = list(refs)
    total_in = None if begin else refs.pop(0)
    hidden = [refs.pop(0) for _ in places]
    own_hbm, mate_hbm, out, weight, sems = refs
    core = lax.axis_index("core")
    level, line, lines = lax.axis_index("zl"), lax.axis_index("y"), lax.axis_size("y")
    span = own_hbm.shape[1]
    width = hidden[0].shape[1]
    loads = []
    for n, (z, y) in enumerate(places):
        at = ((level + z) % 2 * lines + (line + y) % lines) * width
        for k, source in enumerate((own_hbm, mate_hbm)):
            loads.append(pltpu.make_async_copy(source.at[pl.ds(pl.multiple_of(at, width), width), :],
                                               weight.at[pl.ds(n * width, width), pl.ds(k * span, span)], sems.at[n, k]))
            loads[-1].start()
    for load in loads:
        load.wait()
    h = jnp.concatenate([block[...] for block in hidden], axis=1)
    done = jnp.dot(h, weight[...], preferred_element_type=f32)
    if not begin:
        done += total_in[...]
    if not end:
        out[...] = done
        return
    share = out.shape[1]
    tokens = done.shape[0]
    high, across, size = lax.axis_index("zh"), lax.axis_index("x"), lax.axis_size("x")
    for q in range(tokens // share):
        rows = jnp.concatenate([done[b * share + q * 8:b * share + q * 8 + 8, :] for b in range(8)], axis=0).astype(bf16)
        r = (high + q // size) % 2 * size + (across + size - q % size) % size
        out[2 * r + core] = rows[:, 0:span]
        out[2 * r + 1 - core] = rows[:, span:2 * span]


def mix_call(total, blocks, own, mate, end=False):
    places = tuple(place for place, _ in blocks)
    hidden = [block for _, block in blocks]
    tokens, width = hidden[0].shape
    span = own.shape[1]
    begin = total is None
    shape = jax.ShapeDtypeStruct((16, tokens // 8, span), bf16) if end else jax.ShapeDtypeStruct((tokens, 2 * span), f32)
    vm = pl.BlockSpec(memory_space=pltpu.VMEM)
    hb = pl.BlockSpec(memory_space=pltpu.HBM)
    return pl.pallas_call(
        functools.partial(mix_kernel, places, begin, end),
        out_shape=shape,
        in_specs=[vm] * (len(hidden) + (not begin)) + [hb, hb],
        out_specs=vm,
        scratch_shapes=[
            pltpu.VMEM((len(places) * width, 2 * span), bf16),
            pltpu.SemaphoreType.DMA((len(places), 2)),
        ],
        compiler_params=pltpu.CompilerParams(vmem_limit_bytes=24 << 20),
        cost_estimate=pl.CostEstimate(flops=2 * len(places) * tokens * width * 2 * span, transcendentals=0,
                                      bytes_accessed=len(places) * (tokens + 2 * span) * width * 2 + tokens * span * 8),
        name="mlp_out_" + str(len(places)),
    )(*([] if begin else [total]), *hidden, own, mate)


def split_kernel(whole, blocks, sems):
    width = blocks.shape[2]
    loads = [pltpu.make_async_copy(whole.at[:, pl.ds(b * width, width)], blocks.at[b], sems.at[b])
             for b in range(blocks.shape[0])]
    for load in loads:
        load.start()
    for load in loads:
        load.wait()


def split_call(whole, count):
    depth, width = whole.shape[0], whole.shape[1] // count
    return pl.pallas_call(
        split_kernel,
        out_shape=jax.ShapeDtypeStruct((count, depth, width), whole.dtype),
        in_specs=[pl.BlockSpec(memory_space=pltpu.HBM)],
        out_specs=pl.BlockSpec(memory_space=pltpu.VMEM),
        scratch_shapes=[pltpu.SemaphoreType.DMA((count,))],
        compiler_params=pltpu.CompilerParams(vmem_limit_bytes=58 << 20),
        cost_estimate=pl.CostEstimate(flops=0, transcendentals=0, bytes_accessed=2 * whole.size * 2),
        name="split_columns",
    )(whole)


def shift(value, axis, k):
    n = lax.axis_size(axis)
    return lax.ppermute(value, axis, [(i, (i + k) % n) for i in range(n)])


def swap(value):
    return lax.ppermute(value, "core", [(0, 1), (1, 0)])


def on_device(images, noise_field, stem_weight, level_one, down_weight, level_two, up_weight,
              out_weight, embed_weight, embed_bias, mlp_in, mlp_out):
    span = mlp_in.shape[0]
    own_in = lax.all_to_all(split_call(mlp_in, 8), ("zl", "y"), 0, 0)
    mate_out = swap(mlp_out)

    purified, patches = score_call(images, noise_field, stem_weight, level_one, down_weight, level_two,
                                   up_weight, out_weight)
    mate_out, patches = lax.optimization_barrier((mate_out, patches))
    patches = jnp.concatenate([patches] + [shift(patches, "x", k) for k in (1, 2, 3)], axis=0)
    both = lax.ppermute(patches, ("zh", "zl"), [(i, 3 - i) for i in range(4)])
    patches = jnp.concatenate([patches, shift(patches, "zh", 1), shift(patches, "zl", 1), both], axis=0)
    pieces = [patches] + [shift(patches, "y", k) for k in (1, 2, 3)]
    own_in, *pieces = lax.optimization_barrier((own_in, *pieces))
    mate_in = swap(own_in)
    *carry, kept = embed_call(pieces, embed_weight, embed_bias[None], own_in, ())
    hidden, sent = embed_call(pieces, embed_weight, embed_bias[None], mate_in, tuple(carry))
    other = swap(sent)
    far = shift(hidden, "zl", 1)
    below = shift(hidden, "y", 1)
    above = shift(hidden, "y", 3)
    far, below, above = lax.optimization_barrier((far, below, above))
    across = shift(below, "y", 1)
    far_above = shift(far, "y", 3)
    far_below = shift(below, "zl", 1)
    total = mix_call(None, [((0, 0), hidden), ((1, 0), far), ((0, 3), below), ((0, 1), above)], mlp_out, mate_out)
    far_below, far_above, total = lax.optimization_barrier((far_below, far_above, total))
    half = hidden.shape[0] // 2
    last = jnp.concatenate([shift(far_below[:half], "y", 1), shift(far_above[half:], "y", 3)], axis=0)
    total = mix_call(total, [((0, 2), across), ((1, 1), far_above), ((1, 3), far_below)], mlp_out, mate_out)
    shares = mix_call(total, [((1, 2), last)], mlp_out, mate_out, end=True)
    shares = lax.all_to_all(shares, ("zh", "x", "core"), 0, 0)
    mixed = jnp.sum(shares.reshape(8, 2, 8, 8, span).astype(f32), axis=0)
    core = lax.axis_index("core")
    values = jnp.where(core == 0, jnp.stack([kept, other]), jnp.stack([other, kept]))
    encoded = mixed + values.reshape(2, 8, 8, span).astype(f32)
    encoded = encoded.transpose(1, 0, 2, 3).reshape(128, span).astype(bf16)
    return purified, encoded


def solution(mesh):
    fine = Mesh(mesh.devices.reshape(2, 4, 2, 4, 2), ("zh", "x", "zl", "y", "core"))
    row, col = ("zh", "x"), ("zl", "y", "core")
    images = P(row + col, None, None, None)
    placed = (images, images) + (P(),) * 8 + (P(col, row), P(row, col))
    return jax.shard_map(on_device, mesh=fine, in_specs=placed, out_specs=(images, P(row, col)),
                         check_vma=False)
```

```python
import functools
import math

import jax
import jax.numpy as jnp
from jax import lax
from jax.experimental import pallas as pl
from jax.experimental.pallas import tpu as pltpu
from jax.sharding import Mesh, PartitionSpec as P

step_size = 0.25
noise_gain = math.sqrt(0.5)
ln_epsilon = 1e-06
PATCH = 14
W1, W2 = 32, 16
CH = 256
f32, bf16 = jnp.float32, jnp.bfloat16


def gelu(v):
    inner = v * (0.7978845608028654 + 0.035677408136300125 * (v * v))
    half = 0.5 * v
    return half + half * jnp.tanh(inner)


def score_kernel(side, count, images, noise, stem_w, l1_hbm, down_hbm, l2_hbm, up_hbm, out_w,
                 purified, patches, raw, extra, pix, stem_x, stem_k, out_k, xa, xb, ca, cb, stream, coarse,
                 l1, down, l2, up, sems):
    half = side // 2
    span1, span2 = side * W1, half * W2
    pitch1, pitch2 = span1 + W1, span2 + W2
    loads = [pltpu.make_async_copy(l1_hbm.at[0], l1.at[0], sems.at[0]),
             pltpu.make_async_copy(l1_hbm.at[1], l1.at[1], sems.at[1]),
             pltpu.make_async_copy(down_hbm, down, sems.at[2]),
             pltpu.make_async_copy(l2_hbm, l2, sems.at[3]),
             pltpu.make_async_copy(up_hbm, up, sems.at[4]),
             pltpu.make_async_copy(l1_hbm.at[2], l1.at[2], sems.at[5]),
             pltpu.make_async_copy(l1_hbm.at[3], l1.at[3], sems.at[6])]
    for load in loads:
        load.start()

    mask1 = (lax.broadcasted_iota(jnp.int32, (span1, 1), 0) % W1) < side
    mask2 = (lax.broadcasted_iota(jnp.int32, (span2, 1), 0) % W2) < half

    def read(rows):
        return jnp.concatenate([stream[0, rows, :], stream[1, rows, :]], axis=1)

    def write(rows, value):
        stream[0, rows, :] = value[:, 0:128]
        stream[1, rows, :] = value[:, 128:256]

    for i in range(count + 1):
        z1 = jnp.zeros((W1, 3 * CH), bf16)
        z2 = jnp.zeros((W2, 3 * CH), bf16)
        xa[i * pitch1:i * pitch1 + W1, :] = z1
        xb[i * pitch1:i * pitch1 + W1, :] = z1
        ca[i * pitch2:i * pitch2 + W2, :] = z2
        cb[i * pitch2:i * pitch2 + W2, :] = z2
    raw[...] = jnp.zeros_like(raw)
    extra[...] = jnp.zeros_like(extra)
    stem_k[...] = jnp.zeros_like(stem_k)
    stem = stem_w[...].astype(f32)
    for dy in range(3):
        for dx in range(3):
            for c in range(3):
                k = (3 * dy + dx) * 3 + c
                at = 128 * dx + W1 * c + dy
                stem_k[at:at + 1, :] = stem[k:k + 1, :]
    column = lax.broadcasted_iota(jnp.int32, (8, 128), 1)
    colour = lax.broadcasted_iota(jnp.int32, (8, 128), 0)
    place = ((column == W1 * colour) & (colour < 3)).astype(bf16)
    out_k[...] = lax.dot_general(out_w[...], place[0:3, :], (((0,), (0,)), ((), ())), preferred_element_type=f32).astype(bf16)

    for y in range(side):
        for c in range(3):
            at = W1 * c + y
            v, n = images[y, c], noise[y, c]
            for i in range(count):
                raw[i, at:at + 1, 0:side] = v[i:i + 1, :]
                extra[i, at:at + 1, 0:side] = n[i:i + 1, :]

    def shifted(ref, base, value):
        n, wide = value.shape
        ref[pl.ds(base, n), 0:wide] = pltpu.roll(value, 1, 0).astype(bf16)
        ref[pl.ds(base, n), wide:2 * wide] = value.astype(bf16)
        ref[pl.ds(base, n), 2 * wide:3 * wide] = pltpu.roll(value, n - 1, 0).astype(bf16)

    def each(body):
        def step(i, _):
            body(i, pl.multiple_of(W1 + i * pitch1, W1))
            return 0
        lax.fori_loop(0, count, step, 0)

    def conv(ref, base, n, width, weights):
        near = jnp.concatenate([ref[pl.ds(base - width, n), :], ref[pl.ds(base, n), :],
                                ref[pl.ds(base + width, n), :]], axis=1)
        return jnp.dot(near, weights[...], preferred_element_type=f32)

    def begin(i, base):
        across = jnp.transpose(raw[i].astype(bf16).astype(f32))[0:W1, :]
        for y in range(side):
            pix[y * W1:(y + 1) * W1, :] = pltpu.roll(across, (1 - y) % 128, 1)
        shifted(stem_x, 0, pix[...])
        acc = jnp.dot(stem_x[...], stem_k[...].astype(bf16), preferred_element_type=f32)
        write(pl.ds(base, span1), acc)
        shifted(xa, base, jnp.where(mask1, gelu(acc), 0.0))
    each(begin)

    loads[0].wait()

    def layer0(i, base):
        s = read(pl.ds(base, span1)) + conv(xa, base, span1, W1, l1.at[0])
        write(pl.ds(base, span1), s)
        shifted(xb, base, jnp.where(mask1, gelu(s), 0.0))
    each(layer0)

    loads[1].wait()

    def layer1(i, base):
        write(pl.ds(base, span1), read(pl.ds(base, span1)) + conv(xb, base, span1, W1, l1.at[1]))
    each(layer1)

    loads[2].wait()
    loads[3].wait()
    loads[4].wait()
    for i in range(count):
        base1, base2 = W1 + i * pitch1, W2 + i * pitch2
        cols = [read(pl.ds(base1 + b, span1 // 2, stride=2)).astype(bf16).reshape(half, 2, W2, CH) for b in range(2)]
        cells = jnp.concatenate([cols[b][:, a].reshape(span2, CH) for a in range(2) for b in range(2)], axis=1)
        acc = jnp.dot(cells, down[...], preferred_element_type=f32)
        coarse[base2:base2 + span2, :] = acc
        shifted(ca, base2, jnp.where(mask2, gelu(acc), 0.0))
    for i in range(count):
        base2 = W2 + i * pitch2
        s = coarse[base2:base2 + span2, :] + conv(ca, base2, span2, W2, l2.at[0])
        coarse[base2:base2 + span2, :] = s
        shifted(cb, base2, jnp.where(mask2, gelu(s), 0.0))
    for i in range(count):
        base1, base2 = W1 + i * pitch1, W2 + i * pitch2
        s = coarse[base2:base2 + span2, :] + conv(cb, base2, span2, W2, l2.at[1])
        s = s.astype(bf16)
        for a in range(2):
            for b in range(2):
                g = (2 * a + b) * CH
                part = jnp.dot(s, up[:, g:g + CH], preferred_element_type=f32)
                for y in range(half):
                    rows = pl.ds(base1 + (2 * y + a) * W1 + b, W2, stride=2)
                    write(rows, read(rows) + part[y * W2:(y + 1) * W2, :])

    def enter(i, base):
        shifted(xa, base, jnp.where(mask1, gelu(read(pl.ds(base, span1))), 0.0))
    each(enter)

    loads[5].wait()

    def layer2(i, base):
        s = read(pl.ds(base, span1)) + conv(xa, base, span1, W1, l1.at[2])
        write(pl.ds(base, span1), s)
        shifted(xb, base, jnp.where(mask1, gelu(s), 0.0))
    each(layer2)

    loads[6].wait()

    def layer3(i, base):
        s = read(pl.ds(base, span1)) + conv(xb, base, span1, W1, l1.at[3])
        score = jnp.dot(gelu(s).astype(bf16), out_k[...], preferred_element_type=f32)
        across = score[0:W1, :]
        for y in range(1, side):
            across += pltpu.roll(score[y * W1:(y + 1) * W1, :], y, 1)
        across = jnp.concatenate([across, jnp.zeros((128 - W1, 128), f32)], axis=0)
        raw[i] = raw[i] + step_size * jnp.transpose(across) + noise_gain * extra[i]
    each(layer3)

    for y in range(side):
        for c in range(3):
            at = W1 * c + y
            purified[y, c] = jnp.concatenate([raw[i, at:at + 1, 0:side] for i in range(count)], axis=0)

    lane = lax.broadcasted_iota(jnp.int32, (128, 128), 1)
    line = lax.broadcasted_iota(jnp.int32, (128, 128), 0)
    wide = []
    for i in range(count):
        rows = None
        for c in range(3):
            spread = ((lane == 3 * line + c) & (line < side)).astype(bf16)
            part = jnp.dot(raw[i, W1 * c:W1 * (c + 1), :].astype(bf16), spread, preferred_element_type=f32)
            rows = part if rows is None else rows + part
        wide.append(rows)
    wide = jnp.concatenate(wide, axis=0).astype(bf16)
    many, run = 4 * count, 3 * PATCH
    token = lax.broadcasted_iota(jnp.int32, (many, count * W1), 0)
    source = lax.broadcasted_iota(jnp.int32, (many, count * W1), 1)
    first = (token // 4) * W1 + ((token // 2) % 2) * PATCH
    lanes = lax.broadcasted_iota(jnp.int32, (many, 128), 1)
    second = (lax.broadcasted_iota(jnp.int32, (many, 128), 0) % 2) == 1
    pieces = [jnp.zeros((many, 128), f32) for _ in range(5)]
    for r in range(PATCH):
        z = jnp.dot((source == first + r).astype(bf16), wide, preferred_element_type=f32)
        z = jnp.where(second, pltpu.roll(z, 128 - run, 1), z)
        z = jnp.where(lanes < run, z, 0.0)
        k, at = (run * r) // 128, (run * r) % 128
        z = pltpu.roll(z, at, 1) if at else z
        pieces[k] += jnp.where(lanes >= at, z, 0.0)
        if at + run > 128:
            pieces[k + 1] += jnp.where(lanes < at, z, 0.0)
    tokens = jnp.concatenate(pieces, axis=1).astype(bf16)
    patches[...] = tokens


def score_call(images, noise, stem_w, l1, down, l2, up, out_w):
    count, side = images.shape[0], images.shape[1]
    rows1 = W1 + count * (side + 1) * W1
    rows2 = W2 + count * (side // 2 + 1) * W2
    images, noise = images.transpose(1, 3, 0, 2), noise.transpose(1, 3, 0, 2)
    l1, down, l2, up = (pltpu.with_memory_space_constraint(w, pltpu.HBM) for w in (l1, down, l2, up))
    vm = pl.BlockSpec(memory_space=pltpu.VMEM)
    hb = pl.BlockSpec(memory_space=pltpu.HBM)
    purified, patches = pl.pallas_call(
        functools.partial(score_kernel, side, count),
        out_shape=(jax.ShapeDtypeStruct(images.shape, f32), jax.ShapeDtypeStruct((4 * count, 640), bf16)),
        in_specs=[vm, vm, vm, hb, hb, hb, hb, vm],
        out_specs=(vm, vm),
        scratch_shapes=[
            pltpu.VMEM((count, 128, 128), f32),
            pltpu.VMEM((count, 128, 128), f32),
            pltpu.VMEM((side * W1, 128), f32),
            pltpu.VMEM((side * W1, 3 * 128), bf16),
            pltpu.VMEM((3 * 128, CH), f32),
            pltpu.VMEM((CH, 128), bf16),
            pltpu.VMEM((rows1, 3 * CH), bf16),
            pltpu.VMEM((rows1, 3 * CH), bf16),
            pltpu.VMEM((rows2, 3 * CH), bf16),
            pltpu.VMEM((rows2, 3 * CH), bf16),
            pltpu.VMEM((CH // 128, rows1, 128), f32),
            pltpu.VMEM((rows2, CH), f32),
            pltpu.VMEM(l1.shape, bf16),
            pltpu.VMEM(down.shape, bf16),
            pltpu.VMEM(l2.shape, bf16),
            pltpu.VMEM(up.shape, bf16),
            pltpu.SemaphoreType.DMA((7,)),
        ],
        compiler_params=pltpu.CompilerParams(vmem_limit_bytes=36 << 20),
        cost_estimate=pl.CostEstimate(flops=10_000_000_000, transcendentals=3_000_000, bytes_accessed=12_000_000),
        name="score_net",
    )(images, noise, stem_w, l1, down, l2, up, out_w.T)
    return purified.transpose(2, 0, 3, 1), patches


def embed_kernel(flip, piece0, piece1, piece2, piece3, weight_hbm, bias, mixer_hbm, *refs):
    if flip:
        (total_in, sums_in, squares_in, hidden, sent, total, sums, squares,
         patches, weight, offset, mixer, sems, mixer_sems, piece_sems) = refs
    else:
        total, sums, squares, sent, patches, weight, offset, mixer, sems, mixer_sems, piece_sems = refs
    core = lax.axis_index("core")
    side = 1 - core if flip else core
    level, line, lines = lax.axis_index("zl"), lax.axis_index("y"), lax.axis_size("y")
    place = level * lines + line
    depth, features = weight_hbm.shape
    blocks, span, width = mixer_hbm.shape
    tokens = patches.shape[0]
    step = 1024

    def first(b):
        return pl.multiple_of((2 * b + side) * span, 128)
    loads = [pltpu.make_async_copy(weight_hbm.at[:, pl.ds(first(b), span)], weight.at[:, pl.ds(b * span, span)], sems.at[b])
             for b in range(blocks)]
    mixes = [pltpu.make_async_copy(mixer_hbm.at[b], mixer.at[pl.ds(b * span, span), :], mixer_sems.at[b])
             for b in range(blocks)]
    share = tokens // 8
    moves = []
    for k, piece in enumerate((piece0, piece1, piece2, piece3)):
        for part in range(2):
            to = (level + part) % 2 * lines + (line + lines - k) % lines
            moves.append(pltpu.make_async_copy(
                piece.at[pl.ds(part * share, share), :],
                patches.at[pl.ds(pl.multiple_of(to * share, share), share), :], piece_sems.at[2 * k + part]))
    for move in moves:
        move.start()
    for b in range(blocks):
        loads[b].start()
        mixes[b].start()
    for b in range(blocks):
        offset[:, b * span:(b + 1) * span] = bias[:, pl.ds(first(b), span)]
    for move in moves:
        move.wait()
    pixels = patches[:, 0:depth]
    ones = jnp.ones((16, step), bf16)
    ready = 0
    for c in range(blocks * span // step):
        at = slice(c * step, (c + 1) * step)
        while ready * span < (c + 1) * step:
            loads[ready].wait()
            mixes[ready].wait()
            ready += 1
        e = jnp.dot(pixels, weight[:, at], preferred_element_type=f32)
        e = (e + offset[:, at]).astype(bf16)
        v = e.astype(f32)
        q = v * v
        a = sum(v[:, k:k + 128] for k in range(128, step, 128)) + v[:, 0:128]
        b = sum(q[:, k:k + 128] for k in range(128, step, 128)) + q[:, 0:128]
        part = jnp.dot(jnp.concatenate([e, ones], axis=0), mixer[at, :], preferred_element_type=f32)
        if c:
            a, b, part = a + sums[...], b + squares[...], part + total[...]
        elif flip:
            a, b, part = a + sums_in[...], b + squares_in[...], part + total_in[...]
        sums[...], squares[...], total[...] = a, b, part
    mine = jnp.concatenate([patches[b * share:b * share + 8, 0:depth].astype(f32) for b in range(8)], axis=0).astype(bf16)
    at = pl.ds(pl.multiple_of(place * span, 128), span)
    sent[...] = (jnp.dot(mine, weight[:, at], preferred_element_type=f32) + offset[:, at]).astype(bf16)
    if flip:
        mean = jnp.sum(sums[...], axis=1, keepdims=True) / features
        square = jnp.sum(squares[...], axis=1, keepdims=True) / features
        scale = lax.rsqrt(square - mean * mean + ln_epsilon)
        column = total[tokens:tokens + 1, :]
        value = gelu((total[0:tokens, :] - mean * column) * scale).astype(bf16)
        hidden[...] = value


def embed_call(pieces, weight, bias, mixer, carry):
    tokens, depth = 4 * pieces[0].shape[0], weight.shape[0]
    blocks, span, width = mixer.shape
    flip = 1 if carry else 0
    free = pl.BlockSpec(memory_space=pl.ANY)
    sent = jax.ShapeDtypeStruct((tokens // 8, span), bf16)
    state = [(tokens + 16, width), (tokens, 128), (tokens, 128)]
    weight = pltpu.with_memory_space_constraint(weight, pltpu.HBM)
    vm = pl.BlockSpec(memory_space=pltpu.VMEM)
    hb = pl.BlockSpec(memory_space=pltpu.HBM)
    if flip:
        shapes = (jax.ShapeDtypeStruct((tokens, width), bf16), sent)
        scratch = [pltpu.VMEM(shape, f32) for shape in state]
    else:
        shapes = tuple(jax.ShapeDtypeStruct(shape, f32) for shape in state) + (sent,)
        scratch = []
    return pl.pallas_call(
        functools.partial(embed_kernel, flip),
        out_shape=shapes,
        in_specs=[free] * 4 + [hb, vm, free] + [vm] * len(carry),
        out_specs=(vm,) * len(shapes),
        scratch_shapes=scratch + [
            pltpu.VMEM((tokens, pieces[0].shape[1]), bf16),
            pltpu.VMEM((depth, blocks * span), bf16),
            pltpu.VMEM((1, blocks * span), f32),
            pltpu.VMEM((blocks * span, width), bf16),
            pltpu.SemaphoreType.DMA((blocks,)),
            pltpu.SemaphoreType.DMA((blocks,)),
            pltpu.SemaphoreType.DMA((8,)),
        ],
        compiler_params=pltpu.CompilerParams(vmem_limit_bytes=40 << 20),
        cost_estimate=pl.CostEstimate(flops=3_500_000_000, transcendentals=100_000, bytes_accessed=8_000_000),
        name="embed_mate" if flip else "embed_own",
    )(*pieces, weight, bias, mixer, *carry)


def mix_kernel(places, begin, end, *refs):
    refs = list(refs)
    total_in = None if begin else refs.pop(0)
    hidden = [refs.pop(0) for _ in places]
    own_hbm, mate_hbm, out, weight, sems = refs
    core = lax.axis_index("core")
    level, line, lines = lax.axis_index("zl"), lax.axis_index("y"), lax.axis_size("y")
    span = own_hbm.shape[1]
    width = hidden[0].shape[1]
    loads = []
    for n, (z, y) in enumerate(places):
        at = ((level + z) % 2 * lines + (line + y) % lines) * width
        for k, source in enumerate((own_hbm, mate_hbm)):
            loads.append(pltpu.make_async_copy(source.at[pl.ds(pl.multiple_of(at, width), width), :],
                                               weight.at[pl.ds(n * width, width), pl.ds(k * span, span)], sems.at[n, k]))
            loads[-1].start()
    for load in loads:
        load.wait()
    h = jnp.concatenate([block[...] for block in hidden], axis=1)
    done = jnp.dot(h, weight[...], preferred_element_type=f32)
    if not begin:
        done += total_in[...]
    if not end:
        out[...] = done
        return
    share = out.shape[1]
    tokens = done.shape[0]
    high, across, size = lax.axis_index("zh"), lax.axis_index("x"), lax.axis_size("x")
    for q in range(tokens // share):
        rows = jnp.concatenate([done[b * share + q * 8:b * share + q * 8 + 8, :] for b in range(8)], axis=0).astype(bf16)
        r = (high + q // size) % 2 * size + (across + size - q % size) % size
        out[2 * r + core] = rows[:, 0:span]
        out[2 * r + 1 - core] = rows[:, span:2 * span]


def mix_call(total, blocks, own, mate, end=False):
    places = tuple(place for place, _ in blocks)
    hidden = [block for _, block in blocks]
    tokens, width = hidden[0].shape
    span = own.shape[1]
    begin = total is None
    shape = jax.ShapeDtypeStruct((16, tokens // 8, span), bf16) if end else jax.ShapeDtypeStruct((tokens, 2 * span), f32)
    vm = pl.BlockSpec(memory_space=pltpu.VMEM)
    hb = pl.BlockSpec(memory_space=pltpu.HBM)
    return pl.pallas_call(
        functools.partial(mix_kernel, places, begin, end),
        out_shape=shape,
        in_specs=[vm] * (len(hidden) + (not begin)) + [hb, hb],
        out_specs=vm,
        scratch_shapes=[
            pltpu.VMEM((len(places) * width, 2 * span), bf16),
            pltpu.SemaphoreType.DMA((len(places), 2)),
        ],
        compiler_params=pltpu.CompilerParams(vmem_limit_bytes=24 << 20),
        cost_estimate=pl.CostEstimate(flops=2 * len(places) * tokens * width * 2 * span, transcendentals=0,
                                      bytes_accessed=len(places) * (tokens + 2 * span) * width * 2 + tokens * span * 8),
        name="mlp_out_" + str(len(places)),
    )(*([] if begin else [total]), *hidden, own, mate)


def split_kernel(whole, blocks, sems):
    width = blocks.shape[2]
    loads = [pltpu.make_async_copy(whole.at[:, pl.ds(b * width, width)], blocks.at[b], sems.at[b])
             for b in range(blocks.shape[0])]
    for load in loads:
        load.start()
    for load in loads:
        load.wait()


def split_call(whole, count):
    depth, width = whole.shape[0], whole.shape[1] // count
    return pl.pallas_call(
        split_kernel,
        out_shape=jax.ShapeDtypeStruct((count, depth, width), whole.dtype),
        in_specs=[pl.BlockSpec(memory_space=pltpu.HBM)],
        out_specs=pl.BlockSpec(memory_space=pltpu.VMEM),
        scratch_shapes=[pltpu.SemaphoreType.DMA((count,))],
        compiler_params=pltpu.CompilerParams(vmem_limit_bytes=8 << 20),
        cost_estimate=pl.CostEstimate(flops=0, transcendentals=0, bytes_accessed=2 * whole.size * 2),
        name="split_columns",
    )(pltpu.with_memory_space_constraint(whole, pltpu.HBM))


def shift(value, axis, k):
    n = lax.axis_size(axis)
    return lax.ppermute(value, axis, [(i, (i + k) % n) for i in range(n)])


def swap(value):
    return lax.ppermute(value, "core", [(0, 1), (1, 0)])


def on_device(images, noise_field, stem_weight, level_one, down_weight, level_two, up_weight,
              out_weight, embed_weight, embed_bias, mlp_in, mlp_out):
    span = mlp_in.shape[0]
    own_in = lax.all_to_all(split_call(mlp_in, 8), ("zl", "y"), 0, 0)
    mate_out = swap(mlp_out)

    purified, patches = score_call(images, noise_field, stem_weight, level_one, down_weight, level_two,
                                   up_weight, out_weight)
    mate_out, patches = lax.optimization_barrier((mate_out, patches))
    patches = jnp.concatenate([patches] + [shift(patches, "x", k) for k in (1, 2, 3)], axis=0)
    both = lax.ppermute(patches, ("zh", "zl"), [(i, 3 - i) for i in range(4)])
    patches = jnp.concatenate([patches, shift(patches, "zh", 1), shift(patches, "zl", 1), both], axis=0)
    pieces = [patches] + [shift(patches, "y", k) for k in (1, 2, 3)]
    own_in, *pieces = lax.optimization_barrier((own_in, *pieces))
    mate_in = swap(own_in)
    *carry, kept = embed_call(pieces, embed_weight, embed_bias[None], own_in, ())
    hidden, sent = embed_call(pieces, embed_weight, embed_bias[None], mate_in, tuple(carry))
    other = swap(sent)
    far = shift(hidden, "zl", 1)
    below = shift(hidden, "y", 1)
    above = shift(hidden, "y", 3)
    far, below, above = lax.optimization_barrier((far, below, above))
    across = shift(below, "y", 1)
    far_above = shift(far, "y", 3)
    far_below = shift(below, "zl", 1)
    total = mix_call(None, [((0, 0), hidden), ((1, 0), far), ((0, 3), below), ((0, 1), above)], mlp_out, mate_out)
    far_below, far_above, total = lax.optimization_barrier((far_below, far_above, total))
    half = hidden.shape[0] // 2
    last = jnp.concatenate([shift(far_below[:half], "y", 1), shift(far_above[half:], "y", 3)], axis=0)
    total = mix_call(total, [((0, 2), across), ((1, 1), far_above), ((1, 3), far_below)], mlp_out, mate_out)
    shares = mix_call(total, [((1, 2), last)], mlp_out, mate_out, end=True)
    shares = lax.all_to_all(shares, ("zh", "x", "core"), 0, 0)
    mixed = jnp.sum(shares.reshape(8, 2, 8, 8, span).astype(f32), axis=0)
    core = lax.axis_index("core")
    values = jnp.where(core == 0, jnp.stack([kept, other]), jnp.stack([other, kept]))
    encoded = mixed + values.reshape(2, 8, 8, span).astype(f32)
    encoded = encoded.transpose(1, 0, 2, 3).reshape(128, span).astype(bf16)
    return purified, encoded


def solution(mesh):
    fine = Mesh(mesh.devices.reshape(2, 4, 2, 4, 2), ("zh", "x", "zl", "y", "core"))
    row, col = ("zh", "x"), ("zl", "y", "core")
    images = P(row + col, None, None, None)
    placed = (images, images) + (P(),) * 8 + (P(col, row), P(row, col))
    return jax.shard_map(on_device, mesh=fine, in_specs=placed, out_specs=(images, P(row, col)),
                         check_vma=False)
```

```python
import functools
import math

import jax
import jax.numpy as jnp
from jax import lax
from jax.experimental import pallas as pl
from jax.experimental.pallas import tpu as pltpu
from jax.sharding import Mesh, PartitionSpec as P

step_size = 0.25
noise_gain = math.sqrt(0.5)
ln_epsilon = 1e-06
PATCH = 14
W1, W2 = 32, 16
CH = 256
f32, bf16 = jnp.float32, jnp.bfloat16


def gelu(v):
    inner = v * (0.7978845608028654 + 0.035677408136300125 * (v * v))
    half = 0.5 * v
    return half + half * jnp.tanh(inner)


def score_kernel(side, count, images, noise, stem_w, l1_hbm, down_hbm, l2_hbm, up_hbm, out_w,
                 purified, patches, raw, extra, pix, stem_x, stem_k, out_k, xa, xb, ca, cb, stream, coarse,
                 l1, down, l2, up, sems):
    half = side // 2
    span1, span2 = side * W1, half * W2
    pitch1, pitch2 = span1 + W1, span2 + W2
    loads = [pltpu.make_async_copy(l1_hbm.at[0], l1.at[0], sems.at[0]),
             pltpu.make_async_copy(l1_hbm.at[1], l1.at[1], sems.at[1]),
             pltpu.make_async_copy(down_hbm, down, sems.at[2]),
             pltpu.make_async_copy(l2_hbm, l2, sems.at[3]),
             pltpu.make_async_copy(up_hbm, up, sems.at[4]),
             pltpu.make_async_copy(l1_hbm.at[2], l1.at[2], sems.at[5]),
             pltpu.make_async_copy(l1_hbm.at[3], l1.at[3], sems.at[6])]
    for load in loads:
        load.start()

    mask1 = (lax.broadcasted_iota(jnp.int32, (span1, 1), 0) % W1) < side
    mask2 = (lax.broadcasted_iota(jnp.int32, (span2, 1), 0) % W2) < half

    def read(rows):
        return jnp.concatenate([stream[0, rows, :], stream[1, rows, :]], axis=1)

    def write(rows, value):
        stream[0, rows, :] = value[:, 0:128]
        stream[1, rows, :] = value[:, 128:256]

    for i in range(count + 1):
        z1 = jnp.zeros((W1, 3 * CH), bf16)
        z2 = jnp.zeros((W2, 3 * CH), bf16)
        xa[i * pitch1:i * pitch1 + W1, :] = z1
        xb[i * pitch1:i * pitch1 + W1, :] = z1
        ca[i * pitch2:i * pitch2 + W2, :] = z2
        cb[i * pitch2:i * pitch2 + W2, :] = z2
    raw[...] = jnp.zeros_like(raw)
    extra[...] = jnp.zeros_like(extra)
    stem_k[...] = jnp.zeros_like(stem_k)
    stem = stem_w[...].astype(f32)
    for dy in range(3):
        for dx in range(3):
            for c in range(3):
                k = (3 * dy + dx) * 3 + c
                at = 128 * dx + W1 * c + dy
                stem_k[at:at + 1, :] = stem[k:k + 1, :]
    column = lax.broadcasted_iota(jnp.int32, (8, 128), 1)
    colour = lax.broadcasted_iota(jnp.int32, (8, 128), 0)
    place = ((column == W1 * colour) & (colour < 3)).astype(bf16)
    out_k[...] = lax.dot_general(out_w[...], place[0:3, :], (((0,), (0,)), ((), ())), preferred_element_type=f32).astype(bf16)

    for y in range(side):
        for c in range(3):
            at = W1 * c + y
            v, n = images[y, c], noise[y, c]
            for i in range(count):
                raw[i, at:at + 1, 0:side] = v[i:i + 1, :]
                extra[i, at:at + 1, 0:side] = n[i:i + 1, :]

    def shifted(ref, base, value):
        n, wide = value.shape
        ref[pl.ds(base, n), 0:wide] = pltpu.roll(value, 1, 0).astype(bf16)
        ref[pl.ds(base, n), wide:2 * wide] = value.astype(bf16)
        ref[pl.ds(base, n), 2 * wide:3 * wide] = pltpu.roll(value, n - 1, 0).astype(bf16)

    def each(body):
        def step(i, _):
            body(i, pl.multiple_of(W1 + i * pitch1, W1))
            return 0
        lax.fori_loop(0, count, step, 0)

    def conv(ref, base, n, width, weights):
        near = jnp.concatenate([ref[pl.ds(base - width, n), :], ref[pl.ds(base, n), :],
                                ref[pl.ds(base + width, n), :]], axis=1)
        return jnp.dot(near, weights[...], preferred_element_type=f32)

    def begin(i, base):
        across = jnp.transpose(raw[i].astype(bf16).astype(f32))[0:W1, :]
        for y in range(side):
            pix[y * W1:(y + 1) * W1, :] = pltpu.roll(across, (1 - y) % 128, 1)
        shifted(stem_x, 0, pix[...])
        acc = jnp.dot(stem_x[...], stem_k[...].astype(bf16), preferred_element_type=f32)
        write(pl.ds(base, span1), acc)
        shifted(xa, base, jnp.where(mask1, gelu(acc), 0.0))
    each(begin)

    loads[0].wait()

    def layer0(i, base):
        s = read(pl.ds(base, span1)) + conv(xa, base, span1, W1, l1.at[0])
        write(pl.ds(base, span1), s)
        shifted(xb, base, jnp.where(mask1, gelu(s), 0.0))
    each(layer0)

    loads[1].wait()

    def layer1(i, base):
        write(pl.ds(base, span1), read(pl.ds(base, span1)) + conv(xb, base, span1, W1, l1.at[1]))
    each(layer1)

    loads[2].wait()
    loads[3].wait()
    loads[4].wait()
    for i in range(count):
        base1, base2 = W1 + i * pitch1, W2 + i * pitch2
        cols = [read(pl.ds(base1 + b, span1 // 2, stride=2)).astype(bf16).reshape(half, 2, W2, CH) for b in range(2)]
        cells = jnp.concatenate([cols[b][:, a].reshape(span2, CH) for a in range(2) for b in range(2)], axis=1)
        acc = jnp.dot(cells, down[...], preferred_element_type=f32)
        coarse[base2:base2 + span2, :] = acc
        shifted(ca, base2, jnp.where(mask2, gelu(acc), 0.0))
    for i in range(count):
        base2 = W2 + i * pitch2
        s = coarse[base2:base2 + span2, :] + conv(ca, base2, span2, W2, l2.at[0])
        coarse[base2:base2 + span2, :] = s
        shifted(cb, base2, jnp.where(mask2, gelu(s), 0.0))
    for i in range(count):
        base1, base2 = W1 + i * pitch1, W2 + i * pitch2
        s = coarse[base2:base2 + span2, :] + conv(cb, base2, span2, W2, l2.at[1])
        s = s.astype(bf16)
        for a in range(2):
            for b in range(2):
                g = (2 * a + b) * CH
                part = jnp.dot(s, up[:, g:g + CH], preferred_element_type=f32)
                for y in range(half):
                    rows = pl.ds(base1 + (2 * y + a) * W1 + b, W2, stride=2)
                    write(rows, read(rows) + part[y * W2:(y + 1) * W2, :])

    def enter(i, base):
        shifted(xa, base, jnp.where(mask1, gelu(read(pl.ds(base, span1))), 0.0))
    each(enter)

    loads[5].wait()

    def layer2(i, base):
        s = read(pl.ds(base, span1)) + conv(xa, base, span1, W1, l1.at[2])
        write(pl.ds(base, span1), s)
        shifted(xb, base, jnp.where(mask1, gelu(s), 0.0))
    each(layer2)

    loads[6].wait()

    def layer3(i, base):
        s = read(pl.ds(base, span1)) + conv(xb, base, span1, W1, l1.at[3])
        score = jnp.dot(gelu(s).astype(bf16), out_k[...], preferred_element_type=f32)
        across = score[0:W1, :]
        for y in range(1, side):
            across += pltpu.roll(score[y * W1:(y + 1) * W1, :], y, 1)
        across = jnp.concatenate([across, jnp.zeros((128 - W1, 128), f32)], axis=0)
        raw[i] = raw[i] + step_size * jnp.transpose(across) + noise_gain * extra[i]
    each(layer3)

    for y in range(side):
        for c in range(3):
            at = W1 * c + y
            purified[y, c] = jnp.concatenate([raw[i, at:at + 1, 0:side] for i in range(count)], axis=0)

    lane = lax.broadcasted_iota(jnp.int32, (128, 128), 1)
    line = lax.broadcasted_iota(jnp.int32, (128, 128), 0)
    wide = []
    for i in range(count):
        rows = None
        for c in range(3):
            spread = ((lane == 3 * line + c) & (line < side)).astype(bf16)
            part = jnp.dot(raw[i, W1 * c:W1 * (c + 1), :].astype(bf16), spread, preferred_element_type=f32)
            rows = part if rows is None else rows + part
        wide.append(rows)
    wide = jnp.concatenate(wide, axis=0).astype(bf16)
    many, run = 4 * count, 3 * PATCH
    token = lax.broadcasted_iota(jnp.int32, (many, count * W1), 0)
    source = lax.broadcasted_iota(jnp.int32, (many, count * W1), 1)
    first = (token // 4) * W1 + ((token // 2) % 2) * PATCH
    lanes = lax.broadcasted_iota(jnp.int32, (many, 128), 1)
    second = (lax.broadcasted_iota(jnp.int32, (many, 128), 0) % 2) == 1
    pieces = [jnp.zeros((many, 128), f32) for _ in range(5)]
    for r in range(PATCH):
        z = jnp.dot((source == first + r).astype(bf16), wide, preferred_element_type=f32)
        z = jnp.where(second, pltpu.roll(z, 128 - run, 1), z)
        z = jnp.where(lanes < run, z, 0.0)
        k, at = (run * r) // 128, (run * r) % 128
        z = pltpu.roll(z, at, 1) if at else z
        pieces[k] += jnp.where(lanes >= at, z, 0.0)
        if at + run > 128:
            pieces[k + 1] += jnp.where(lanes < at, z, 0.0)
    tokens = jnp.concatenate(pieces, axis=1).astype(bf16)
    patches[...] = tokens


def score_call(images, noise, stem_w, l1, down, l2, up, out_w):
    count, side = images.shape[0], images.shape[1]
    rows1 = W1 + count * (side + 1) * W1
    rows2 = W2 + count * (side // 2 + 1) * W2
    images, noise = images.transpose(1, 3, 0, 2), noise.transpose(1, 3, 0, 2)
    l1, down, l2, up = (pltpu.with_memory_space_constraint(w, pltpu.HBM) for w in (l1, down, l2, up))
    vm = pl.BlockSpec(memory_space=pltpu.VMEM)
    hb = pl.BlockSpec(memory_space=pltpu.HBM)
    purified, patches = pl.pallas_call(
        functools.partial(score_kernel, side, count),
        out_shape=(jax.ShapeDtypeStruct(images.shape, f32), jax.ShapeDtypeStruct((4 * count, 640), bf16)),
        in_specs=[vm, vm, vm, hb, hb, hb, hb, vm],
        out_specs=(vm, vm),
        scratch_shapes=[
            pltpu.VMEM((count, 128, 128), f32),
            pltpu.VMEM((count, 128, 128), f32),
            pltpu.VMEM((side * W1, 128), f32),
            pltpu.VMEM((side * W1, 3 * 128), bf16),
            pltpu.VMEM((3 * 128, CH), f32),
            pltpu.VMEM((CH, 128), bf16),
            pltpu.VMEM((rows1, 3 * CH), bf16),
            pltpu.VMEM((rows1, 3 * CH), bf16),
            pltpu.VMEM((rows2, 3 * CH), bf16),
            pltpu.VMEM((rows2, 3 * CH), bf16),
            pltpu.VMEM((CH // 128, rows1, 128), f32),
            pltpu.VMEM((rows2, CH), f32),
            pltpu.VMEM(l1.shape, bf16),
            pltpu.VMEM(down.shape, bf16),
            pltpu.VMEM(l2.shape, bf16),
            pltpu.VMEM(up.shape, bf16),
            pltpu.SemaphoreType.DMA((7,)),
        ],
        compiler_params=pltpu.CompilerParams(vmem_limit_bytes=36 << 20),
        cost_estimate=pl.CostEstimate(flops=10_000_000_000, transcendentals=3_000_000, bytes_accessed=12_000_000),
        name="score_net",
    )(images, noise, stem_w, l1, down, l2, up, out_w.T)
    return purified.transpose(2, 0, 3, 1), patches


def embed_kernel(flip, piece0, piece1, piece2, piece3, weight_hbm, bias, mixer_hbm, *refs):
    if flip:
        (total_in, sums_in, squares_in, hidden, sent, total, sums, squares,
         patches, weight, offset, mixer, sems, mixer_sems, piece_sems) = refs
    else:
        total, sums, squares, sent, patches, weight, offset, mixer, sems, mixer_sems, piece_sems = refs
    core = lax.axis_index("core")
    side = 1 - core if flip else core
    level, line, lines = lax.axis_index("zl"), lax.axis_index("y"), lax.axis_size("y")
    place = level * lines + line
    depth, features = weight_hbm.shape
    blocks, span, width = mixer_hbm.shape
    tokens = patches.shape[0]
    step = 1024

    def first(b):
        return pl.multiple_of((2 * b + side) * span, 128)
    loads = [pltpu.make_async_copy(weight_hbm.at[:, pl.ds(first(b), span)], weight.at[:, pl.ds(b * span, span)], sems.at[b])
             for b in range(blocks)]
    mixes = [pltpu.make_async_copy(mixer_hbm.at[b], mixer.at[pl.ds(b * span, span), :], mixer_sems.at[b])
             for b in range(blocks)]
    share = tokens // 8
    moves = []
    for k, piece in enumerate((piece0, piece1, piece2, piece3)):
        for part in range(2):
            to = (level + part) % 2 * lines + (line + lines - k) % lines
            moves.append(pltpu.make_async_copy(
                piece.at[pl.ds(part * share, share), :],
                patches.at[pl.ds(pl.multiple_of(to * share, share), share), :], piece_sems.at[2 * k + part]))
    for move in moves:
        move.start()
    for b in range(blocks):
        loads[b].start()
        mixes[b].start()
    for b in range(blocks):
        offset[:, b * span:(b + 1) * span] = bias[:, pl.ds(first(b), span)]
    for move in moves:
        move.wait()
    pixels = patches[:, 0:depth]
    ones = jnp.ones((16, step), bf16)
    ready = 0
    for c in range(blocks * span // step):
        at = slice(c * step, (c + 1) * step)
        while ready * span < (c + 1) * step:
            loads[ready].wait()
            mixes[ready].wait()
            ready += 1
        e = jnp.dot(pixels, weight[:, at], preferred_element_type=f32)
        e = (e + offset[:, at]).astype(bf16)
        v = e.astype(f32)
        q = v * v
        a = sum(v[:, k:k + 128] for k in range(128, step, 128)) + v[:, 0:128]
        b = sum(q[:, k:k + 128] for k in range(128, step, 128)) + q[:, 0:128]
        part = jnp.dot(jnp.concatenate([e, ones], axis=0), mixer[at, :], preferred_element_type=f32)
        if c:
            a, b, part = a + sums[...], b + squares[...], part + total[...]
        elif flip:
            a, b, part = a + sums_in[...], b + squares_in[...], part + total_in[...]
        sums[...], squares[...], total[...] = a, b, part
    mine = jnp.concatenate([patches[b * share:b * share + 8, 0:depth].astype(f32) for b in range(8)], axis=0).astype(bf16)
    at = pl.ds(pl.multiple_of(place * span, 128), span)
    sent[...] = (jnp.dot(mine, weight[:, at], preferred_element_type=f32) + offset[:, at]).astype(bf16)
    if flip:
        mean = jnp.sum(sums[...], axis=1, keepdims=True) / features
        square = jnp.sum(squares[...], axis=1, keepdims=True) / features
        scale = lax.rsqrt(square - mean * mean + ln_epsilon)
        column = total[tokens:tokens + 1, :]
        value = gelu((total[0:tokens, :] - mean * column) * scale).astype(bf16)
        hidden[...] = value


def embed_call(pieces, weight, bias, mixer, carry):
    tokens, depth = 4 * pieces[0].shape[0], weight.shape[0]
    blocks, span, width = mixer.shape
    flip = 1 if carry else 0
    free = pl.BlockSpec(memory_space=pl.ANY)
    sent = jax.ShapeDtypeStruct((tokens // 8, span), bf16)
    state = [(tokens + 16, width), (tokens, 128), (tokens, 128)]
    weight = pltpu.with_memory_space_constraint(weight, pltpu.HBM)
    vm = pl.BlockSpec(memory_space=pltpu.VMEM)
    hb = pl.BlockSpec(memory_space=pltpu.HBM)
    if flip:
        shapes = (jax.ShapeDtypeStruct((tokens, width), bf16), sent)
        scratch = [pltpu.VMEM(shape, f32) for shape in state]
    else:
        shapes = tuple(jax.ShapeDtypeStruct(shape, f32) for shape in state) + (sent,)
        scratch = []
    return pl.pallas_call(
        functools.partial(embed_kernel, flip),
        out_shape=shapes,
        in_specs=[free] * 4 + [hb, vm, free] + [vm] * len(carry),
        out_specs=(vm,) * len(shapes),
        scratch_shapes=scratch + [
            pltpu.VMEM((tokens, pieces[0].shape[1]), bf16),
            pltpu.VMEM((depth, blocks * span), bf16),
            pltpu.VMEM((1, blocks * span), f32),
            pltpu.VMEM((blocks * span, width), bf16),
            pltpu.SemaphoreType.DMA((blocks,)),
            pltpu.SemaphoreType.DMA((blocks,)),
            pltpu.SemaphoreType.DMA((8,)),
        ],
        compiler_params=pltpu.CompilerParams(vmem_limit_bytes=40 << 20),
        cost_estimate=pl.CostEstimate(flops=3_500_000_000, transcendentals=100_000, bytes_accessed=8_000_000),
        name="embed_mate" if flip else "embed_own",
    )(*pieces, weight, bias, mixer, *carry)


def mix_kernel(places, begin, end, *refs):
    refs = list(refs)
    total_in = None if begin else refs.pop(0)
    hidden = [refs.pop(0) for _ in places]
    own_hbm, mate_hbm, out, weight, sems = refs
    core = lax.axis_index("core")
    level, line, lines = lax.axis_index("zl"), lax.axis_index("y"), lax.axis_size("y")
    span = own_hbm.shape[1]
    width = hidden[0].shape[1]
    loads = []
    for n, (z, y) in enumerate(places):
        at = ((level + z) % 2 * lines + (line + y) % lines) * width
        for k, source in enumerate((own_hbm, mate_hbm)):
            loads.append(pltpu.make_async_copy(source.at[pl.ds(pl.multiple_of(at, width), width), :],
                                               weight.at[pl.ds(n * width, width), pl.ds(k * span, span)], sems.at[n, k]))
            loads[-1].start()
    for load in loads:
        load.wait()
    h = jnp.concatenate([block[...] for block in hidden], axis=1)
    done = jnp.dot(h, weight[...], preferred_element_type=f32)
    if not begin:
        done += total_in[...]
    if not end:
        out[...] = done
        return
    share = out.shape[1]
    tokens = done.shape[0]
    high, across, size = lax.axis_index("zh"), lax.axis_index("x"), lax.axis_size("x")
    near = (across, across + 1 - 2 * (across % 2), (across + 2) % size, 3 - across)
    for q in range(tokens // share):
        rows = jnp.concatenate([done[b * share + q * 8:b * share + q * 8 + 8, :] for b in range(8)], axis=0).astype(bf16)
        r = (high + q // size) % 2 * size + near[q % size]
        out[2 * r + core] = rows[:, 0:span]
        out[2 * r + 1 - core] = rows[:, span:2 * span]


def mix_call(total, blocks, own, mate, end=False):
    places = tuple(place for place, _ in blocks)
    hidden = [block for _, block in blocks]
    tokens, width = hidden[0].shape
    span = own.shape[1]
    begin = total is None
    shape = jax.ShapeDtypeStruct((16, tokens // 8, span), bf16) if end else jax.ShapeDtypeStruct((tokens, 2 * span), f32)
    vm = pl.BlockSpec(memory_space=pltpu.VMEM)
    hb = pl.BlockSpec(memory_space=pltpu.HBM)
    return pl.pallas_call(
        functools.partial(mix_kernel, places, begin, end),
        out_shape=shape,
        in_specs=[vm] * (len(hidden) + (not begin)) + [hb, hb],
        out_specs=vm,
        scratch_shapes=[
            pltpu.VMEM((len(places) * width, 2 * span), bf16),
            pltpu.SemaphoreType.DMA((len(places), 2)),
        ],
        compiler_params=pltpu.CompilerParams(vmem_limit_bytes=24 << 20),
        cost_estimate=pl.CostEstimate(flops=2 * len(places) * tokens * width * 2 * span, transcendentals=0,
                                      bytes_accessed=len(places) * (tokens + 2 * span) * width * 2 + tokens * span * 8),
        name="mlp_out_" + str(len(places)),
    )(*([] if begin else [total]), *hidden, own, mate)


def split_kernel(whole, blocks, sems):
    width = blocks.shape[2]
    loads = [pltpu.make_async_copy(whole.at[:, pl.ds(b * width, width)], blocks.at[b], sems.at[b])
             for b in range(blocks.shape[0])]
    for load in loads:
        load.start()
    for load in loads:
        load.wait()


def split_call(whole, count):
    depth, width = whole.shape[0], whole.shape[1] // count
    return pl.pallas_call(
        split_kernel,
        out_shape=jax.ShapeDtypeStruct((count, depth, width), whole.dtype),
        in_specs=[pl.BlockSpec(memory_space=pltpu.HBM)],
        out_specs=pl.BlockSpec(memory_space=pltpu.VMEM),
        scratch_shapes=[pltpu.SemaphoreType.DMA((count,))],
        compiler_params=pltpu.CompilerParams(vmem_limit_bytes=8 << 20),
        cost_estimate=pl.CostEstimate(flops=0, transcendentals=0, bytes_accessed=2 * whole.size * 2),
        name="split_columns",
    )(pltpu.with_memory_space_constraint(whole, pltpu.HBM))


def shift(value, axis, k):
    n = lax.axis_size(axis)
    return lax.ppermute(value, axis, [(i, (i + k) % n) for i in range(n)])


def swap(value):
    return lax.ppermute(value, "core", [(0, 1), (1, 0)])


def on_device(images, noise_field, stem_weight, level_one, down_weight, level_two, up_weight,
              out_weight, embed_weight, embed_bias, mlp_in, mlp_out):
    span = mlp_in.shape[0]
    own_in = lax.all_to_all(split_call(mlp_in, 8), ("zl", "y"), 0, 0)
    mate_out = swap(mlp_out)

    purified, patches = score_call(images, noise_field, stem_weight, level_one, down_weight, level_two,
                                   up_weight, out_weight)
    mate_out, patches = lax.optimization_barrier((mate_out, patches))
    pair = lax.ppermute(patches, "x", [(0, 1), (1, 0), (2, 3), (3, 2)])
    patches = jnp.concatenate([patches, pair], axis=0)
    patches = jnp.concatenate([patches, shift(patches, "x", 2)], axis=0)
    both = lax.ppermute(patches, ("zh", "zl"), [(i, 3 - i) for i in range(4)])
    patches = jnp.concatenate([patches, shift(patches, "zh", 1), shift(patches, "zl", 1), both], axis=0)
    pieces = [patches] + [shift(patches, "y", k) for k in (1, 2, 3)]
    own_in, *pieces = lax.optimization_barrier((own_in, *pieces))
    mate_in = swap(own_in)
    *carry, kept = embed_call(pieces, embed_weight, embed_bias[None], own_in, ())
    hidden, sent = embed_call(pieces, embed_weight, embed_bias[None], mate_in, tuple(carry))
    other = swap(sent)
    far = shift(hidden, "zl", 1)
    below = shift(hidden, "y", 1)
    above = shift(hidden, "y", 3)
    far, below, above = lax.optimization_barrier((far, below, above))
    across = shift(below, "y", 1)
    far_above = shift(far, "y", 3)
    far_below = shift(below, "zl", 1)
    total = mix_call(None, [((0, 0), hidden), ((1, 0), far), ((0, 3), below), ((0, 1), above)], mlp_out, mate_out)
    far_below, far_above, total = lax.optimization_barrier((far_below, far_above, total))
    half = hidden.shape[0] // 2
    last = jnp.concatenate([shift(far_below[:half], "y", 1), shift(far_above[half:], "y", 3)], axis=0)
    total = mix_call(total, [((0, 2), across), ((1, 1), far_above), ((1, 3), far_below)], mlp_out, mate_out)
    shares = mix_call(total, [((1, 2), last)], mlp_out, mate_out, end=True)
    shares = lax.all_to_all(shares, ("zh", "x", "core"), 0, 0)
    mixed = jnp.sum(shares.reshape(8, 2, 8, 8, span).astype(f32), axis=0)
    core = lax.axis_index("core")
    values = jnp.where(core == 0, jnp.stack([kept, other]), jnp.stack([other, kept]))
    encoded = mixed + values.reshape(2, 8, 8, span).astype(f32)
    encoded = encoded.transpose(1, 0, 2, 3).reshape(128, span).astype(bf16)
    return purified, encoded


def solution(mesh):
    fine = Mesh(mesh.devices.reshape(2, 4, 2, 4, 2), ("zh", "x", "zl", "y", "core"))
    row, col = ("zh", "x"), ("zl", "y", "core")
    images = P(row + col, None, None, None)
    placed = (images, images) + (P(),) * 8 + (P(col, row), P(row, col))
    return jax.shard_map(on_device, mesh=fine, in_specs=placed, out_specs=(images, P(row, col)),
                         check_vma=False)
```
